32 devices in a mesh: req: 8 (over z, x), tp: 4 (over y, core).
Axes of the slice: x: 2, y: 2, z: 4, core: 2. Of those that a mesh axis runs over, the one named last changes fastest.
Arguments:
- hidden_in: bfloat16 [1024, 4096], P(('req', 'tp')), may hold values from -6 to 6
- queries: bfloat16 [1024, 4096], P(('req', 'tp')), may hold values from -6 to 6
- new_keys: bfloat16 [1024, 1024], P(('req', 'tp')), may hold values from -6 to 6
- new_values: bfloat16 [1024, 1024], P(('req', 'tp')), may hold values from -6 to 6
- key_cache: bfloat16 [32768, 1024], P(('req', 'tp'))
- value_cache: bfloat16 [32768, 1024], P(('req', 'tp')), may hold values from -6 to 6
- cache_lengths: int32 [16], replicated, may hold values from 256 to 2048, as said below
- parent_ids: int32 [16, 64], replicated, may hold values from 0 to 62, as said below
- accepted_leaf: int32 [16], replicated, may hold values from 0 to 63
- query_gain: bfloat16 [128], replicated, may hold values from 0.5 to 1.5
- key_gain: bfloat16 [128], replicated, may hold values from 0.5 to 1.5
- post_gain: bfloat16 [4096], replicated, may hold values from 0.5 to 1.5
- out_weight: bfloat16 [4096, 4096], P('req', 'tp'), may hold values from -0.09375 to 0.09375
- gate_weight: bfloat16 [4096, 6144], P('req', 'tp'), may hold values from -0.09375 to 0.09375
- up_weight: bfloat16 [4096, 6144], P('req', 'tp'), may hold values from -0.09375 to 0.09375
- down_weight: bfloat16 [6144, 4096], P('tp', 'req'), may hold values from -0.078125 to 0.078125
Outputs:
- layer_out: bfloat16 [1024, 4096], P(('req', 'tp'))
- accepted_kv: bfloat16 [1024, 2048], P(('req', 'tp'))
The draws below stay inside these ranges and needn't reach their ends.
Inputs may be any that keep to these rules, and one draw needn't show every extreme that they name: `cache_lengths`: some request has exactly 2048 live positions and some exactly 256. parent_ids[r, 0] = 0; every other node j has a parent among nodes j - 4 to j - 1.
All inputs are finite; a program needn't handle non-finite values.
Results may differ from the reference program's by a relative error of at most 0.018.
Values may be sent and summed in bfloat16 or wider, within the bound.
A program may use at most 128 MiB of HBM per device.

```python
import jax
import jax.numpy as jnp
from jax import lax

D = 4096
HEADS = 32
KV_HEADS = 8
HEAD_DIM = 128
FF = 6144
TREE = 64
CAP = 2048
QDIM = 4096
KVDIM = 1024
REQ = 16
TOKENS = 1024
CACHE_ROWS = 32768


def draw_key_cache(key, part):
    drawn = jax.random.normal(jax.random.fold_in(key, 11), (CACHE_ROWS, KVDIM), jnp.float32)
    return drawn.astype(jnp.bfloat16)


def draw_cache_lengths(key, part):
    short_len = jax.random.randint(jax.random.fold_in(key, 21), (REQ,), CAP // 8, CAP // 4 + 1)
    long_len = jax.random.randint(jax.random.fold_in(key, 22), (REQ,), 3 * CAP // 4, CAP + 1)
    selector = jax.random.randint(jax.random.fold_in(key, 23), (REQ,), 0, 8)
    lengths = jnp.where(selector == 0, long_len, short_len)
    longest = jax.random.randint(jax.random.fold_in(key, 24), (), 0, REQ)
    lengths = lengths.at[longest].set(CAP)
    lengths = lengths.at[(longest + 1) % REQ].set(CAP // 8)
    return lengths.astype(jnp.int32)


def draw_parent_ids(key, part):
    node_ids = jnp.arange(TREE, dtype=jnp.int32)
    step_back = jax.random.randint(jax.random.fold_in(key, 31), (REQ, TREE), 0, 4)
    step_back = jnp.minimum(step_back, jnp.maximum(node_ids - 1, 0)[None, :])
    return jnp.where(node_ids[None, :] == 0, 0, node_ids[None, :] - 1 - step_back).astype(jnp.int32)


def plant(values, own_key, low, high):
    longest = values.shape.index(max(values.shape))
    spots = []
    for shift in (0, 1):
        where = [jax.random.randint(jax.random.fold_in(own_key, axis), (), 0, length) for axis, length in enumerate(values.shape)]
        where[longest] = (where[longest] + shift) % values.shape[longest]
        spots.append(tuple(where))
    return values.at[spots[0]].set(low).at[spots[1]].set(high)


def level_of(rng, shape, shards, least, high):
    factor_of = 1.0
    for axis_at, blocks in shards:
        draws = jax.random.uniform(jax.random.fold_in(jax.random.fold_in(rng, 6), axis_at), (blocks,), jnp.float32, least / len(shards), high / len(shards))
        factor_of = factor_of * jnp.repeat(jnp.exp(draws), shape[axis_at] // blocks).reshape((-1,) + (1,) * (len(shape) - 1 - axis_at))
    return factor_of


def noise(key, shape, spread, most, split=(), kind=jnp.bfloat16):
    entries = spread * jax.random.normal(key, shape, jnp.float32)
    if split:
        entries = entries * level_of(key, shape, split, -0.22, 0.18)
    return jnp.clip(entries, -most, most).astype(kind)


def setup_inputs(seed: int = 0) -> dict:
    key_of = jax.random.split(jax.random.key(seed), 17)
    return {
        "hidden_in": noise(key_of[0], (TOKENS, D), 1.0, 6.0, ((0, 32),)),
        "queries": noise(key_of[1], (TOKENS, QDIM), 1.0, 6.0, ((0, 32),)),
        "new_keys": noise(key_of[2], (TOKENS, KVDIM), 1.0, 6.0, ((0, 32),)),
        "new_values": noise(key_of[3], (TOKENS, KVDIM), 1.0, 6.0, ((0, 32),)),
        "key_cache": draw_key_cache(jax.random.fold_in(key_of[16], 71), 0),
        "value_cache": noise(key_of[5], (CACHE_ROWS, KVDIM), 1.0, 6.0, ((0, 32),)),
        "cache_lengths": draw_cache_lengths(jax.random.fold_in(key_of[16], 71), 0),
        "parent_ids": draw_parent_ids(jax.random.fold_in(key_of[16], 71), 0),
        "accepted_leaf": plant(jax.random.randint(key_of[8], (REQ,), 0, TREE), jax.random.fold_in(key_of[8], 1), 0, TREE - 1).astype(jnp.int32),
        "query_gain": jnp.clip(1.0 + 0.1 * jax.random.normal(key_of[9], (HEAD_DIM,), jnp.float32), 0.5, 1.5).astype(jnp.bfloat16),
        "key_gain": jnp.clip(1.0 + 0.1 * jax.random.normal(key_of[10], (HEAD_DIM,), jnp.float32), 0.5, 1.5).astype(jnp.bfloat16),
        "post_gain": jnp.clip(1.0 + 0.1 * jax.random.normal(key_of[11], (D,), jnp.float32), 0.5, 1.5).astype(jnp.bfloat16),
        "out_weight": noise(key_of[12], (QDIM, D), QDIM ** -0.5, 0.09375, ((0, 8), (1, 4))),
        "gate_weight": noise(key_of[13], (D, FF), D ** -0.5, 0.09375, ((0, 8), (1, 4))),
        "up_weight": noise(key_of[14], (D, FF), D ** -0.5, 0.09375, ((0, 8), (1, 4))),
        "down_weight": noise(key_of[15], (FF, D), FF ** -0.5, 0.078125, ((0, 4), (1, 8))),
    }


NEG = -1e+30
EPS = 1e-06
ROPE_BASE = 1000000.0

def settle(values):
    return lax.optimization_barrier(values.astype(jnp.bfloat16)).astype(jnp.float32)

def head_norm(values, gain_vec):
    mean_sq = lax.optimization_barrier(jnp.mean(values * values, axis=-1, keepdims=True))
    return values * lax.rsqrt(mean_sq + EPS) * gain_vec.astype(jnp.float32)

def rotate(values, position):
    head_width = values.shape[-1]
    half_width = head_width // 2
    frequency = ROPE_BASE ** (-2.0 * jnp.arange(half_width, dtype=jnp.float32) / head_width)
    angles = position[:, None] * frequency[None, :]
    cosine = jnp.cos(angles)[:, None, :]
    sine_part = jnp.sin(angles)[:, None, :]
    front_half = values[..., :half_width]
    back_half = values[..., half_width:]
    return jnp.concatenate([front_half * cosine - back_half * sine_part, back_half * cosine + front_half * sine_part], axis=-1)

def ancestors(parent_row):
    node_count = parent_row.shape[0]
    node_ids = jnp.arange(node_count, dtype=jnp.int32)
    identity_mat = (node_ids[:, None] == node_ids[None, :]).astype(jnp.float32)
    parent_mat = (parent_row[:, None] == node_ids[None, :]).astype(jnp.float32) * (1.0 - identity_mat)
    reached = jnp.minimum(identity_mat + parent_mat, 1.0)
    for sweep in range(node_count.bit_length()):
        reached = jnp.minimum(jnp.dot(reached, reached, precision=lax.Precision.HIGHEST), 1.0)
    return reached

def reference(hidden_in, queries, new_keys, new_values, key_cache, value_cache, cache_lengths, parent_ids, accepted_leaf, query_gain, key_gain, post_gain, out_weight, gate_weight, up_weight, down_weight):
    group_size = HEADS // KV_HEADS
    score_scale = HEAD_DIM ** (-0.5)

    def one_request(packed):
        query_rows, key_rows, value_rows, cache_keys, cache_values, cache_length, parent_row, leaf_index = packed
        reached = ancestors(parent_row)
        node_depth = lax.optimization_barrier(jnp.sum(reached, axis=1)) - 1.0
        position = cache_length.astype(jnp.float32) + node_depth
        query_heads = rotate(head_norm(query_rows.astype(jnp.float32).reshape(TREE, HEADS, HEAD_DIM), query_gain), position).astype(jnp.bfloat16)
        key_heads = rotate(head_norm(key_rows.astype(jnp.float32).reshape(TREE, KV_HEADS, HEAD_DIM), key_gain), position).astype(jnp.bfloat16)
        grouped = query_heads.astype(jnp.float32).reshape(TREE, KV_HEADS, group_size, HEAD_DIM)
        stored_keys = cache_keys.astype(jnp.float32).reshape(CAP, KV_HEADS, HEAD_DIM)
        stored_values = cache_values.astype(jnp.float32).reshape(CAP, KV_HEADS, HEAD_DIM)
        draft_values = value_rows.astype(jnp.float32).reshape(TREE, KV_HEADS, HEAD_DIM)
        live_slots = jnp.arange(CAP, dtype=jnp.int32) < cache_length
        tree_mask = reached > 0.5
        cache_scores = jnp.where(live_slots, jnp.einsum('qhgd,khd->hgqk', grouped, stored_keys) * score_scale, NEG)
        tree_scores = jnp.where(tree_mask, jnp.einsum('qhgd,khd->hgqk', grouped, key_heads.astype(jnp.float32)) * score_scale, NEG)
        row_top = jnp.maximum(lax.optimization_barrier(jnp.max(cache_scores, axis=-1, keepdims=True)), lax.optimization_barrier(jnp.max(tree_scores, axis=-1, keepdims=True)))
        cache_weights = settle(jnp.where(live_slots, jnp.exp(cache_scores - row_top), 0.0))
        tree_weights = settle(jnp.where(tree_mask, jnp.exp(tree_scores - row_top), 0.0))
        weight_total = lax.optimization_barrier(jnp.sum(cache_weights, axis=-1, keepdims=True)) + lax.optimization_barrier(jnp.sum(tree_weights, axis=-1, keepdims=True))
        mixed = jnp.einsum('hgqk,khd->hgqd', cache_weights, stored_values) + jnp.einsum('hgqk,khd->hgqd', tree_weights, draft_values)
        attended = jnp.transpose(mixed / weight_total, (2, 0, 1, 3)).reshape(TREE, QDIM).astype(jnp.bfloat16)
        node_ids = jnp.arange(TREE, dtype=jnp.int32)
        leaf_pick = (node_ids == leaf_index).astype(jnp.float32)
        leaf_row = jnp.dot(leaf_pick, reached, precision=lax.Precision.HIGHEST)
        chosen = leaf_row[None, :] * (node_depth[None, :] == node_ids[:, None].astype(jnp.float32)).astype(jnp.float32)
        fresh_rows = jnp.concatenate([key_heads.reshape(TREE, KVDIM), value_rows], axis=1)
        compact = jnp.dot(chosen.astype(jnp.bfloat16), fresh_rows, preferred_element_type=jnp.float32).astype(jnp.bfloat16)
        return (attended, compact)
    attended, compact = lax.map(one_request, (queries.reshape(REQ, TREE, QDIM), new_keys.reshape(REQ, TREE, KVDIM), new_values.reshape(REQ, TREE, KVDIM), key_cache.reshape(REQ, CAP, KVDIM), value_cache.reshape(REQ, CAP, KVDIM), cache_lengths, parent_ids, accepted_leaf))
    attended = attended.reshape(TOKENS, QDIM)
    projected = jnp.dot(attended, out_weight, preferred_element_type=jnp.float32)
    residual = settle(hidden_in.astype(jnp.float32) + projected)
    mean_sq = lax.optimization_barrier(jnp.mean(residual * residual, axis=-1, keepdims=True))
    normed = (residual * lax.rsqrt(mean_sq + EPS) * post_gain.astype(jnp.float32)).astype(jnp.bfloat16)
    gate_sum = jnp.dot(normed, gate_weight, preferred_element_type=jnp.float32)
    up_sum = jnp.dot(normed, up_weight, preferred_element_type=jnp.float32)
    hidden = (jax.nn.silu(gate_sum) * up_sum).astype(jnp.bfloat16)
    mlp_sum = jnp.dot(hidden, down_weight, preferred_element_type=jnp.float32)
    layer_out = (residual + mlp_sum).astype(jnp.bfloat16)
    return (layer_out, compact.reshape(TOKENS, 2 * KVDIM))
```

```python
import functools

import jax
import jax.numpy as jnp
from jax import lax
from jax.experimental import pallas as pl
from jax.experimental.pallas import tpu as pltpu
from jax.sharding import PartitionSpec as P

HEADS = 32
KV_HEADS = 8
HEAD_DIM = 128


NEG = -1e30
EPS = 1e-06
ROPE_BASE = 1000000.0


def swapped(value, axis, bit):
    mask = 2**bit
    pairs = [(source, source ^ mask) for source in range(lax.axis_size(axis))]
    return lax.ppermute(value, axis, pairs)


def head_norm(values, gain_vec):
    mean_sq = jnp.mean(values * values, axis=-1, keepdims=True)
    return values * lax.rsqrt(mean_sq + EPS) * gain_vec.astype(jnp.float32)


def rotate(values, position):
    head_width = values.shape[-1]
    half_width = head_width // 2
    frequency = ROPE_BASE ** (-2.0 * jnp.arange(half_width, dtype=jnp.float32) / head_width)
    angles = position[:, None] * frequency[None, :]
    cosine = jnp.cos(angles)[:, None, :]
    sine_part = jnp.sin(angles)[:, None, :]
    front_half = values[..., :half_width]
    back_half = values[..., half_width:]
    return jnp.concatenate(
        [front_half * cosine - back_half * sine_part, back_half * cosine + front_half * sine_part],
        axis=-1,
    )


SIDE = 2
MESH = pl.DeviceIdType.MESH
ANY = pl.BlockSpec(memory_space=pl.ANY)


def meet(peers):
    barrier = pltpu.get_barrier_semaphore()
    for peer in peers:
        pl.semaphore_signal(barrier, inc=1, device_id=peer, device_id_type=MESH)
    pl.semaphore_wait(barrier, len(peers))


def remote(source, target, send_sem, recv_sem, peer):
    return pltpu.make_async_remote_copy(
        src_ref=source,
        dst_ref=target,
        send_sem=send_sem,
        recv_sem=recv_sem,
        device_id=peer,
        device_id_type=MESH,
    )


def line_of(along):
    tp_count = lax.axis_size("tp")
    req, tp = lax.axis_index("req"), lax.axis_index("tp")
    level, side = req // SIDE, req % SIDE
    if along == "level":
        return (
            lax.axis_size("req") // SIDE,
            level,
            lambda index: {"req": index * SIDE + side, "tp": tp},
        )
    return (
        SIDE * tp_count,
        side * tp_count + tp,
        lambda index: {"req": level * SIDE + index // tp_count, "tp": index % tp_count},
    )


def exchange_kernel(along, rows_ref, out_ref, send_sem, recv_sem, own_sem):
    count, mine, device = line_of(along)

    def part(index):
        return rows_ref.at[index]

    others = [(mine + step) % count for step in range(1, count)]
    meet([device(index) for index in others])
    copies = [
        remote(part(index), out_ref.at[mine], send_sem.at[at], recv_sem.at[at], device(index))
        for at, index in enumerate(others)
    ]
    for copy in copies:
        copy.start()
    own = pltpu.make_async_copy(part(mine), out_ref.at[mine], own_sem)
    own.start()
    for copy in copies:
        copy.wait()
    own.wait()


def exchange(rows, along, collective_id):
    count = lax.axis_size("req") // SIDE if along == "level" else SIDE * lax.axis_size("tp")
    part_shape = rows.shape[1:]
    return pl.pallas_call(
        functools.partial(exchange_kernel, along),
        out_shape=jax.ShapeDtypeStruct((count, *part_shape), rows.dtype),
        in_specs=[ANY],
        out_specs=ANY,
        scratch_shapes=[
            pltpu.SemaphoreType.DMA((count - 1,)),
            pltpu.SemaphoreType.DMA((count - 1,)),
            pltpu.SemaphoreType.DMA,
        ],
        compiler_params=pltpu.CompilerParams(collective_id=collective_id, has_side_effects=True),
    )(rows)


def reduce_kernel(
    along, mode, rows_ref, out_ref, landed, held,
    pair_send, pair_recv, far_send, far_recv, last_send, last_recv, own_sems,
):
    count, mine, device = line_of(along)
    half, place, parity = count // 2, mine // 2, mine % 2
    depth = landed.shape[1]
    piece = depth // 2

    def part(index, start, size):
        if mode == "inner":
            return rows_ref.at[pl.ds(start, size), index]
        return rows_ref.at[index, pl.ds(start, size)]

    order = [(place + step) % half for step in range(1, half)]
    pair = device(place * 2 + 1 - parity)
    far_devices = [device(index * 2 + parity) for index in order]
    meet(far_devices + [pair])
    inward, kept, outward = [], [], []
    for at, index in enumerate(order):
        for cut in range(2):
            copy = remote(
                part(index * 2 + 1 - parity, cut * piece, piece),
                landed.at[at, pl.ds(cut * piece, piece)],
                pair_send.at[at * 2 + cut],
                pair_recv.at[at * 2 + cut],
                pair,
            )
            copy.start()
            inward.append(copy)
        copy = pltpu.make_async_copy(
            part(index * 2 + parity, 0, depth), held.at[at], own_sems.at[at + 1]
        )
        copy.start()
        kept.append(copy)
    last = remote(
        part(place * 2 + 1 - parity, 0, depth), out_ref.at[1], last_send, last_recv, pair
    )
    last.start()
    own = pltpu.make_async_copy(part(mine, 0, depth), out_ref.at[0], own_sems.at[0])
    own.start()
    for at, peer in enumerate(far_devices):
        kept[at].wait()
        for cut in range(2):
            inward[at * 2 + cut].wait_recv()

            @pl.loop(cut * piece, (cut + 1) * piece)
            def _(row):
                total = held[at, row].astype(jnp.float32) + landed[at, row].astype(jnp.float32)
                held[at, row] = total.astype(held.dtype)

            copy = remote(
                held.at[at, pl.ds(cut * piece, piece)],
                out_ref.at[at + 2, pl.ds(cut * piece, piece)],
                far_send.at[at * 2 + cut],
                far_recv.at[at * 2 + cut],
                peer,
            )
            copy.start()
            outward.append(copy)
    own.wait()
    last.wait()
    for copy in inward:
        copy.wait_send()
    for copy in outward:
        copy.wait()


def reduced(rows, along, mode, collective_id):
    count = lax.axis_size("req") // SIDE if along == "level" else SIDE * lax.axis_size("tp")
    half = count // 2
    if mode == "inner":
        part_shape = rows.shape[:1] + rows.shape[2:]
    else:
        part_shape = rows.shape[1:]
    parts = pl.pallas_call(
        functools.partial(reduce_kernel, along, mode),
        out_shape=jax.ShapeDtypeStruct((half + 1, *part_shape), rows.dtype),
        in_specs=[ANY],
        out_specs=ANY,
        scratch_shapes=[
            pltpu.VMEM((half - 1, *part_shape), rows.dtype),
            pltpu.VMEM((half - 1, *part_shape), rows.dtype),
            pltpu.SemaphoreType.DMA((2 * (half - 1),)),
            pltpu.SemaphoreType.DMA((2 * (half - 1),)),
            pltpu.SemaphoreType.DMA((2 * (half - 1),)),
            pltpu.SemaphoreType.DMA((2 * (half - 1),)),
            pltpu.SemaphoreType.DMA,
            pltpu.SemaphoreType.DMA,
            pltpu.SemaphoreType.DMA((half,)),
        ],
        compiler_params=pltpu.CompilerParams(
            collective_id=collective_id, has_side_effects=True, vmem_limit_bytes=40 * 2**20
        ),
    )(rows)
    return jnp.sum(parts.astype(jnp.float32), axis=0)


def gather_kernel(rows_ref, out_ref, far_send, far_recv, near_send, near_recv, own_sem):
    count, mine, device = line_of("level")
    half, place, parity = count // 2, mine // 2, mine % 2
    pair = device(place * 2 + 1 - parity)
    order = [(place + step) % half for step in range(1, half)]
    far_devices = [device(index * 2 + parity) for index in order]
    meet(far_devices + [pair])
    far, near = [], []
    for cut in range(2):
        for peer in far_devices:
            at = len(far)
            copy = remote(
                rows_ref.at[cut], out_ref.at[mine, cut], far_send.at[at], far_recv.at[at], peer
            )
            copy.start()
            far.append(copy)
    own = pltpu.make_async_copy(rows_ref, out_ref.at[mine], own_sem)
    own.start()
    for cut in range(2):
        at = len(near)
        copy = remote(
            rows_ref.at[cut], out_ref.at[mine, cut], near_send.at[at], near_recv.at[at], pair
        )
        copy.start()
        near.append(copy)
    for cut in range(2):
        for step in range(1, half):
            far[cut * (half - 1) + step - 1].wait_recv()
            landed = out_ref.at[((place - step + half) % half) * 2 + parity, cut]
            at = len(near)
            copy = remote(landed, landed, near_send.at[at], near_recv.at[at], pair)
            copy.start()
            near.append(copy)
    own.wait()
    for copy in near:
        copy.wait()
    for copy in far:
        copy.wait_send()


def gathered_levels(rows, collective_id):
    count = lax.axis_size("req") // SIDE
    half = count // 2
    rows = rows.reshape(2, rows.shape[0] // 2, rows.shape[1])
    return pl.pallas_call(
        gather_kernel,
        out_shape=jax.ShapeDtypeStruct((count, *rows.shape), rows.dtype),
        in_specs=[ANY],
        out_specs=ANY,
        scratch_shapes=[
            pltpu.SemaphoreType.DMA((2 * (half - 1),)),
            pltpu.SemaphoreType.DMA((2 * (half - 1),)),
            pltpu.SemaphoreType.DMA((2 * half,)),
            pltpu.SemaphoreType.DMA((2 * half,)),
            pltpu.SemaphoreType.DMA,
        ],
        compiler_params=pltpu.CompilerParams(collective_id=collective_id, has_side_effects=True),
    )(rows)


def slices_kernel(
    rows_ref, out_ref, send_level, recv_level, send_far, recv_far, send_core, recv_core, own_sem
):
    tp_count = lax.axis_size("tp")
    levels = lax.axis_size("req") // SIDE
    req, tp = lax.axis_index("req"), lax.axis_index("tp")
    level, side = req // SIDE, req % SIDE
    place = side * tp_count + tp
    core, chip = tp % 2, place // 2
    chips = SIDE * tp_count // 2
    width = rows_ref.shape[1] // levels

    def columns(index):
        return rows_ref.at[:, pl.ds(pl.multiple_of(index * width, width), width)]

    def chip_place(index):
        return index * 2 + core

    def device(at):
        return {"req": level * SIDE + at // tp_count, "tp": at % tp_count}

    level_ids = [(level + step) % levels for step in range(1, levels)]
    level_devices = [{"req": index * SIDE + side, "tp": tp} for index in level_ids]
    far_devices = [device(chip_place((chip + step) % chips)) for step in range(1, chips)]
    core_device = device(chip * 2 + 1 - core)
    meet(level_devices + far_devices + [core_device])
    first = [
        remote(columns(index), out_ref.at[level, place], send_level.at[at], recv_level.at[at], peer)
        for at, (index, peer) in enumerate(zip(level_ids, level_devices))
    ]
    for copy in first:
        copy.start()
    own = pltpu.make_async_copy(columns(level), out_ref.at[level, place], own_sem)
    own.start()
    far, near = [], []
    for step in range(levels):
        source_level = (level - step + levels) % levels
        target = out_ref.at[source_level, place]
        if step > 0:
            first[step - 1].wait_recv()
        source = columns(level) if step == 0 else target
        for peer in far_devices:
            at = len(far)
            copy = remote(source, target, send_far.at[at], recv_far.at[at], peer)
            copy.start()
            far.append(copy)
        at = len(near)
        copy = remote(source, target, send_core.at[at], recv_core.at[at], core_device)
        copy.start()
        near.append(copy)
    for step in range(levels):
        source_level = (level - step + levels) % levels
        for hop in range(1, chips):
            far[step * (chips - 1) + hop - 1].wait_recv()
            landed = out_ref.at[source_level, chip_place((chip - hop + chips) % chips)]
            at = len(near)
            copy = remote(landed, landed, send_core.at[at], recv_core.at[at], core_device)
            copy.start()
            near.append(copy)
    own.wait()
    for copy in near:
        copy.wait()
    for copy in first + far:
        copy.wait_send()


def feature_slices(rows, collective_id):
    levels = lax.axis_size("req") // SIDE
    places = SIDE * lax.axis_size("tp")
    width = rows.shape[1] // levels
    chips = places // 2
    gathered = pl.pallas_call(
        slices_kernel,
        out_shape=jax.ShapeDtypeStruct((levels, places, rows.shape[0], width), rows.dtype),
        in_specs=[ANY],
        out_specs=ANY,
        scratch_shapes=[
            pltpu.SemaphoreType.DMA((levels - 1,)),
            pltpu.SemaphoreType.DMA((levels - 1,)),
            pltpu.SemaphoreType.DMA((levels * (chips - 1),)),
            pltpu.SemaphoreType.DMA((levels * (chips - 1),)),
            pltpu.SemaphoreType.DMA((levels * chips,)),
            pltpu.SemaphoreType.DMA((levels * chips,)),
            pltpu.SemaphoreType.DMA,
        ],
        compiler_params=pltpu.CompilerParams(collective_id=collective_id, has_side_effects=True),
    )(rows)
    return gathered.reshape(-1, width)


def paired_halves(shard, axis):
    side = lax.axis_index("req") % SIDE
    half = shard.shape[axis] // 2
    kept = lax.dynamic_slice_in_dim(shard, side * half, half, axis)
    sent = lax.dynamic_slice_in_dim(shard, (1 - side) * half, half, axis)
    return kept, sent


def joined(kept, received, axis):
    side = lax.axis_index("req") % SIDE
    low = jnp.where(side == 0, kept, received)
    high = jnp.where(side == 0, received, kept)
    return jnp.concatenate([low, high], axis=axis)


def attention_kernel(
    limit_ref, query_ref, key_ref, value_ref, fresh_key_ref, fresh_value_ref, allowed_ref,
    top_ref, total_ref, sum_ref,
):
    group_size = query_ref.shape[1] // HEAD_DIM
    query = jnp.concatenate(
        [query_ref[:, at * HEAD_DIM : (at + 1) * HEAD_DIM] for at in range(group_size)], axis=0
    )
    score_scale = HEAD_DIM ** (-0.5)
    limit = limit_ref[0]
    chunk = key_ref.shape[0] // 4

    def score(keys):
        return (
            lax.dot_general(
                query, keys, (((1,), (1,)), ((), ())), preferred_element_type=jnp.float32
            )
            * score_scale
        )

    def weigh(scores, top, allowed):
        weights = jnp.where(allowed, jnp.exp(scores - top), 0.0).astype(jnp.bfloat16)
        return weights, jnp.sum(weights.astype(jnp.float32), axis=-1, keepdims=True)

    allowed = jnp.concatenate([allowed_ref[...]] * group_size, axis=0) > 0.5
    scores = jnp.where(allowed, score(fresh_key_ref[...]), NEG)
    top = jnp.max(scores, axis=-1, keepdims=True)
    weights, total = weigh(scores, top, allowed)
    summed = jnp.dot(weights, fresh_value_ref[...], preferred_element_type=jnp.float32)

    def step(index, running):
        top, total, summed = running
        start = pl.multiple_of(index * chunk, chunk)
        keys = key_ref[pl.ds(start, chunk), :]
        values = value_ref[pl.ds(start, chunk), :]
        allowed = lax.broadcasted_iota(jnp.int32, (query.shape[0], chunk), 1) + start < limit
        scores = jnp.where(allowed, score(keys), NEG)
        new_top = jnp.maximum(top, jnp.max(scores, axis=-1, keepdims=True))
        weights, chunk_total = weigh(scores, new_top, allowed)
        shrink = jnp.exp(top - new_top)
        summed = summed * shrink + jnp.dot(weights, values, preferred_element_type=jnp.float32)
        return new_top, total * shrink + chunk_total, summed

    live = jnp.clip((limit + chunk - 1) // chunk, 0, 4)
    top, total, summed = lax.fori_loop(0, live, step, (top, total, summed))
    top_ref[0] = top
    total_ref[0] = total
    sum_ref[0] = summed


def attend(limit, query, keys, values, fresh_keys, fresh_values, allowed):
    rows, fresh_rows, cached_rows = query.shape[0], fresh_keys.shape[0], keys.shape[0]
    group_size = HEADS // KV_HEADS
    group_rows = rows * group_size

    def columns(block_rows, width):
        return pl.BlockSpec((block_rows, width), lambda head, limit_ref: (0, head))

    def lead(width):
        return pl.BlockSpec((1, group_rows, width), lambda head, limit_ref: (head, 0, 0))

    results = pl.pallas_call(
        attention_kernel,
        out_shape=[
            jax.ShapeDtypeStruct((KV_HEADS, group_rows, width), jnp.float32)
            for width in (1, 1, HEAD_DIM)
        ],
        grid_spec=pltpu.PrefetchScalarGridSpec(
            num_scalar_prefetch=1,
            grid=(KV_HEADS,),
            in_specs=[
                columns(rows, group_size * HEAD_DIM),
                columns(cached_rows, HEAD_DIM),
                columns(cached_rows, HEAD_DIM),
                columns(fresh_rows, HEAD_DIM),
                columns(fresh_rows, HEAD_DIM),
                pl.BlockSpec((rows, fresh_rows), lambda head, limit_ref: (0, 0)),
            ],
            out_specs=[lead(1), lead(1), lead(HEAD_DIM)],
        ),
        compiler_params=pltpu.CompilerParams(vmem_limit_bytes=32 * 2**20),
        cost_estimate=pl.CostEstimate(
            flops=4 * group_rows * cached_rows * KV_HEADS * HEAD_DIM,
            bytes_accessed=4 * cached_rows * KV_HEADS * HEAD_DIM,
            transcendentals=group_rows * cached_rows * KV_HEADS,
        ),
    )(limit, query, keys, values, fresh_keys, fresh_values, allowed)
    return [
        result.reshape(KV_HEADS, group_size, rows, result.shape[2]) for result in results
    ]


def ancestors(parent_row):
    node_count = parent_row.shape[0]
    node_ids = jnp.arange(node_count, dtype=jnp.int32)
    identity_mat = (node_ids[:, None] == node_ids[None, :]).astype(jnp.float32)
    parent_mat = (parent_row[:, None] == node_ids[None, :]).astype(jnp.float32) * (
        1.0 - identity_mat
    )
    reached = jnp.minimum(identity_mat + parent_mat, 1.0)
    for sweep in range(node_count.bit_length()):
        reached = jnp.minimum(jnp.dot(reached, reached, precision=lax.Precision.HIGHEST), 1.0)
    return reached


def per_device(
    hidden_in,
    queries,
    new_keys,
    new_values,
    key_cache,
    value_cache,
    cache_lengths,
    parent_ids,
    accepted_leaf,
    query_gain,
    key_gain,
    post_gain,
    out_weight,
    gate_weight,
    up_weight,
    down_weight,
):
    half_rows = queries.shape[0]
    out_kept, out_sent = paired_halves(out_weight, 1)
    out_received = swapped(out_sent, "req", 0)
    gate_kept, gate_sent = paired_halves(gate_weight, 1)
    up_kept, up_sent = paired_halves(up_weight, 1)
    gate_up_received = swapped(jnp.concatenate([gate_sent, up_sent], axis=1), "req", 0)
    gate_up_kept = jnp.concatenate([gate_kept, up_kept], axis=1)
    down_kept, down_sent = paired_halves(down_weight, 0)
    out_full = joined(out_kept, out_received, 0)
    gate_up_full = joined(gate_up_kept, gate_up_received, 0)
    tree_size = 2 * half_rows
    kv_width = new_keys.shape[1]
    q_width = queries.shape[1]
    tp_count = lax.axis_size("tp")
    device = lax.axis_index(("req", "tp"))
    request = device // 2
    pair_side = lax.axis_index("tp") % 2
    cache_length = lax.dynamic_index_in_dim(cache_lengths, request, 0, keepdims=False)
    parent_row = lax.dynamic_index_in_dim(parent_ids, request, 0, keepdims=False)
    leaf_index = lax.dynamic_index_in_dim(accepted_leaf, request, 0, keepdims=False)
    reached = ancestors(parent_row)
    node_depth = jnp.sum(reached, axis=1) - 1.0
    node_ids = jnp.arange(tree_size, dtype=jnp.int32)
    local_ids = jnp.arange(half_rows, dtype=jnp.int32)
    node_order = jnp.concatenate(
        [pair_side * half_rows + local_ids, (1 - pair_side) * half_rows + local_ids]
    )
    reorder = (node_order[:, None] == node_ids[None, :]).astype(jnp.float32)
    reached_rows = jnp.dot(reorder, reached, precision=lax.Precision.HIGHEST)
    own_cols = jnp.dot(reached_rows, reorder[:half_rows].T, precision=lax.Precision.HIGHEST) > 0.5
    own_depth = jnp.dot(reorder[:half_rows], node_depth, precision=lax.Precision.HIGHEST)
    position = cache_length.astype(jnp.float32) + own_depth
    query_heads = rotate(
        head_norm(queries.astype(jnp.float32).reshape(half_rows, HEADS, HEAD_DIM), query_gain),
        position,
    ).astype(jnp.bfloat16)
    key_heads = rotate(
        head_norm(new_keys.astype(jnp.float32).reshape(half_rows, KV_HEADS, HEAD_DIM), key_gain),
        position,
    ).astype(jnp.bfloat16)
    query_own = query_heads.reshape(half_rows, q_width)
    fresh_own = jnp.concatenate([key_heads.reshape(half_rows, kv_width), new_values], axis=1)
    query_other, fresh_other = swapped((query_own, fresh_own), "tp", 0)
    query_all = jnp.concatenate([query_own, query_other], axis=0)
    limit = (cache_length - pair_side * key_cache.shape[0]).reshape(1)
    run_top, run_total, summed = attend(
        limit,
        query_all,
        key_cache,
        value_cache,
        key_heads.reshape(half_rows, kv_width),
        new_values,
        own_cols.astype(jnp.float32),
    )
    far_top, far_total, far_sum = (
        swapped(run_top[:, :, half_rows:].astype(jnp.bfloat16), "tp", 0).astype(jnp.float32),
        swapped(run_total[:, :, half_rows:].astype(jnp.bfloat16), "tp", 0).astype(jnp.float32),
        swapped(summed[:, :, half_rows:].astype(jnp.bfloat16), "tp", 0).astype(jnp.float32),
    )
    near_top = run_top[:, :, :half_rows]
    joint_top = jnp.maximum(near_top, far_top)
    near_scale = jnp.exp(near_top - joint_top)
    far_scale = jnp.exp(far_top - joint_top)
    denominator = run_total[:, :, :half_rows] * near_scale + far_total * far_scale
    merged = (summed[:, :, :half_rows] * near_scale + far_sum * far_scale) / denominator
    attended = jnp.transpose(merged, (2, 0, 1, 3)).reshape(half_rows, q_width).astype(jnp.bfloat16)
    leaf_pick = (node_ids == leaf_index).astype(jnp.float32)
    leaf_row = jnp.dot(leaf_pick, reached, precision=lax.Precision.HIGHEST)
    out_depths = (pair_side * half_rows + local_ids).astype(jnp.float32)
    chosen = leaf_row[None, :] * (node_depth[None, :] == out_depths[:, None]).astype(jnp.float32)
    chosen = jnp.dot(chosen, reorder.T, precision=lax.Precision.HIGHEST)
    fresh_all = jnp.concatenate([fresh_own, fresh_other], axis=0)
    accepted_kv = jnp.dot(
        chosen.astype(jnp.bfloat16), fresh_all, preferred_element_type=jnp.float32
    ).astype(jnp.bfloat16)
    levels = lax.axis_size("req") // SIDE
    places = SIDE * tp_count
    attn_slice = feature_slices(attended, 0)
    attn_slice, down_sent = lax.optimization_barrier((attn_slice, down_sent))
    down_full = joined(down_kept, swapped(down_sent, "req", 0), 1)
    projected = jnp.dot(attn_slice, out_full, preferred_element_type=jnp.float32)
    projected = projected.astype(jnp.bfloat16).reshape(levels, places, half_rows, -1)
    projected = reduced(projected, "level", "lead", 1).astype(jnp.bfloat16)
    projected = exchange(projected.reshape(places, half_rows, -1), "place", 2)
    own_projected = jnp.transpose(
        projected.reshape(SIDE, tp_count, half_rows, -1), (2, 1, 0, 3)
    ).reshape(half_rows, -1)
    residual = (hidden_in.astype(jnp.float32) + own_projected.astype(jnp.float32)).astype(
        jnp.bfloat16
    )
    residual_wide = residual.astype(jnp.float32)
    mean_sq = jnp.mean(residual_wide * residual_wide, axis=-1, keepdims=True)
    normed = (residual_wide * lax.rsqrt(mean_sq + EPS) * post_gain.astype(jnp.float32)).astype(
        jnp.bfloat16
    )
    normed_slice = feature_slices(normed, 3)
    sums = jnp.dot(normed_slice, gate_up_full, preferred_element_type=jnp.float32)
    sums = sums.astype(jnp.bfloat16).reshape(levels, places, half_rows, -1)
    sums = reduced(sums, "level", "lead", 4).reshape(places * half_rows, -1)
    hidden_width = sums.shape[1] // 2
    hidden = (jax.nn.silu(sums[:, :hidden_width]) * sums[:, hidden_width:]).astype(jnp.bfloat16)
    hidden_all = gathered_levels(hidden, 5).reshape(-1, hidden_width)
    partial_out = jnp.dot(hidden_all, down_full, preferred_element_type=jnp.float32)
    partial_out = partial_out.astype(jnp.bfloat16).reshape(levels, places, half_rows, -1)
    paired_sum = reduced(partial_out, "place", "inner", 6).astype(jnp.bfloat16)
    mlp_own = exchange(paired_sum, "level", 7)
    mlp_own = jnp.transpose(mlp_own, (1, 0, 2)).reshape(half_rows, -1).astype(jnp.float32)
    layer_out = (residual_wide + mlp_own).astype(jnp.bfloat16)
    return (layer_out, accepted_kv)


def flip(value, bit):
    return 1 - value if bit else value


class Place:
    def __init__(self):
        req, tp = lax.axis_index("req"), lax.axis_index("tp")
        level = req // SIDE
        self.h, self.p = level // 2, level % 2
        self.x, self.y, self.c = req % SIDE, tp // 2, tp % 2

    def away(self, h=0, p=0, x=0, y=0, c=0):
        return self.at(flip(self.h, h), flip(self.p, p), flip(self.x, x), flip(self.y, y), flip(self.c, c))

    def at(self, h, p, x, y, c):
        return {"req": (h * 2 + p) * SIDE + x, "tp": y * 2 + c}


class Wires:
    def __init__(self, send_sems, recv_sems):
        self.send_sems, self.recv_sems = send_sems, recv_sems
        self.started = []

    def make(self, source, target, peer):
        at = len(self.started)
        copy = remote(source, target, self.send_sems.at[at], self.recv_sems.at[at], peer)
        self.started.append(copy)
        return copy

    def send(self, source, target, peer):
        copy = self.make(source, target, peer)
        copy.start()
        return copy


def aligned(value, by):
    return pl.multiple_of(value, by)


HOPS = ((0, 0), (1, 0), (0, 1), (1, 1))


class Gather:
    def __init__(self, place, wires, own_ref, all_ref, local_sem):
        self.place, self.wires, self.all_ref = place, wires, all_ref
        self.rows, self.width = own_ref.shape[0], all_ref.shape[2]
        at, width = place, self.width
        kept = own_ref.at[:, pl.ds(aligned(at.h * width, width), width)]
        given = own_ref.at[:, pl.ds(aligned((1 - at.h) * width, width), width)]
        self.far = wires.send(given, self.block(0, 0, 0), at.away(h=1))
        mine = self.block(0, 0, 0)
        self.local = pltpu.make_async_copy(kept, mine, local_sem)
        self.local.start()
        self.pair = [wires.send(kept, mine, at.away(p=1))]
        self.inward = {1: [], 2: [], 3: [None] * 4}
        self.core = {0: [], 1: [], 2: [], 3: []}
        self.spread(kept, 0, 0)

    def block(self, chunk, dh, dp):
        at = self.place
        level = flip(at.h, dh) * 2 + flip(at.p, dp)
        start = aligned((level * 2 + at.c) * self.rows, self.rows)
        return self.all_ref.at[chunk, pl.ds(start, self.rows)]

    def spread(self, source, dh, dp):
        at, wires = self.place, self.wires
        self.core[0].append(wires.send(source, self.block(0, dh, dp), at.away(c=1)))
        self.inward[1].append(wires.send(source, self.block(1, dh, dp), at.away(x=1)))
        self.inward[2].append(wires.send(source, self.block(2, dh, dp), at.away(y=1)))

    def own_column(self):
        far = self.block(0, 1, 0)
        self.far.wait_recv()
        self.pair.append(self.wires.send(far, far, self.place.away(p=1)))
        self.spread(far, 1, 0)
        self.pair[0].wait_recv()
        self.spread(self.block(0, 0, 1), 0, 1)
        self.pair[1].wait_recv()
        self.spread(self.block(0, 1, 1), 1, 1)
        self.local.wait()
        for copy in self.core[0]:
            copy.wait_recv()

    def forward(self, chunk):
        at, wires = self.place, self.wires
        order = ((0, 0), (1, 0), (0, 1), (1, 1))
        for index, (dh, dp) in enumerate(order):
            self.inward[chunk][index].wait_recv()
            block = self.block(chunk, dh, dp)
            self.core[chunk].append(wires.send(block, block, at.away(c=1)))
            if chunk == 1 and index % 2 == 0:
                self.inward[3][index] = wires.send(block, self.block(3, dh, dp), at.away(y=1))
            if chunk == 2 and index % 2 == 1:
                self.inward[3][index] = wires.send(block, self.block(3, dh, dp), at.away(x=1))

    def landed(self, chunk):
        for copy in self.core[chunk]:
            copy.wait_recv()


def layer_kernel(
    attended_ref, hidden_ref, gain_ref, out_w_ref, gate_w_ref, up_w_ref, down_w_ref,
    o_ref,
    att_all, norm_all, out_w, gate_up_w, down_w,
    out_total, out_sent, out_landed, out_done, projected, residual_ref, normed_ref,
    total, sums_sent, sums_landed, hidden_all,
    partial, partial_landed, pair_sent, pair_landed, last_sent, final,
    send_sems, recv_sems, local_sems,
):
    at = Place()
    wires = Wires(send_sems, recv_sems)
    rows = attended_ref.shape[0]
    column = 4 * 2 * rows
    half_rows = column // 2
    local = []

    def keep(source, target):
        copy = pltpu.make_async_copy(source, target, local_sems.at[len(local)])
        local.append(copy)
        copy.start()
        return copy

    barrier = pltpu.get_barrier_semaphore()
    peers = [
        at.away(p=dp, x=dx, y=dy, c=dc)
        for dp in range(2) for dx in range(2) for dy in range(2) for dc in range(2)
        if dp + dx + dy + dc
    ] + [at.away(h=1), at.away(h=1, c=1)]
    for peer in peers:
        pl.semaphore_signal(barrier, inc=1, device_id=peer, device_id_type=MESH)
    pl.semaphore_wait(barrier, len(peers))

    def row_block(ref, start_col, cols):
        depth = ref.shape[0] // 4
        start = aligned((at.p * 2 + at.x) * depth, depth)
        return ref.at[pl.ds(start, depth), pl.ds(start_col, cols)]

    def quarters(source_ref, target_ref, start_col):
        width = source_ref.shape[1] // 4
        copies = []
        for dp, dx in ((0, 1), (1, 0), (1, 1)):
            quarter = flip(at.p, dp) * 2 + flip(at.x, dx)
            source = source_ref.at[:, pl.ds(aligned(quarter * width, width), width)]
            copies.append(
                wires.send(source, row_block(target_ref, start_col, width), at.away(p=dp, x=dx))
            )
        quarter = at.p * 2 + at.x
        source = source_ref.at[:, pl.ds(aligned(quarter * width, width), width)]
        own = keep(source, row_block(target_ref, start_col, width))
        return copies, own

    def down_blocks():
        depth, width = down_w.shape[0] // 2, down_w_ref.shape[1]
        target = down_w.at[
            pl.ds(aligned(at.c * depth, depth), depth), pl.ds(aligned(at.x * width, width), width)
        ]
        copies = []
        for da, db in ((0, 1), (1, 0), (1, 1), (0, 0)):
            pt, xt, ct = flip(at.c, db), flip(at.x, da), at.p
            start = aligned((pt * 2 + xt) * depth, depth)
            source = down_w_ref.at[pl.ds(start, depth)]
            copies.append(wires.make(source, target, at.at(at.h, pt, xt, at.y, ct)))
            if da + db:
                copies[-1].start()
        own = pltpu.make_async_copy(
            down_w_ref.at[pl.ds(aligned((at.p * 2 + at.x) * depth, depth), depth)],
            target,
            local_sems.at[7],
        )

        @pl.when(at.p != at.c)
        def _():
            copies[-1].start()

        @pl.when(at.p == at.c)
        def _():
            own.start()

        return copies, own

    def arrived(copies, own):
        for copy in copies:
            copy.wait_recv()
        own.wait()

    moving_out = quarters(out_w_ref, out_w, 0)
    gather = Gather(at, wires, attended_ref, att_all, local_sems.at[8])
    gather.own_column()
    moving_gate = quarters(gate_w_ref, gate_up_w, 0)
    moving_up = quarters(up_w_ref, gate_up_w, gate_up_w.shape[1] // 2)

    near = pl.ds(aligned(at.h * half_rows, half_rows), half_rows)
    far = pl.ds(aligned((1 - at.h) * half_rows, half_rows), half_rows)
    tile = 256

    def multiply(chunk, all_ref, weight, total_ref, sent_ref):
        @pl.loop(0, weight.shape[1] // tile)
        def _(index):
            cols = pl.ds(aligned(index * tile, tile), tile)
            total_ref[chunk, :, cols] = jnp.dot(
                all_ref[chunk], weight[:, cols], preferred_element_type=jnp.float32
            )
        sent_ref[chunk] = total_ref[chunk, far, :].astype(sent_ref.dtype)

    arrived(*moving_out)
    crossing = []

    def project(chunk):
        multiply(chunk, att_all, out_w, out_total, out_sent)
        crossing.append(wires.send(out_sent.at[chunk], out_landed.at[chunk], at.away(h=1)))

    project(0)
    gather.forward(1)
    gather.forward(2)
    gather.landed(1)
    project(1)
    gather.landed(2)
    project(2)
    gather.forward(3)
    gather.landed(3)
    project(3)
    moving_down = down_blocks()
    width = out_w.shape[1]

    def out_column(p, x, y, c):
        return pl.ds(aligned((y * 2 + c) * (4 * width) + (p * 2 + x) * width, width), width)

    own_cols = out_column(at.p, at.x, at.y, at.c)
    returning = []
    for chunk, (dx, dy) in enumerate(HOPS):
        crossing[chunk].wait_recv()
        done = out_total[chunk, near, :] + out_landed[chunk].astype(jnp.float32)
        out_done[chunk] = done.astype(out_done.dtype)
        for dp in range(2):
            for dc in range(2):
                start = aligned((flip(at.p, dp) * 2 + flip(at.c, dc)) * rows, rows)
                source = out_done.at[chunk, pl.ds(start, rows)]
                target = projected.at[:, own_cols]
                if dx + dy + dp + dc:
                    returning.append(
                        wires.send(source, target, at.away(p=dp, x=dx, y=dy, c=dc))
                    )
                else:
                    own_projected = keep(source, target)
    for copy in returning:
        copy.wait_recv()
    own_projected.wait()
    residual = (hidden_ref[...].astype(jnp.float32) + projected[...].astype(jnp.float32)).astype(
        jnp.bfloat16
    )
    residual_ref[...] = residual
    wide = residual.astype(jnp.float32)
    mean_sq = jnp.mean(wide * wide, axis=-1, keepdims=True)
    normed_ref[...] = (
        wide * lax.rsqrt(mean_sq + EPS) * gain_ref[...].astype(jnp.float32)
    ).astype(jnp.bfloat16)

    gather = Gather(at, wires, normed_ref, norm_all, local_sems.at[9])
    gather.own_column()
    arrived(*moving_gate)
    arrived(*moving_up)
    units = gate_up_w.shape[1] // 2
    own_units = pl.ds(aligned(at.c * units, units), units)
    crossing, hidden_far, hidden_core = [], [], {}

    def expand(chunk):
        multiply(chunk, norm_all, gate_up_w, total, sums_sent)
        crossing.append(wires.send(sums_sent.at[chunk], sums_landed.at[chunk], at.away(h=1)))

    def activate(chunk):
        crossing[chunk].wait_recv()
        gate = total[chunk, near, :units] + sums_landed[chunk, :, :units].astype(jnp.float32)
        up = total[chunk, near, units:] + sums_landed[chunk, :, units:].astype(jnp.float32)
        hidden = gate / (1.0 + jnp.exp(-gate)) * up
        hidden_all[chunk, near, own_units] = hidden.astype(hidden_all.dtype)
        block = hidden_all.at[chunk, near, own_units]
        hidden_far.append(wires.send(block, block, at.away(h=1)))
        hidden_core[chunk] = [wires.send(block, block, at.away(c=1))]

    def relay(chunk):
        hidden_far[chunk].wait_recv()
        block = hidden_all.at[chunk, far, own_units]
        hidden_core[chunk].append(wires.send(block, block, at.away(c=1)))

    back = {}

    def contract(chunk):
        for copy in hidden_core[chunk]:
            copy.wait_recv()

        @pl.loop(0, down_w.shape[1] // tile)
        def _(index):
            cols = pl.ds(aligned(index * tile, tile), tile)
            partial[chunk, :, cols] = jnp.dot(
                hidden_all[chunk], down_w[:, cols], preferred_element_type=jnp.float32
            ).astype(partial.dtype)

        dx, dy = HOPS[chunk]
        if chunk:
            back[chunk] = wires.send(
                partial.at[chunk], partial_landed.at[chunk - 1], at.away(x=dx, y=dy)
            )

    expand(0)
    gather.forward(1)
    gather.forward(2)
    gather.landed(1)
    expand(1)
    activate(0)
    gather.landed(2)
    expand(2)
    gather.forward(3)
    activate(1)
    relay(0)
    gather.landed(3)
    expand(3)
    activate(2)
    relay(1)
    down_copies, down_own = moving_down
    for copy in down_copies[:-1]:
        copy.wait_recv()

    @pl.when(at.p != at.c)
    def _():
        down_copies[-1].wait_recv()

    @pl.when(at.p == at.c)
    def _():
        down_own.wait()

    contract(1)
    activate(3)
    relay(2)
    contract(2)
    relay(3)
    contract(3)
    contract(0)

    level_rows = 2 * rows
    for chunk in (1, 2, 3):
        back[chunk].wait_recv()

    def level_sum(level):
        span = pl.ds(aligned(level * level_rows, level_rows), level_rows)
        sums = partial[0, span, :].astype(jnp.float32)
        for chunk in range(3):
            sums = sums + partial_landed[chunk, span, :].astype(jnp.float32)
        return sums

    paired = []
    for half in range(2):
        pair_sent[half] = level_sum(half * 2 + 1 - at.p).astype(pair_sent.dtype)
        paired.append(wires.send(pair_sent.at[half], pair_landed.at[half], at.away(p=1)))
    out_width = last_sent.shape[2]
    final_cols = pl.ds(aligned((at.h * 2 + at.c) * out_width, out_width), out_width)
    for half in range(2):
        paired[half].wait_recv()
        last_sent[half] = (
            level_sum(half * 2 + at.p) + pair_landed[half].astype(jnp.float32)
        ).astype(last_sent.dtype)
    lasting = []
    for dh, dc in ((1, 0), (1, 1), (0, 1), (0, 0)):
        start = aligned(flip(at.c, dc) * rows, rows)
        source = last_sent.at[flip(at.h, dh), pl.ds(start, rows)]
        target = final.at[:, final_cols]
        if dh + dc:
            lasting.append(wires.send(source, target, at.away(h=dh, c=dc)))
        else:
            own_last = keep(source, target)
    for copy in lasting:
        copy.wait_recv()
    own_last.wait()
    o_ref[...] = (
        residual_ref[...].astype(jnp.float32) + final[...].astype(jnp.float32)
    ).astype(o_ref.dtype)

    for copy in wires.started:
        if copy is not down_copies[-1]:
            copy.wait_send()

    @pl.when(at.p != at.c)
    def _():
        down_copies[-1].wait_send()


SEMAPHORES = 192


def fused_layer(attended, hidden_in, post_gain, out_weight, gate_weight, up_weight, down_weight):
    rows, model = attended.shape
    column = 8 * rows
    out_cols = out_weight.shape[1] // 4
    units = gate_weight.shape[1] // 4
    bf16, f32 = jnp.bfloat16, jnp.float32
    vmem = pl.BlockSpec(memory_space=pltpu.VMEM)
    return pl.pallas_call(
        layer_kernel,
        out_shape=jax.ShapeDtypeStruct((rows, model), bf16),
        in_specs=[vmem, vmem, vmem, ANY, ANY, ANY, ANY],
        out_specs=vmem,
        scratch_shapes=[
            pltpu.VMEM((4, column, model // 2), bf16),
            pltpu.VMEM((4, column, model // 2), bf16),
            pltpu.VMEM((model // 2, out_cols), bf16),
            pltpu.VMEM((model // 2, 2 * units), bf16),
            pltpu.VMEM((2 * units, model // 4), bf16),
            pltpu.VMEM((4, column, out_cols), f32),
            pltpu.VMEM((4, column // 2, out_cols), bf16),
            pltpu.VMEM((4, column // 2, out_cols), bf16),
            pltpu.VMEM((4, column // 2, out_cols), bf16),
            pltpu.VMEM((rows, model), bf16),
            pltpu.VMEM((rows, model), bf16),
            pltpu.VMEM((rows, model), bf16),
            pltpu.VMEM((4, column, 2 * units), f32),
            pltpu.VMEM((4, column // 2, 2 * units), bf16),
            pltpu.VMEM((4, column // 2, 2 * units), bf16),
            pltpu.VMEM((4, column, 2 * units), bf16),
            pltpu.VMEM((4, column, model // 4), bf16),
            pltpu.VMEM((3, column, model // 4), bf16),
            pltpu.VMEM((2, 2 * rows, model // 4), bf16),
            pltpu.VMEM((2, 2 * rows, model // 4), bf16),
            pltpu.VMEM((2, 2 * rows, model // 4), bf16),
            pltpu.VMEM((rows, model), bf16),
            pltpu.SemaphoreType.DMA((SEMAPHORES,)),
            pltpu.SemaphoreType.DMA((SEMAPHORES,)),
            pltpu.SemaphoreType.DMA((10,)),
        ],
        compiler_params=pltpu.CompilerParams(
            collective_id=8, has_side_effects=True, vmem_limit_bytes=48 * 2**20
        ),
    )(attended, hidden_in, post_gain.reshape(1, -1), out_weight, gate_weight, up_weight, down_weight)


def attended_of(
    queries, new_keys, new_values, key_cache, value_cache, cache_lengths, parent_ids,
    accepted_leaf, query_gain, key_gain,
):
    half_rows = queries.shape[0]
    tree_size = 2 * half_rows
    kv_width = new_keys.shape[1]
    q_width = queries.shape[1]
    tp_count = lax.axis_size("tp")
    device = lax.axis_index(("req", "tp"))
    request = device // 2
    pair_side = lax.axis_index("tp") % 2
    cache_length = lax.dynamic_index_in_dim(cache_lengths, request, 0, keepdims=False)
    parent_row = lax.dynamic_index_in_dim(parent_ids, request, 0, keepdims=False)
    leaf_index = lax.dynamic_index_in_dim(accepted_leaf, request, 0, keepdims=False)
    reached = ancestors(parent_row)
    node_depth = jnp.sum(reached, axis=1) - 1.0
    node_ids = jnp.arange(tree_size, dtype=jnp.int32)
    local_ids = jnp.arange(half_rows, dtype=jnp.int32)
    node_order = jnp.concatenate(
        [pair_side * half_rows + local_ids, (1 - pair_side) * half_rows + local_ids]
    )
    reorder = (node_order[:, None] == node_ids[None, :]).astype(jnp.float32)
    reached_rows = jnp.dot(reorder, reached, precision=lax.Precision.HIGHEST)
    own_cols = jnp.dot(reached_rows, reorder[:half_rows].T, precision=lax.Precision.HIGHEST) > 0.5
    own_depth = jnp.dot(reorder[:half_rows], node_depth, precision=lax.Precision.HIGHEST)
    position = cache_length.astype(jnp.float32) + own_depth
    query_heads = rotate(
        head_norm(queries.astype(jnp.float32).reshape(half_rows, HEADS, HEAD_DIM), query_gain),
        position,
    ).astype(jnp.bfloat16)
    key_heads = rotate(
        head_norm(new_keys.astype(jnp.float32).reshape(half_rows, KV_HEADS, HEAD_DIM), key_gain),
        position,
    ).astype(jnp.bfloat16)
    query_own = query_heads.reshape(half_rows, q_width)
    fresh_own = jnp.concatenate([key_heads.reshape(half_rows, kv_width), new_values], axis=1)
    query_other, fresh_other = swapped((query_own, fresh_own), "tp", 0)
    query_all = jnp.concatenate([query_own, query_other], axis=0)
    limit = (cache_length - pair_side * key_cache.shape[0]).reshape(1)
    run_top, run_total, summed = attend(
        limit,
        query_all,
        key_cache,
        value_cache,
        key_heads.reshape(half_rows, kv_width),
        new_values,
        own_cols.astype(jnp.float32),
    )
    far_top, far_total, far_sum = (
        swapped(run_top[:, :, half_rows:].astype(jnp.bfloat16), "tp", 0).astype(jnp.float32),
        swapped(run_total[:, :, half_rows:].astype(jnp.bfloat16), "tp", 0).astype(jnp.float32),
        swapped(summed[:, :, half_rows:].astype(jnp.bfloat16), "tp", 0).astype(jnp.float32),
    )
    near_top = run_top[:, :, :half_rows]
    joint_top = jnp.maximum(near_top, far_top)
    near_scale = jnp.exp(near_top - joint_top)
    far_scale = jnp.exp(far_top - joint_top)
    denominator = run_total[:, :, :half_rows] * near_scale + far_total * far_scale
    merged = (summed[:, :, :half_rows] * near_scale + far_sum * far_scale) / denominator
    attended = jnp.transpose(merged, (2, 0, 1, 3)).reshape(half_rows, q_width).astype(jnp.bfloat16)
    leaf_pick = (node_ids == leaf_index).astype(jnp.float32)
    leaf_row = jnp.dot(leaf_pick, reached, precision=lax.Precision.HIGHEST)
    out_depths = (pair_side * half_rows + local_ids).astype(jnp.float32)
    chosen = leaf_row[None, :] * (node_depth[None, :] == out_depths[:, None]).astype(jnp.float32)
    chosen = jnp.dot(chosen, reorder.T, precision=lax.Precision.HIGHEST)
    fresh_all = jnp.concatenate([fresh_own, fresh_other], axis=0)
    accepted_kv = jnp.dot(
        chosen.astype(jnp.bfloat16), fresh_all, preferred_element_type=jnp.float32
    ).astype(jnp.bfloat16)
    return attended, accepted_kv


def per_device_halves(
    hidden_in, queries, new_keys, new_values, key_cache, value_cache, cache_lengths, parent_ids,
    accepted_leaf, query_gain, key_gain, post_gain, out_weight, gate_weight, up_weight, down_weight,
):
    attended, accepted_kv = attended_of(
        queries, new_keys, new_values, key_cache, value_cache, cache_lengths, parent_ids,
        accepted_leaf, query_gain, key_gain,
    )
    layer_out = fused_layer(
        attended, hidden_in, post_gain, out_weight, gate_weight, up_weight, down_weight
    )
    return layer_out, accepted_kv


def solution(mesh):
    in_specs = (
        P(("req", "tp"), None),
        P(("req", "tp"), None),
        P(("req", "tp"), None),
        P(("req", "tp"), None),
        P(("req", "tp"), None),
        P(("req", "tp"), None),
        P(),
        P(),
        P(),
        P(),
        P(),
        P(),
        P("req", "tp"),
        P("req", "tp"),
        P("req", "tp"),
        P("tp", "req"),
    )
    out_specs = (P(("req", "tp"), None), P(("req", "tp"), None))
    by_halves = mesh.shape["req"] == 4 * SIDE and mesh.shape["tp"] == 4
    return jax.shard_map(
        per_device_halves if by_halves else per_device, mesh=mesh, in_specs=in_specs, out_specs=out_specs, check_vma=False
    )
```

```python
import functools

import jax
import jax.numpy as jnp
from jax import lax
from jax.experimental import pallas as pl
from jax.experimental.pallas import tpu as pltpu
from jax.sharding import PartitionSpec as P

HEADS = 32
KV_HEADS = 8
HEAD_DIM = 128


NEG = -1e30
EPS = 1e-06
ROPE_BASE = 1000000.0


def swapped(value, axis, bit):
    mask = 2**bit
    pairs = [(source, source ^ mask) for source in range(lax.axis_size(axis))]
    return lax.ppermute(value, axis, pairs)


def head_norm(values, gain_vec):
    mean_sq = jnp.mean(values * values, axis=-1, keepdims=True)
    return values * lax.rsqrt(mean_sq + EPS) * gain_vec.astype(jnp.float32)


def rotate(values, position):
    head_width = values.shape[-1]
    half_width = head_width // 2
    frequency = ROPE_BASE ** (-2.0 * jnp.arange(half_width, dtype=jnp.float32) / head_width)
    angles = position[:, None] * frequency[None, :]
    cosine = jnp.cos(angles)[:, None, :]
    sine_part = jnp.sin(angles)[:, None, :]
    front_half = values[..., :half_width]
    back_half = values[..., half_width:]
    return jnp.concatenate(
        [front_half * cosine - back_half * sine_part, back_half * cosine + front_half * sine_part],
        axis=-1,
    )


SIDE = 2
MESH = pl.DeviceIdType.MESH
ANY = pl.BlockSpec(memory_space=pl.ANY)


def meet(peers):
    barrier = pltpu.get_barrier_semaphore()
    for peer in peers:
        pl.semaphore_signal(barrier, inc=1, device_id=peer, device_id_type=MESH)
    pl.semaphore_wait(barrier, len(peers))


def remote(source, target, send_sem, recv_sem, peer):
    return pltpu.make_async_remote_copy(
        src_ref=source,
        dst_ref=target,
        send_sem=send_sem,
        recv_sem=recv_sem,
        device_id=peer,
        device_id_type=MESH,
    )


def line_of(along):
    tp_count = lax.axis_size("tp")
    req, tp = lax.axis_index("req"), lax.axis_index("tp")
    level, side = req // SIDE, req % SIDE
    if along == "level":
        return (
            lax.axis_size("req") // SIDE,
            level,
            lambda index: {"req": index * SIDE + side, "tp": tp},
        )
    return (
        SIDE * tp_count,
        side * tp_count + tp,
        lambda index: {"req": level * SIDE + index // tp_count, "tp": index % tp_count},
    )


def exchange_kernel(along, rows_ref, out_ref, send_sem, recv_sem, own_sem):
    count, mine, device = line_of(along)

    def part(index):
        return rows_ref.at[index]

    others = [(mine + step) % count for step in range(1, count)]
    meet([device(index) for index in others])
    copies = [
        remote(part(index), out_ref.at[mine], send_sem.at[at], recv_sem.at[at], device(index))
        for at, index in enumerate(others)
    ]
    for copy in copies:
        copy.start()
    own = pltpu.make_async_copy(part(mine), out_ref.at[mine], own_sem)
    own.start()
    for copy in copies:
        copy.wait()
    own.wait()


def exchange(rows, along, collective_id):
    count = lax.axis_size("req") // SIDE if along == "level" else SIDE * lax.axis_size("tp")
    part_shape = rows.shape[1:]
    return pl.pallas_call(
        functools.partial(exchange_kernel, along),
        out_shape=jax.ShapeDtypeStruct((count, *part_shape), rows.dtype),
        in_specs=[ANY],
        out_specs=ANY,
        scratch_shapes=[
            pltpu.SemaphoreType.DMA((count - 1,)),
            pltpu.SemaphoreType.DMA((count - 1,)),
            pltpu.SemaphoreType.DMA,
        ],
        compiler_params=pltpu.CompilerParams(collective_id=collective_id, has_side_effects=True),
    )(rows)


def reduce_kernel(
    along, mode, rows_ref, out_ref, landed, held,
    pair_send, pair_recv, far_send, far_recv, last_send, last_recv, own_sems,
):
    count, mine, device = line_of(along)
    half, place, parity = count // 2, mine // 2, mine % 2
    depth = landed.shape[1]
    piece = depth // 2

    def part(index, start, size):
        if mode == "inner":
            return rows_ref.at[pl.ds(start, size), index]
        return rows_ref.at[index, pl.ds(start, size)]

    order = [(place + step) % half for step in range(1, half)]
    pair = device(place * 2 + 1 - parity)
    far_devices = [device(index * 2 + parity) for index in order]
    meet(far_devices + [pair])
    inward, kept, outward = [], [], []
    for at, index in enumerate(order):
        for cut in range(2):
            copy = remote(
                part(index * 2 + 1 - parity, cut * piece, piece),
                landed.at[at, pl.ds(cut * piece, piece)],
                pair_send.at[at * 2 + cut],
                pair_recv.at[at * 2 + cut],
                pair,
            )
            copy.start()
            inward.append(copy)
        copy = pltpu.make_async_copy(
            part(index * 2 + parity, 0, depth), held.at[at], own_sems.at[at + 1]
        )
        copy.start()
        kept.append(copy)
    last = remote(
        part(place * 2 + 1 - parity, 0, depth), out_ref.at[1], last_send, last_recv, pair
    )
    last.start()
    own = pltpu.make_async_copy(part(mine, 0, depth), out_ref.at[0], own_sems.at[0])
    own.start()
    for at, peer in enumerate(far_devices):
        kept[at].wait()
        for cut in range(2):
            inward[at * 2 + cut].wait_recv()

            @pl.loop(cut * piece, (cut + 1) * piece)
            def _(row):
                total = held[at, row].astype(jnp.float32) + landed[at, row].astype(jnp.float32)
                held[at, row] = total.astype(held.dtype)

            copy = remote(
                held.at[at, pl.ds(cut * piece, piece)],
                out_ref.at[at + 2, pl.ds(cut * piece, piece)],
                far_send.at[at * 2 + cut],
                far_recv.at[at * 2 + cut],
                peer,
            )
            copy.start()
            outward.append(copy)
    own.wait()
    last.wait()
    for copy in inward:
        copy.wait_send()
    for copy in outward:
        copy.wait()


def reduced(rows, along, mode, collective_id):
    count = lax.axis_size("req") // SIDE if along == "level" else SIDE * lax.axis_size("tp")
    half = count // 2
    if mode == "inner":
        part_shape = rows.shape[:1] + rows.shape[2:]
    else:
        part_shape = rows.shape[1:]
    parts = pl.pallas_call(
        functools.partial(reduce_kernel, along, mode),
        out_shape=jax.ShapeDtypeStruct((half + 1, *part_shape), rows.dtype),
        in_specs=[ANY],
        out_specs=ANY,
        scratch_shapes=[
            pltpu.VMEM((half - 1, *part_shape), rows.dtype),
            pltpu.VMEM((half - 1, *part_shape), rows.dtype),
            pltpu.SemaphoreType.DMA((2 * (half - 1),)),
            pltpu.SemaphoreType.DMA((2 * (half - 1),)),
            pltpu.SemaphoreType.DMA((2 * (half - 1),)),
            pltpu.SemaphoreType.DMA((2 * (half - 1),)),
            pltpu.SemaphoreType.DMA,
            pltpu.SemaphoreType.DMA,
            pltpu.SemaphoreType.DMA((half,)),
        ],
        compiler_params=pltpu.CompilerParams(
            collective_id=collective_id, has_side_effects=True, vmem_limit_bytes=40 * 2**20
        ),
    )(rows)
    return jnp.sum(parts.astype(jnp.float32), axis=0)


def gather_kernel(rows_ref, out_ref, far_send, far_recv, near_send, near_recv, own_sem):
    count, mine, device = line_of("level")
    half, place, parity = count // 2, mine // 2, mine % 2
    pair = device(place * 2 + 1 - parity)
    order = [(place + step) % half for step in range(1, half)]
    far_devices = [device(index * 2 + parity) for index in order]
    meet(far_devices + [pair])
    far, near = [], []
    for cut in range(2):
        for peer in far_devices:
            at = len(far)
            copy = remote(
                rows_ref.at[cut], out_ref.at[mine, cut], far_send.at[at], far_recv.at[at], peer
            )
            copy.start()
            far.append(copy)
    own = pltpu.make_async_copy(rows_ref, out_ref.at[mine], own_sem)
    own.start()
    for cut in range(2):
        at = len(near)
        copy = remote(
            rows_ref.at[cut], out_ref.at[mine, cut], near_send.at[at], near_recv.at[at], pair
        )
        copy.start()
        near.append(copy)
    for cut in range(2):
        for step in range(1, half):
            far[cut * (half - 1) + step - 1].wait_recv()
            landed = out_ref.at[((place - step + half) % half) * 2 + parity, cut]
            at = len(near)
            copy = remote(landed, landed, near_send.at[at], near_recv.at[at], pair)
            copy.start()
            near.append(copy)
    own.wait()
    for copy in near:
        copy.wait()
    for copy in far:
        copy.wait_send()


def gathered_levels(rows, collective_id):
    count = lax.axis_size("req") // SIDE
    half = count // 2
    rows = rows.reshape(2, rows.shape[0] // 2, rows.shape[1])
    return pl.pallas_call(
        gather_kernel,
        out_shape=jax.ShapeDtypeStruct((count, *rows.shape), rows.dtype),
        in_specs=[ANY],
        out_specs=ANY,
        scratch_shapes=[
            pltpu.SemaphoreType.DMA((2 * (half - 1),)),
            pltpu.SemaphoreType.DMA((2 * (half - 1),)),
            pltpu.SemaphoreType.DMA((2 * half,)),
            pltpu.SemaphoreType.DMA((2 * half,)),
            pltpu.SemaphoreType.DMA,
        ],
        compiler_params=pltpu.CompilerParams(collective_id=collective_id, has_side_effects=True),
    )(rows)


def slices_kernel(
    rows_ref, out_ref, send_level, recv_level, send_far, recv_far, send_core, recv_core, own_sem
):
    tp_count = lax.axis_size("tp")
    levels = lax.axis_size("req") // SIDE
    req, tp = lax.axis_index("req"), lax.axis_index("tp")
    level, side = req // SIDE, req % SIDE
    place = side * tp_count + tp
    core, chip = tp % 2, place // 2
    chips = SIDE * tp_count // 2
    width = rows_ref.shape[1] // levels

    def columns(index):
        return rows_ref.at[:, pl.ds(pl.multiple_of(index * width, width), width)]

    def chip_place(index):
        return index * 2 + core

    def device(at):
        return {"req": level * SIDE + at // tp_count, "tp": at % tp_count}

    level_ids = [(level + step) % levels for step in range(1, levels)]
    level_devices = [{"req": index * SIDE + side, "tp": tp} for index in level_ids]
    far_devices = [device(chip_place((chip + step) % chips)) for step in range(1, chips)]
    core_device = device(chip * 2 + 1 - core)
    meet(level_devices + far_devices + [core_device])
    first = [
        remote(columns(index), out_ref.at[level, place], send_level.at[at], recv_level.at[at], peer)
        for at, (index, peer) in enumerate(zip(level_ids, level_devices))
    ]
    for copy in first:
        copy.start()
    own = pltpu.make_async_copy(columns(level), out_ref.at[level, place], own_sem)
    own.start()
    far, near = [], []
    for step in range(levels):
        source_level = (level - step + levels) % levels
        target = out_ref.at[source_level, place]
        if step > 0:
            first[step - 1].wait_recv()
        source = columns(level) if step == 0 else target
        for peer in far_devices:
            at = len(far)
            copy = remote(source, target, send_far.at[at], recv_far.at[at], peer)
            copy.start()
            far.append(copy)
        at = len(near)
        copy = remote(source, target, send_core.at[at], recv_core.at[at], core_device)
        copy.start()
        near.append(copy)
    for step in range(levels):
        source_level = (level - step + levels) % levels
        for hop in range(1, chips):
            far[step * (chips - 1) + hop - 1].wait_recv()
            landed = out_ref.at[source_level, chip_place((chip - hop + chips) % chips)]
            at = len(near)
            copy = remote(landed, landed, send_core.at[at], recv_core.at[at], core_device)
            copy.start()
            near.append(copy)
    own.wait()
    for copy in near:
        copy.wait()
    for copy in first + far:
        copy.wait_send()


def feature_slices(rows, collective_id):
    levels = lax.axis_size("req") // SIDE
    places = SIDE * lax.axis_size("tp")
    width = rows.shape[1] // levels
    chips = places // 2
    gathered = pl.pallas_call(
        slices_kernel,
        out_shape=jax.ShapeDtypeStruct((levels, places, rows.shape[0], width), rows.dtype),
        in_specs=[ANY],
        out_specs=ANY,
        scratch_shapes=[
            pltpu.SemaphoreType.DMA((levels - 1,)),
            pltpu.SemaphoreType.DMA((levels - 1,)),
            pltpu.SemaphoreType.DMA((levels * (chips - 1),)),
            pltpu.SemaphoreType.DMA((levels * (chips - 1),)),
            pltpu.SemaphoreType.DMA((levels * chips,)),
            pltpu.SemaphoreType.DMA((levels * chips,)),
            pltpu.SemaphoreType.DMA,
        ],
        compiler_params=pltpu.CompilerParams(collective_id=collective_id, has_side_effects=True),
    )(rows)
    return gathered.reshape(-1, width)


def paired_halves(shard, axis):
    side = lax.axis_index("req") % SIDE
    half = shard.shape[axis] // 2
    kept = lax.dynamic_slice_in_dim(shard, side * half, half, axis)
    sent = lax.dynamic_slice_in_dim(shard, (1 - side) * half, half, axis)
    return kept, sent


def joined(kept, received, axis):
    side = lax.axis_index("req") % SIDE
    low = jnp.where(side == 0, kept, received)
    high = jnp.where(side == 0, received, kept)
    return jnp.concatenate([low, high], axis=axis)


def attention_kernel(
    limit_ref, query_ref, key_ref, value_ref, fresh_key_ref, fresh_value_ref, allowed_ref,
    top_ref, total_ref, sum_ref,
):
    group_size = query_ref.shape[1] // HEAD_DIM
    query = jnp.concatenate(
        [query_ref[:, at * HEAD_DIM : (at + 1) * HEAD_DIM] for at in range(group_size)], axis=0
    )
    score_scale = HEAD_DIM ** (-0.5)
    limit = limit_ref[0]
    chunk = key_ref.shape[0] // 4

    def score(keys):
        return (
            lax.dot_general(
                query, keys, (((1,), (1,)), ((), ())), preferred_element_type=jnp.float32
            )
            * score_scale
        )

    def weigh(scores, top, allowed):
        weights = jnp.where(allowed, jnp.exp(scores - top), 0.0).astype(jnp.bfloat16)
        return weights, jnp.sum(weights.astype(jnp.float32), axis=-1, keepdims=True)

    allowed = jnp.concatenate([allowed_ref[...]] * group_size, axis=0) > 0.5
    scores = jnp.where(allowed, score(fresh_key_ref[...]), NEG)
    top = jnp.max(scores, axis=-1, keepdims=True)
    weights, total = weigh(scores, top, allowed)
    summed = jnp.dot(weights, fresh_value_ref[...], preferred_element_type=jnp.float32)

    def step(index, running):
        top, total, summed = running
        start = pl.multiple_of(index * chunk, chunk)
        keys = key_ref[pl.ds(start, chunk), :]
        values = value_ref[pl.ds(start, chunk), :]
        allowed = lax.broadcasted_iota(jnp.int32, (query.shape[0], chunk), 1) + start < limit
        scores = jnp.where(allowed, score(keys), NEG)
        new_top = jnp.maximum(top, jnp.max(scores, axis=-1, keepdims=True))
        weights, chunk_total = weigh(scores, new_top, allowed)
        shrink = jnp.exp(top - new_top)
        summed = summed * shrink + jnp.dot(weights, values, preferred_element_type=jnp.float32)
        return new_top, total * shrink + chunk_total, summed

    live = jnp.clip((limit + chunk - 1) // chunk, 0, 4)
    top, total, summed = lax.fori_loop(0, live, step, (top, total, summed))
    top_ref[0] = top
    total_ref[0] = total
    sum_ref[0] = summed


def attend(limit, query, keys, values, fresh_keys, fresh_values, allowed):
    rows, fresh_rows, cached_rows = query.shape[0], fresh_keys.shape[0], keys.shape[0]
    group_size = HEADS // KV_HEADS
    group_rows = rows * group_size

    def columns(block_rows, width):
        return pl.BlockSpec((block_rows, width), lambda head, limit_ref: (0, head))

    def lead(width):
        return pl.BlockSpec((1, group_rows, width), lambda head, limit_ref: (head, 0, 0))

    results = pl.pallas_call(
        attention_kernel,
        out_shape=[
            jax.ShapeDtypeStruct((KV_HEADS, group_rows, width), jnp.float32)
            for width in (1, 1, HEAD_DIM)
        ],
        grid_spec=pltpu.PrefetchScalarGridSpec(
            num_scalar_prefetch=1,
            grid=(KV_HEADS,),
            in_specs=[
                columns(rows, group_size * HEAD_DIM),
                columns(cached_rows, HEAD_DIM),
                columns(cached_rows, HEAD_DIM),
                columns(fresh_rows, HEAD_DIM),
                columns(fresh_rows, HEAD_DIM),
                pl.BlockSpec((rows, fresh_rows), lambda head, limit_ref: (0, 0)),
            ],
            out_specs=[lead(1), lead(1), lead(HEAD_DIM)],
        ),
        compiler_params=pltpu.CompilerParams(vmem_limit_bytes=32 * 2**20),
        cost_estimate=pl.CostEstimate(
            flops=4 * group_rows * cached_rows * KV_HEADS * HEAD_DIM,
            bytes_accessed=4 * cached_rows * KV_HEADS * HEAD_DIM,
            transcendentals=group_rows * cached_rows * KV_HEADS,
        ),
    )(limit, query, keys, values, fresh_keys, fresh_values, allowed)
    return [
        result.reshape(KV_HEADS, group_size, rows, result.shape[2]) for result in results
    ]


def ancestors(parent_row):
    node_count = parent_row.shape[0]
    node_ids = jnp.arange(node_count, dtype=jnp.int32)
    identity_mat = (node_ids[:, None] == node_ids[None, :]).astype(jnp.float32)
    parent_mat = (parent_row[:, None] == node_ids[None, :]).astype(jnp.float32) * (
        1.0 - identity_mat
    )
    reached = jnp.minimum(identity_mat + parent_mat, 1.0)
    for sweep in range(node_count.bit_length()):
        reached = jnp.minimum(jnp.dot(reached, reached, precision=lax.Precision.HIGHEST), 1.0)
    return reached


def per_device(
    hidden_in,
    queries,
    new_keys,
    new_values,
    key_cache,
    value_cache,
    cache_lengths,
    parent_ids,
    accepted_leaf,
    query_gain,
    key_gain,
    post_gain,
    out_weight,
    gate_weight,
    up_weight,
    down_weight,
):
    half_rows = queries.shape[0]
    out_kept, out_sent = paired_halves(out_weight, 1)
    out_received = swapped(out_sent, "req", 0)
    gate_kept, gate_sent = paired_halves(gate_weight, 1)
    up_kept, up_sent = paired_halves(up_weight, 1)
    gate_up_received = swapped(jnp.concatenate([gate_sent, up_sent], axis=1), "req", 0)
    gate_up_kept = jnp.concatenate([gate_kept, up_kept], axis=1)
    down_kept, down_sent = paired_halves(down_weight, 0)
    out_full = joined(out_kept, out_received, 0)
    gate_up_full = joined(gate_up_kept, gate_up_received, 0)
    tree_size = 2 * half_rows
    kv_width = new_keys.shape[1]
    q_width = queries.shape[1]
    tp_count = lax.axis_size("tp")
    device = lax.axis_index(("req", "tp"))
    request = device // 2
    pair_side = lax.axis_index("tp") % 2
    cache_length = lax.dynamic_index_in_dim(cache_lengths, request, 0, keepdims=False)
    parent_row = lax.dynamic_index_in_dim(parent_ids, request, 0, keepdims=False)
    leaf_index = lax.dynamic_index_in_dim(accepted_leaf, request, 0, keepdims=False)
    reached = ancestors(parent_row)
    node_depth = jnp.sum(reached, axis=1) - 1.0
    node_ids = jnp.arange(tree_size, dtype=jnp.int32)
    local_ids = jnp.arange(half_rows, dtype=jnp.int32)
    node_order = jnp.concatenate(
        [pair_side * half_rows + local_ids, (1 - pair_side) * half_rows + local_ids]
    )
    reorder = (node_order[:, None] == node_ids[None, :]).astype(jnp.float32)
    reached_rows = jnp.dot(reorder, reached, precision=lax.Precision.HIGHEST)
    own_cols = jnp.dot(reached_rows, reorder[:half_rows].T, precision=lax.Precision.HIGHEST) > 0.5
    own_depth = jnp.dot(reorder[:half_rows], node_depth, precision=lax.Precision.HIGHEST)
    position = cache_length.astype(jnp.float32) + own_depth
    query_heads = rotate(
        head_norm(queries.astype(jnp.float32).reshape(half_rows, HEADS, HEAD_DIM), query_gain),
        position,
    ).astype(jnp.bfloat16)
    key_heads = rotate(
        head_norm(new_keys.astype(jnp.float32).reshape(half_rows, KV_HEADS, HEAD_DIM), key_gain),
        position,
    ).astype(jnp.bfloat16)
    query_own = query_heads.reshape(half_rows, q_width)
    fresh_own = jnp.concatenate([key_heads.reshape(half_rows, kv_width), new_values], axis=1)
    query_other, fresh_other = swapped((query_own, fresh_own), "tp", 0)
    query_all = jnp.concatenate([query_own, query_other], axis=0)
    limit = (cache_length - pair_side * key_cache.shape[0]).reshape(1)
    run_top, run_total, summed = attend(
        limit,
        query_all,
        key_cache,
        value_cache,
        key_heads.reshape(half_rows, kv_width),
        new_values,
        own_cols.astype(jnp.float32),
    )
    far_top, far_total, far_sum = (
        swapped(run_top[:, :, half_rows:].astype(jnp.bfloat16), "tp", 0).astype(jnp.float32),
        swapped(run_total[:, :, half_rows:].astype(jnp.bfloat16), "tp", 0).astype(jnp.float32),
        swapped(summed[:, :, half_rows:].astype(jnp.bfloat16), "tp", 0).astype(jnp.float32),
    )
    near_top = run_top[:, :, :half_rows]
    joint_top = jnp.maximum(near_top, far_top)
    near_scale = jnp.exp(near_top - joint_top)
    far_scale = jnp.exp(far_top - joint_top)
    denominator = run_total[:, :, :half_rows] * near_scale + far_total * far_scale
    merged = (summed[:, :, :half_rows] * near_scale + far_sum * far_scale) / denominator
    attended = jnp.transpose(merged, (2, 0, 1, 3)).reshape(half_rows, q_width).astype(jnp.bfloat16)
    leaf_pick = (node_ids == leaf_index).astype(jnp.float32)
    leaf_row = jnp.dot(leaf_pick, reached, precision=lax.Precision.HIGHEST)
    out_depths = (pair_side * half_rows + local_ids).astype(jnp.float32)
    chosen = leaf_row[None, :] * (node_depth[None, :] == out_depths[:, None]).astype(jnp.float32)
    chosen = jnp.dot(chosen, reorder.T, precision=lax.Precision.HIGHEST)
    fresh_all = jnp.concatenate([fresh_own, fresh_other], axis=0)
    accepted_kv = jnp.dot(
        chosen.astype(jnp.bfloat16), fresh_all, preferred_element_type=jnp.float32
    ).astype(jnp.bfloat16)
    levels = lax.axis_size("req") // SIDE
    places = SIDE * tp_count
    attn_slice = feature_slices(attended, 0)
    attn_slice, down_sent = lax.optimization_barrier((attn_slice, down_sent))
    down_full = joined(down_kept, swapped(down_sent, "req", 0), 1)
    projected = jnp.dot(attn_slice, out_full, preferred_element_type=jnp.float32)
    projected = projected.astype(jnp.bfloat16).reshape(levels, places, half_rows, -1)
    projected = reduced(projected, "level", "lead", 1).astype(jnp.bfloat16)
    projected = exchange(projected.reshape(places, half_rows, -1), "place", 2)
    own_projected = jnp.transpose(
        projected.reshape(SIDE, tp_count, half_rows, -1), (2, 1, 0, 3)
    ).reshape(half_rows, -1)
    residual = (hidden_in.astype(jnp.float32) + own_projected.astype(jnp.float32)).astype(
        jnp.bfloat16
    )
    residual_wide = residual.astype(jnp.float32)
    mean_sq = jnp.mean(residual_wide * residual_wide, axis=-1, keepdims=True)
    normed = (residual_wide * lax.rsqrt(mean_sq + EPS) * post_gain.astype(jnp.float32)).astype(
        jnp.bfloat16
    )
    normed_slice = feature_slices(normed, 3)
    sums = jnp.dot(normed_slice, gate_up_full, preferred_element_type=jnp.float32)
    sums = sums.astype(jnp.bfloat16).reshape(levels, places, half_rows, -1)
    sums = reduced(sums, "level", "lead", 4).reshape(places * half_rows, -1)
    hidden_width = sums.shape[1] // 2
    hidden = (jax.nn.silu(sums[:, :hidden_width]) * sums[:, hidden_width:]).astype(jnp.bfloat16)
    hidden_all = gathered_levels(hidden, 5).reshape(-1, hidden_width)
    partial_out = jnp.dot(hidden_all, down_full, preferred_element_type=jnp.float32)
    partial_out = partial_out.astype(jnp.bfloat16).reshape(levels, places, half_rows, -1)
    paired_sum = reduced(partial_out, "place", "inner", 6).astype(jnp.bfloat16)
    mlp_own = exchange(paired_sum, "level", 7)
    mlp_own = jnp.transpose(mlp_own, (1, 0, 2)).reshape(half_rows, -1).astype(jnp.float32)
    layer_out = (residual_wide + mlp_own).astype(jnp.bfloat16)
    return (layer_out, accepted_kv)


def flip(value, bit):
    return 1 - value if bit else value


class Place:
    def __init__(self):
        req, tp = lax.axis_index("req"), lax.axis_index("tp")
        level = req // SIDE
        self.h, self.p = level // 2, level % 2
        self.x, self.y, self.c = req % SIDE, tp // 2, tp % 2

    def away(self, h=0, p=0, x=0, y=0, c=0):
        return self.at(flip(self.h, h), flip(self.p, p), flip(self.x, x), flip(self.y, y), flip(self.c, c))

    def at(self, h, p, x, y, c):
        return {"req": (h * 2 + p) * SIDE + x, "tp": y * 2 + c}


class Wires:
    def __init__(self, send_sems, recv_sems):
        self.send_sems, self.recv_sems = send_sems, recv_sems
        self.started = []

    def make(self, source, target, peer):
        at = len(self.started)
        copy = remote(source, target, self.send_sems.at[at], self.recv_sems.at[at], peer)
        self.started.append(copy)
        return copy

    def send(self, source, target, peer):
        copy = self.make(source, target, peer)
        copy.start()
        return copy


def aligned(value, by):
    return pl.multiple_of(value, by)


HOPS = ((0, 0), (1, 0), (0, 1), (1, 1))


class Gather:
    def __init__(self, place, wires, own_ref, all_ref, local_sem):
        self.place, self.wires, self.all_ref = place, wires, all_ref
        self.rows, self.width = own_ref.shape[0], all_ref.shape[2]
        at, width = place, self.width
        kept = own_ref.at[:, pl.ds(aligned(at.h * width, width), width)]
        given = own_ref.at[:, pl.ds(aligned((1 - at.h) * width, width), width)]
        self.far = wires.send(given, self.block(0, 0, 0), at.away(h=1))
        mine = self.block(0, 0, 0)
        self.local = pltpu.make_async_copy(kept, mine, local_sem)
        self.local.start()
        self.pair = [wires.send(kept, mine, at.away(p=1))]
        self.inward = {1: [], 2: [], 3: [None] * 4}
        self.core = {0: [], 1: [], 2: [], 3: []}
        self.spread(kept, 0, 0)

    def block(self, chunk, dh, dp):
        at = self.place
        level = flip(at.h, dh) * 2 + flip(at.p, dp)
        start = aligned((level * 2 + at.c) * self.rows, self.rows)
        return self.all_ref.at[chunk, pl.ds(start, self.rows)]

    def spread(self, source, dh, dp):
        at, wires = self.place, self.wires
        self.core[0].append(wires.send(source, self.block(0, dh, dp), at.away(c=1)))
        self.inward[1].append(wires.send(source, self.block(1, dh, dp), at.away(x=1)))
        self.inward[2].append(wires.send(source, self.block(2, dh, dp), at.away(y=1)))

    def own_column(self):
        far = self.block(0, 1, 0)
        self.far.wait_recv()
        self.pair.append(self.wires.send(far, far, self.place.away(p=1)))
        self.spread(far, 1, 0)
        self.pair[0].wait_recv()
        self.spread(self.block(0, 0, 1), 0, 1)
        self.pair[1].wait_recv()
        self.spread(self.block(0, 1, 1), 1, 1)
        self.local.wait()
        for copy in self.core[0]:
            copy.wait_recv()

    def forward(self, chunk):
        at, wires = self.place, self.wires
        order = ((0, 0), (1, 0), (0, 1), (1, 1))
        for index, (dh, dp) in enumerate(order):
            self.inward[chunk][index].wait_recv()
            block = self.block(chunk, dh, dp)
            self.core[chunk].append(wires.send(block, block, at.away(c=1)))
            if chunk == 1 and index % 2 == 0:
                self.inward[3][index] = wires.send(block, self.block(3, dh, dp), at.away(y=1))
            if chunk == 2 and index % 2 == 1:
                self.inward[3][index] = wires.send(block, self.block(3, dh, dp), at.away(x=1))

    def landed(self, chunk):
        for copy in self.core[chunk]:
            copy.wait_recv()


def normalized(values, gain):
    mean_sq = jnp.mean(values * values, axis=-1, keepdims=True)
    return values * lax.rsqrt(mean_sq + EPS) * gain


def closure(parent_row):
    count = parent_row.shape[1]
    down = lax.broadcasted_iota(jnp.int32, (count, count), 0)
    across = lax.broadcasted_iota(jnp.int32, (count, count), 1)
    same = down == across
    identity = jnp.where(same, 1.0, 0.0).astype(jnp.bfloat16)
    turned = jnp.where(same | (parent_row == down), 1.0, 0.0)
    for sweep in range((count - 1).bit_length()):
        factor = turned.astype(jnp.bfloat16)
        turned = jnp.minimum(jnp.dot(factor, factor, preferred_element_type=jnp.float32), 1.0)
    reached = lax.dot_general(
        identity, turned.astype(jnp.bfloat16), (((1,), (1,)), ((), ())),
        preferred_element_type=jnp.float32,
    )
    return reached, turned


def attention_phase(
    at, request, lengths_ref, leaf_ref, parent_ref, frequency_ref, query_gain_ref, key_gain_ref,
    query_rows, key_rows, value_rows, arrived_rows, arrived_cache, cache_k, cache_v,
    query_heads, key_heads, mixed, accepted_ref,
):
    bf16, f32 = jnp.bfloat16, jnp.float32
    tree = key_rows.shape[0]
    rows = tree // 2
    groups = query_heads.shape[0]
    group_size = HEADS // KV_HEADS
    reached, turned = closure(parent_ref[pl.ds(request, 1), :])
    length = lengths_ref[request]
    depth = jnp.sum(reached, axis=1, keepdims=True) - 1.0
    depth_across = jnp.sum(turned, axis=0, keepdims=True) - 1.0
    angles = (length.astype(f32) + depth) * frequency_ref[...]
    lane = lax.broadcasted_iota(jnp.int32, angles.shape, 1)
    cosine = jnp.cos(angles)
    sine = jnp.where(lane < HEAD_DIM // 2, -1.0, 1.0) * jnp.sin(angles)

    def rotated(values, gain_ref):
        normed = normalized(values.astype(f32), gain_ref[...].astype(f32))
        return (normed * cosine + pltpu.roll(normed, HEAD_DIM // 2, 1) * sine).astype(bf16)

    def lanes(head):
        return pl.ds(aligned(head * HEAD_DIM, HEAD_DIM), HEAD_DIM)

    arrived_rows()
    for group in range(groups):
        for member in range(group_size):
            head = group * group_size + member
            query_heads[group, pl.ds(member * tree, tree), :] = rotated(
                query_rows[:, head * HEAD_DIM : (head + 1) * HEAD_DIM], query_gain_ref
            )
    for head in range(KV_HEADS):
        span = slice(head * HEAD_DIM, (head + 1) * HEAD_DIM)
        key_heads[:, span] = rotated(key_rows[:, span], key_gain_ref)

    node = lax.broadcasted_iota(jnp.int32, (tree, tree), 0)
    leaf_row = jnp.sum(jnp.where(node == leaf_ref[request], reached, 0.0), axis=0, keepdims=True)
    place = (at.c * rows + lax.broadcasted_iota(jnp.int32, (rows, tree), 0)).astype(f32)
    chosen = jnp.where(depth_across == place, leaf_row, 0.0).astype(bf16)
    kv_width = key_heads.shape[1]
    accepted_ref[:, :kv_width] = jnp.dot(
        chosen, key_heads[...], preferred_element_type=f32
    ).astype(bf16)
    accepted_ref[:, kv_width:] = jnp.dot(
        chosen, value_rows[...], preferred_element_type=f32
    ).astype(bf16)

    scale = HEAD_DIM**-0.5 * 1.4426950408889634
    tree_bias = jnp.where(reached > 0.5, 0.0, NEG)
    tree_bias = jnp.concatenate([tree_bias] * group_size, axis=0)
    chunk = cache_k.shape[0] // 4
    position = lax.broadcasted_iota(jnp.int32, (1, chunk), 1)
    biases = [
        jnp.where(position + index * chunk < length, 0.0, NEG) for index in range(4)
    ]

    def score(query, keys, bias):
        scores = lax.dot_general(
            query, keys, (((1,), (1,)), ((), ())), preferred_element_type=f32
        )
        return scores * scale + bias

    def weighed(scores, top, values):
        weights = jnp.exp2(scores - top).astype(bf16)
        ones = jnp.ones(values.shape, bf16)
        return jnp.dot(
            weights, jnp.concatenate([values, ones], axis=1), preferred_element_type=f32
        )

    arrived_cache()

    @pl.loop(0, groups)
    def _(group):
        query = query_heads[group]
        own = lanes(at.c * groups + group)
        scores = score(query, key_heads[:, own], tree_bias)
        top = jnp.max(scores, axis=-1, keepdims=True)
        summed = weighed(scores, top, value_rows[:, own])
        for index in range(4):
            span = pl.ds(index * chunk, chunk)
            scores = score(query, cache_k[span, lanes(group)], biases[index])
            new_top = jnp.maximum(top, jnp.max(scores, axis=-1, keepdims=True))
            summed = summed * jnp.exp2(top - new_top) + weighed(
                scores, new_top, cache_v[span, lanes(group)]
            )
            top = new_top
        result = (summed[:, :HEAD_DIM] / summed[:, HEAD_DIM:]).astype(bf16)
        for member in range(group_size):
            mixed[:, lanes(group * group_size + member)] = result[
                member * tree : (member + 1) * tree
            ]


def layer_kernel(
    lengths_ref, leaf_ref, parent_ref, frequency_ref, query_gain_ref, key_gain_ref, gain_ref,
    queries_ref, new_keys_ref, new_values_ref, key_cache_ref, value_cache_ref, hidden_in_ref,
    out_w_ref, gate_w_ref, up_w_ref, down_w_ref,
    o_ref, accepted_ref,
    query_rows, key_rows, value_rows, cache_k, cache_v, query_heads, key_heads, mixed, attended_ref,
    hidden_ref,
    att_all, norm_all, out_w, gate_up_w, down_w,
    out_total, out_sent, out_landed, out_done, projected, residual_ref, normed_ref,
    total, sums_sent, sums_landed, hidden_all,
    partial, partial_landed, pair_sent, pair_landed, last_sent, final,
    send_sems, recv_sems, local_sems,
):
    at = Place()
    wires = Wires(send_sems, recv_sems)
    rows = queries_ref.shape[0]
    column = 4 * 2 * rows
    half_rows = column // 2
    local = []

    def keep(source, target):
        copy = pltpu.make_async_copy(source, target, local_sems.at[len(local)])
        local.append(copy)
        copy.start()
        return copy

    barrier = pltpu.get_barrier_semaphore()
    peers = [
        at.away(p=dp, x=dx, y=dy, c=dc)
        for dp in range(2) for dx in range(2) for dy in range(2) for dc in range(2)
        if dp + dx + dy + dc
    ] + [at.away(h=1), at.away(h=1, c=1)]
    for peer in peers:
        pl.semaphore_signal(barrier, inc=1, device_id=peer, device_id_type=MESH)
    pl.semaphore_wait(barrier, len(peers))

    def row_block(ref, start_col, cols):
        depth = ref.shape[0] // 4
        start = aligned((at.p * 2 + at.x) * depth, depth)
        return ref.at[pl.ds(start, depth), pl.ds(start_col, cols)]

    def quarters(source_ref, target_ref, start_col):
        width = source_ref.shape[1] // 4
        copies = []
        for dp, dx in ((0, 1), (1, 0), (1, 1)):
            quarter = flip(at.p, dp) * 2 + flip(at.x, dx)
            source = source_ref.at[:, pl.ds(aligned(quarter * width, width), width)]
            copies.append(
                wires.send(source, row_block(target_ref, start_col, width), at.away(p=dp, x=dx))
            )
        quarter = at.p * 2 + at.x
        source = source_ref.at[:, pl.ds(aligned(quarter * width, width), width)]
        own = keep(source, row_block(target_ref, start_col, width))
        return copies, own

    def down_blocks():
        depth, width = down_w.shape[0] // 2, down_w_ref.shape[1]
        target = down_w.at[
            pl.ds(aligned(at.c * depth, depth), depth), pl.ds(aligned(at.x * width, width), width)
        ]
        copies = []
        for da, db in ((0, 1), (1, 0), (1, 1), (0, 0)):
            pt, xt, ct = flip(at.c, db), flip(at.x, da), at.p
            start = aligned((pt * 2 + xt) * depth, depth)
            source = down_w_ref.at[pl.ds(start, depth)]
            copies.append(wires.make(source, target, at.at(at.h, pt, xt, at.y, ct)))
            if da + db:
                copies[-1].start()
        own = pltpu.make_async_copy(
            down_w_ref.at[pl.ds(aligned((at.p * 2 + at.x) * depth, depth), depth)],
            target,
            local_sems.at[13],
        )

        @pl.when(at.p != at.c)
        def _():
            copies[-1].start()

        @pl.when(at.p == at.c)
        def _():
            own.start()

        return copies, own

    def arrived(copies, own):
        for copy in copies:
            copy.wait_recv()
        own.wait()

    def shared(source_ref, target_ref, split):
        depth, width = source_ref.shape[0], target_ref.shape[1]
        target = target_ref.at[pl.ds(aligned(at.c * depth, depth), depth)]
        if not split:
            own = given = source_ref
        else:
            own = source_ref.at[:, pl.ds(aligned(at.c * width, width), width)]
            given = source_ref.at[:, pl.ds(aligned((1 - at.c) * width, width), width)]
        return [wires.send(given, target, at.away(c=1))], keep(own, target)

    moving_rows = [
        shared(queries_ref, query_rows, True),
        shared(new_keys_ref, key_rows, False),
        shared(new_values_ref, value_rows, False),
    ]
    moving_cache = [
        shared(key_cache_ref, cache_k, True),
        shared(value_cache_ref, cache_v, True),
    ]
    moving_out = quarters(out_w_ref, out_w, 0)
    moving_gate = quarters(gate_w_ref, gate_up_w, 0)
    own_hidden = keep(hidden_in_ref, hidden_ref)
    request = ((at.h * 2 + at.p) * SIDE + at.x) * 2 + at.y

    def arrived_rows():
        for moving in moving_rows:
            arrived(*moving)

    def arrived_cache():
        for moving in moving_cache:
            arrived(*moving)

    attention_phase(
        at, request, lengths_ref, leaf_ref, parent_ref, frequency_ref, query_gain_ref,
        key_gain_ref, query_rows, key_rows, value_rows, arrived_rows, arrived_cache,
        cache_k, cache_v, query_heads, key_heads, mixed, accepted_ref,
    )
    mixed_width = mixed.shape[1]
    mixed_target = attended_ref.at[:, pl.ds(aligned(at.c * mixed_width, mixed_width), mixed_width)]
    mixed_copy = wires.send(
        mixed.at[pl.ds(aligned((1 - at.c) * rows, rows), rows)], mixed_target, at.away(c=1)
    )
    own_mixed = keep(mixed.at[pl.ds(aligned(at.c * rows, rows), rows)], mixed_target)
    arrived([mixed_copy], own_mixed)
    gather = Gather(at, wires, attended_ref, att_all, local_sems.at[14])
    gather.own_column()

    near = pl.ds(aligned(at.h * half_rows, half_rows), half_rows)
    far = pl.ds(aligned((1 - at.h) * half_rows, half_rows), half_rows)
    tile = 256

    def multiply(chunk, all_ref, weight, total_ref, sent_ref):
        @pl.loop(0, weight.shape[1] // tile)
        def _(index):
            cols = pl.ds(aligned(index * tile, tile), tile)
            total_ref[chunk, :, cols] = jnp.dot(
                all_ref[chunk], weight[:, cols], preferred_element_type=jnp.float32
            )
        sent_ref[chunk] = total_ref[chunk, far, :].astype(sent_ref.dtype)

    arrived(*moving_out)
    crossing = []

    def project(chunk):
        multiply(chunk, att_all, out_w, out_total, out_sent)
        crossing.append(wires.send(out_sent.at[chunk], out_landed.at[chunk], at.away(h=1)))

    project(0)
    gather.forward(1)
    gather.forward(2)
    gather.landed(1)
    project(1)
    gather.landed(2)
    project(2)
    gather.forward(3)
    moving_up = quarters(up_w_ref, gate_up_w, gate_up_w.shape[1] // 2)
    gather.landed(3)
    project(3)
    moving_down = down_blocks()
    width = out_w.shape[1]

    def out_column(p, x, y, c):
        return pl.ds(aligned((y * 2 + c) * (4 * width) + (p * 2 + x) * width, width), width)

    own_cols = out_column(at.p, at.x, at.y, at.c)
    returning = []
    for chunk, (dx, dy) in enumerate(HOPS):
        crossing[chunk].wait_recv()
        done = out_total[chunk, near, :] + out_landed[chunk].astype(jnp.float32)
        out_done[chunk] = done.astype(out_done.dtype)
        for dp in range(2):
            for dc in range(2):
                start = aligned((flip(at.p, dp) * 2 + flip(at.c, dc)) * rows, rows)
                source = out_done.at[chunk, pl.ds(start, rows)]
                target = projected.at[:, own_cols]
                if dx + dy + dp + dc:
                    returning.append(
                        wires.send(source, target, at.away(p=dp, x=dx, y=dy, c=dc))
                    )
                else:
                    own_projected = keep(source, target)
    for copy in returning:
        copy.wait_recv()
    own_projected.wait()
    own_hidden.wait()
    residual = (hidden_ref[...].astype(jnp.float32) + projected[...].astype(jnp.float32)).astype(
        jnp.bfloat16
    )
    residual_ref[...] = residual
    wide = residual.astype(jnp.float32)
    mean_sq = jnp.mean(wide * wide, axis=-1, keepdims=True)
    normed_ref[...] = (
        wide * lax.rsqrt(mean_sq + EPS) * gain_ref[...].astype(jnp.float32)
    ).astype(jnp.bfloat16)

    gather = Gather(at, wires, normed_ref, norm_all, local_sems.at[15])
    gather.own_column()
    arrived(*moving_gate)
    arrived(*moving_up)
    units = gate_up_w.shape[1] // 2
    own_units = pl.ds(aligned(at.c * units, units), units)
    crossing, hidden_far, hidden_core = [], [], {}

    def expand(chunk):
        multiply(chunk, norm_all, gate_up_w, total, sums_sent)
        crossing.append(wires.send(sums_sent.at[chunk], sums_landed.at[chunk], at.away(h=1)))

    def activate(chunk):
        crossing[chunk].wait_recv()
        gate = total[chunk, near, :units] + sums_landed[chunk, :, :units].astype(jnp.float32)
        up = total[chunk, near, units:] + sums_landed[chunk, :, units:].astype(jnp.float32)
        hidden = gate / (1.0 + jnp.exp(-gate)) * up
        hidden_all[chunk, near, own_units] = hidden.astype(hidden_all.dtype)
        block = hidden_all.at[chunk, near, own_units]
        hidden_far.append(wires.send(block, block, at.away(h=1)))
        hidden_core[chunk] = [wires.send(block, block, at.away(c=1))]

    def relay(chunk):
        hidden_far[chunk].wait_recv()
        block = hidden_all.at[chunk, far, own_units]
        hidden_core[chunk].append(wires.send(block, block, at.away(c=1)))

    back = {}

    def contract(chunk):
        for copy in hidden_core[chunk]:
            copy.wait_recv()

        @pl.loop(0, down_w.shape[1] // tile)
        def _(index):
            cols = pl.ds(aligned(index * tile, tile), tile)
            partial[chunk, :, cols] = jnp.dot(
                hidden_all[chunk], down_w[:, cols], preferred_element_type=jnp.float32
            ).astype(partial.dtype)

        dx, dy = HOPS[chunk]
        if chunk:
            back[chunk] = wires.send(
                partial.at[chunk], partial_landed.at[chunk - 1], at.away(x=dx, y=dy)
            )

    expand(0)
    gather.forward(1)
    gather.forward(2)
    gather.landed(1)
    expand(1)
    activate(0)
    gather.landed(2)
    expand(2)
    gather.forward(3)
    activate(1)
    relay(0)
    gather.landed(3)
    expand(3)
    activate(2)
    relay(1)
    down_copies, down_own = moving_down
    for copy in down_copies[:-1]:
        copy.wait_recv()

    @pl.when(at.p != at.c)
    def _():
        down_copies[-1].wait_recv()

    @pl.when(at.p == at.c)
    def _():
        down_own.wait()

    contract(1)
    activate(3)
    relay(2)
    contract(2)
    relay(3)
    contract(3)
    contract(0)

    level_rows = 2 * rows
    for chunk in (1, 2, 3):
        back[chunk].wait_recv()

    def level_sum(level):
        span = pl.ds(aligned(level * level_rows, level_rows), level_rows)
        sums = partial[0, span, :].astype(jnp.float32)
        for chunk in range(3):
            sums = sums + partial_landed[chunk, span, :].astype(jnp.float32)
        return sums

    paired = []
    for half in range(2):
        pair_sent[half] = level_sum(half * 2 + 1 - at.p).astype(pair_sent.dtype)
        paired.append(wires.send(pair_sent.at[half], pair_landed.at[half], at.away(p=1)))
    out_width = last_sent.shape[2]
    final_cols = pl.ds(aligned((at.h * 2 + at.c) * out_width, out_width), out_width)
    for half in range(2):
        paired[half].wait_recv()
        last_sent[half] = (
            level_sum(half * 2 + at.p) + pair_landed[half].astype(jnp.float32)
        ).astype(last_sent.dtype)
    lasting = []
    for dh, dc in ((1, 0), (1, 1), (0, 1), (0, 0)):
        start = aligned(flip(at.c, dc) * rows, rows)
        source = last_sent.at[flip(at.h, dh), pl.ds(start, rows)]
        target = final.at[:, final_cols]
        if dh + dc:
            lasting.append(wires.send(source, target, at.away(h=dh, c=dc)))
        else:
            own_last = keep(source, target)
    for copy in lasting:
        copy.wait_recv()
    own_last.wait()
    o_ref[...] = (
        residual_ref[...].astype(jnp.float32) + final[...].astype(jnp.float32)
    ).astype(o_ref.dtype)

    for copy in wires.started:
        if copy is not down_copies[-1]:
            copy.wait_send()

    @pl.when(at.p != at.c)
    def _():
        down_copies[-1].wait_send()


SEMAPHORES = 192


def per_device_halves(
    hidden_in, queries, new_keys, new_values, key_cache, value_cache, cache_lengths, parent_ids,
    accepted_leaf, query_gain, key_gain, post_gain, out_weight, gate_weight, up_weight, down_weight,
):
    rows, model = hidden_in.shape
    kv_width = new_keys.shape[1]
    tree, positions = 2 * rows, 2 * key_cache.shape[0]
    column = 8 * rows
    groups = KV_HEADS // 2
    out_cols = out_weight.shape[1] // 4
    units = gate_weight.shape[1] // 4
    bf16, f32 = jnp.bfloat16, jnp.float32
    half = HEAD_DIM // 2
    frequency = ROPE_BASE ** (-2.0 * jnp.arange(half, dtype=f32) / HEAD_DIM)
    frequency = jnp.concatenate([frequency, frequency]).reshape(1, -1)
    vmem = pl.BlockSpec(memory_space=pltpu.VMEM)
    smem = pl.BlockSpec(memory_space=pltpu.SMEM)
    layer_out, accepted_kv = pl.pallas_call(
        layer_kernel,
        out_shape=[
            jax.ShapeDtypeStruct((rows, model), bf16),
            jax.ShapeDtypeStruct((rows, 2 * kv_width), bf16),
        ],
        in_specs=[smem, smem] + [vmem] * 5 + [ANY] * 10,
        out_specs=[vmem, vmem],
        scratch_shapes=[
            pltpu.VMEM((tree, model // 2), bf16),
            pltpu.VMEM((tree, kv_width), bf16),
            pltpu.VMEM((tree, kv_width), bf16),
            pltpu.VMEM((positions, kv_width // 2), bf16),
            pltpu.VMEM((positions, kv_width // 2), bf16),
            pltpu.VMEM((groups, tree * HEADS // KV_HEADS, HEAD_DIM), bf16),
            pltpu.VMEM((tree, kv_width), bf16),
            pltpu.VMEM((tree, model // 2), bf16),
            pltpu.VMEM((rows, model), bf16),
            pltpu.VMEM((rows, model), bf16),
            pltpu.VMEM((4, column, model // 2), bf16),
            pltpu.VMEM((4, column, model // 2), bf16),
            pltpu.VMEM((model // 2, out_cols), bf16),
            pltpu.VMEM((model // 2, 2 * units), bf16),
            pltpu.VMEM((2 * units, model // 4), bf16),
            pltpu.VMEM((4, column, out_cols), f32),
            pltpu.VMEM((4, column // 2, out_cols), bf16),
            pltpu.VMEM((4, column // 2, out_cols), bf16),
            pltpu.VMEM((4, column // 2, out_cols), bf16),
            pltpu.VMEM((rows, model), bf16),
            pltpu.VMEM((rows, model), bf16),
            pltpu.VMEM((rows, model), bf16),
            pltpu.VMEM((4, column, 2 * units), f32),
            pltpu.VMEM((4, column // 2, 2 * units), bf16),
            pltpu.VMEM((4, column // 2, 2 * units), bf16),
            pltpu.VMEM((4, column, 2 * units), bf16),
            pltpu.VMEM((4, column, model // 4), bf16),
            pltpu.VMEM((3, column, model // 4), bf16),
            pltpu.VMEM((2, 2 * rows, model // 4), bf16),
            pltpu.VMEM((2, 2 * rows, model // 4), bf16),
            pltpu.VMEM((2, 2 * rows, model // 4), bf16),
            pltpu.VMEM((rows, model), bf16),
            pltpu.SemaphoreType.DMA((SEMAPHORES,)),
            pltpu.SemaphoreType.DMA((SEMAPHORES,)),
            pltpu.SemaphoreType.DMA((16,)),
        ],
        compiler_params=pltpu.CompilerParams(
            collective_id=8, has_side_effects=True, vmem_limit_bytes=52 * 2**20
        ),
    )(
        cache_lengths, accepted_leaf, parent_ids, frequency, query_gain.reshape(1, -1),
        key_gain.reshape(1, -1), post_gain.reshape(1, -1), queries, new_keys, new_values,
        key_cache, value_cache, hidden_in, out_weight, gate_weight, up_weight, down_weight,
    )
    return layer_out, accepted_kv


def solution(mesh):
    in_specs = (
        P(("req", "tp"), None),
        P(("req", "tp"), None),
        P(("req", "tp"), None),
        P(("req", "tp"), None),
        P(("req", "tp"), None),
        P(("req", "tp"), None),
        P(),
        P(),
        P(),
        P(),
        P(),
        P(),
        P("req", "tp"),
        P("req", "tp"),
        P("req", "tp"),
        P("tp", "req"),
    )
    out_specs = (P(("req", "tp"), None), P(("req", "tp"), None))
    by_halves = mesh.shape["req"] == 4 * SIDE and mesh.shape["tp"] == 4
    return jax.shard_map(
        per_device_halves if by_halves else per_device, mesh=mesh, in_specs=in_specs, out_specs=out_specs, check_vma=False
    )
```

```python
import functools

import jax
import jax.numpy as jnp
import numpy as np
from jax import lax
from jax.experimental import pallas as pl
from jax.experimental.pallas import tpu as pltpu
from jax.sharding import PartitionSpec as P

HEADS = 32
KV_HEADS = 8
HEAD_DIM = 128


NEG = -1e30
EPS = 1e-06
ROPE_BASE = 1000000.0


def swapped(value, axis, bit):
    mask = 2**bit
    pairs = [(source, source ^ mask) for source in range(lax.axis_size(axis))]
    return lax.ppermute(value, axis, pairs)


def head_norm(values, gain_vec):
    mean_sq = jnp.mean(values * values, axis=-1, keepdims=True)
    return values * lax.rsqrt(mean_sq + EPS) * gain_vec.astype(jnp.float32)


def rotate(values, position):
    head_width = values.shape[-1]
    half_width = head_width // 2
    frequency = ROPE_BASE ** (-2.0 * jnp.arange(half_width, dtype=jnp.float32) / head_width)
    angles = position[:, None] * frequency[None, :]
    cosine = jnp.cos(angles)[:, None, :]
    sine_part = jnp.sin(angles)[:, None, :]
    front_half = values[..., :half_width]
    back_half = values[..., half_width:]
    return jnp.concatenate(
        [front_half * cosine - back_half * sine_part, back_half * cosine + front_half * sine_part],
        axis=-1,
    )


SIDE = 2
MESH = pl.DeviceIdType.MESH
ANY = pl.BlockSpec(memory_space=pl.ANY)


def meet(peers):
    barrier = pltpu.get_barrier_semaphore()
    for peer in peers:
        pl.semaphore_signal(barrier, inc=1, device_id=peer, device_id_type=MESH)
    pl.semaphore_wait(barrier, len(peers))


def remote(source, target, send_sem, recv_sem, peer):
    return pltpu.make_async_remote_copy(
        src_ref=source,
        dst_ref=target,
        send_sem=send_sem,
        recv_sem=recv_sem,
        device_id=peer,
        device_id_type=MESH,
    )


def line_of(along):
    tp_count = lax.axis_size("tp")
    req, tp = lax.axis_index("req"), lax.axis_index("tp")
    level, side = req // SIDE, req % SIDE
    if along == "level":
        return (
            lax.axis_size("req") // SIDE,
            level,
            lambda index: {"req": index * SIDE + side, "tp": tp},
        )
    return (
        SIDE * tp_count,
        side * tp_count + tp,
        lambda index: {"req": level * SIDE + index // tp_count, "tp": index % tp_count},
    )


def exchange_kernel(along, rows_ref, out_ref, send_sem, recv_sem, own_sem):
    count, mine, device = line_of(along)

    def part(index):
        return rows_ref.at[index]

    others = [(mine + step) % count for step in range(1, count)]
    meet([device(index) for index in others])
    copies = [
        remote(part(index), out_ref.at[mine], send_sem.at[at], recv_sem.at[at], device(index))
        for at, index in enumerate(others)
    ]
    for copy in copies:
        copy.start()
    own = pltpu.make_async_copy(part(mine), out_ref.at[mine], own_sem)
    own.start()
    for copy in copies:
        copy.wait()
    own.wait()


def exchange(rows, along, collective_id):
    count = lax.axis_size("req") // SIDE if along == "level" else SIDE * lax.axis_size("tp")
    part_shape = rows.shape[1:]
    return pl.pallas_call(
        functools.partial(exchange_kernel, along),
        out_shape=jax.ShapeDtypeStruct((count, *part_shape), rows.dtype),
        in_specs=[ANY],
        out_specs=ANY,
        scratch_shapes=[
            pltpu.SemaphoreType.DMA((count - 1,)),
            pltpu.SemaphoreType.DMA((count - 1,)),
            pltpu.SemaphoreType.DMA,
        ],
        compiler_params=pltpu.CompilerParams(collective_id=collective_id, has_side_effects=True),
    )(rows)


def reduce_kernel(
    along, mode, rows_ref, out_ref, landed, held,
    pair_send, pair_recv, far_send, far_recv, last_send, last_recv, own_sems,
):
    count, mine, device = line_of(along)
    half, place, parity = count // 2, mine // 2, mine % 2
    depth = landed.shape[1]
    piece = depth // 2

    def part(index, start, size):
        if mode == "inner":
            return rows_ref.at[pl.ds(start, size), index]
        return rows_ref.at[index, pl.ds(start, size)]

    order = [(place + step) % half for step in range(1, half)]
    pair = device(place * 2 + 1 - parity)
    far_devices = [device(index * 2 + parity) for index in order]
    meet(far_devices + [pair])
    inward, kept, outward = [], [], []
    for at, index in enumerate(order):
        for cut in range(2):
            copy = remote(
                part(index * 2 + 1 - parity, cut * piece, piece),
                landed.at[at, pl.ds(cut * piece, piece)],
                pair_send.at[at * 2 + cut],
                pair_recv.at[at * 2 + cut],
                pair,
            )
            copy.start()
            inward.append(copy)
        copy = pltpu.make_async_copy(
            part(index * 2 + parity, 0, depth), held.at[at], own_sems.at[at + 1]
        )
        copy.start()
        kept.append(copy)
    last = remote(
        part(place * 2 + 1 - parity, 0, depth), out_ref.at[1], last_send, last_recv, pair
    )
    last.start()
    own = pltpu.make_async_copy(part(mine, 0, depth), out_ref.at[0], own_sems.at[0])
    own.start()
    for at, peer in enumerate(far_devices):
        kept[at].wait()
        for cut in range(2):
            inward[at * 2 + cut].wait_recv()

            @pl.loop(cut * piece, (cut + 1) * piece)
            def _(row):
                total = held[at, row].astype(jnp.float32) + landed[at, row].astype(jnp.float32)
                held[at, row] = total.astype(held.dtype)

            copy = remote(
                held.at[at, pl.ds(cut * piece, piece)],
                out_ref.at[at + 2, pl.ds(cut * piece, piece)],
                far_send.at[at * 2 + cut],
                far_recv.at[at * 2 + cut],
                peer,
            )
            copy.start()
            outward.append(copy)
    own.wait()
    last.wait()
    for copy in inward:
        copy.wait_send()
    for copy in outward:
        copy.wait()


def reduced(rows, along, mode, collective_id):
    count = lax.axis_size("req") // SIDE if along == "level" else SIDE * lax.axis_size("tp")
    half = count // 2
    if mode == "inner":
        part_shape = rows.shape[:1] + rows.shape[2:]
    else:
        part_shape = rows.shape[1:]
    parts = pl.pallas_call(
        functools.partial(reduce_kernel, along, mode),
        out_shape=jax.ShapeDtypeStruct((half + 1, *part_shape), rows.dtype),
        in_specs=[ANY],
        out_specs=ANY,
        scratch_shapes=[
            pltpu.VMEM((half - 1, *part_shape), rows.dtype),
            pltpu.VMEM((half - 1, *part_shape), rows.dtype),
            pltpu.SemaphoreType.DMA((2 * (half - 1),)),
            pltpu.SemaphoreType.DMA((2 * (half - 1),)),
            pltpu.SemaphoreType.DMA((2 * (half - 1),)),
            pltpu.SemaphoreType.DMA((2 * (half - 1),)),
            pltpu.SemaphoreType.DMA,
            pltpu.SemaphoreType.DMA,
            pltpu.SemaphoreType.DMA((half,)),
        ],
        compiler_params=pltpu.CompilerParams(
            collective_id=collective_id, has_side_effects=True, vmem_limit_bytes=40 * 2**20
        ),
    )(rows)
    return jnp.sum(parts.astype(jnp.float32), axis=0)


def gather_kernel(rows_ref, out_ref, far_send, far_recv, near_send, near_recv, own_sem):
    count, mine, device = line_of("level")
    half, place, parity = count // 2, mine // 2, mine % 2
    pair = device(place * 2 + 1 - parity)
    order = [(place + step) % half for step in range(1, half)]
    far_devices = [device(index * 2 + parity) for index in order]
    meet(far_devices + [pair])
    far, near = [], []
    for cut in range(2):
        for peer in far_devices:
            at = len(far)
            copy = remote(
                rows_ref.at[cut], out_ref.at[mine, cut], far_send.at[at], far_recv.at[at], peer
            )
            copy.start()
            far.append(copy)
    own = pltpu.make_async_copy(rows_ref, out_ref.at[mine], own_sem)
    own.start()
    for cut in range(2):
        at = len(near)
        copy = remote(
            rows_ref.at[cut], out_ref.at[mine, cut], near_send.at[at], near_recv.at[at], pair
        )
        copy.start()
        near.append(copy)
    for cut in range(2):
        for step in range(1, half):
            far[cut * (half - 1) + step - 1].wait_recv()
            landed = out_ref.at[((place - step + half) % half) * 2 + parity, cut]
            at = len(near)
            copy = remote(landed, landed, near_send.at[at], near_recv.at[at], pair)
            copy.start()
            near.append(copy)
    own.wait()
    for copy in near:
        copy.wait()
    for copy in far:
        copy.wait_send()


def gathered_levels(rows, collective_id):
    count = lax.axis_size("req") // SIDE
    half = count // 2
    rows = rows.reshape(2, rows.shape[0] // 2, rows.shape[1])
    return pl.pallas_call(
        gather_kernel,
        out_shape=jax.ShapeDtypeStruct((count, *rows.shape), rows.dtype),
        in_specs=[ANY],
        out_specs=ANY,
        scratch_shapes=[
            pltpu.SemaphoreType.DMA((2 * (half - 1),)),
            pltpu.SemaphoreType.DMA((2 * (half - 1),)),
            pltpu.SemaphoreType.DMA((2 * half,)),
            pltpu.SemaphoreType.DMA((2 * half,)),
            pltpu.SemaphoreType.DMA,
        ],
        compiler_params=pltpu.CompilerParams(collective_id=collective_id, has_side_effects=True),
    )(rows)


def slices_kernel(
    rows_ref, out_ref, send_level, recv_level, send_far, recv_far, send_core, recv_core, own_sem
):
    tp_count = lax.axis_size("tp")
    levels = lax.axis_size("req") // SIDE
    req, tp = lax.axis_index("req"), lax.axis_index("tp")
    level, side = req // SIDE, req % SIDE
    place = side * tp_count + tp
    core, chip = tp % 2, place // 2
    chips = SIDE * tp_count // 2
    width = rows_ref.shape[1] // levels

    def columns(index):
        return rows_ref.at[:, pl.ds(pl.multiple_of(index * width, width), width)]

    def chip_place(index):
        return index * 2 + core

    def device(at):
        return {"req": level * SIDE + at // tp_count, "tp": at % tp_count}

    level_ids = [(level + step) % levels for step in range(1, levels)]
    level_devices = [{"req": index * SIDE + side, "tp": tp} for index in level_ids]
    far_devices = [device(chip_place((chip + step) % chips)) for step in range(1, chips)]
    core_device = device(chip * 2 + 1 - core)
    meet(level_devices + far_devices + [core_device])
    first = [
        remote(columns(index), out_ref.at[level, place], send_level.at[at], recv_level.at[at], peer)
        for at, (index, peer) in enumerate(zip(level_ids, level_devices))
    ]
    for copy in first:
        copy.start()
    own = pltpu.make_async_copy(columns(level), out_ref.at[level, place], own_sem)
    own.start()
    far, near = [], []
    for step in range(levels):
        source_level = (level - step + levels) % levels
        target = out_ref.at[source_level, place]
        if step > 0:
            first[step - 1].wait_recv()
        source = columns(level) if step == 0 else target
        for peer in far_devices:
            at = len(far)
            copy = remote(source, target, send_far.at[at], recv_far.at[at], peer)
            copy.start()
            far.append(copy)
        at = len(near)
        copy = remote(source, target, send_core.at[at], recv_core.at[at], core_device)
        copy.start()
        near.append(copy)
    for step in range(levels):
        source_level = (level - step + levels) % levels
        for hop in range(1, chips):
            far[step * (chips - 1) + hop - 1].wait_recv()
            landed = out_ref.at[source_level, chip_place((chip - hop + chips) % chips)]
            at = len(near)
            copy = remote(landed, landed, send_core.at[at], recv_core.at[at], core_device)
            copy.start()
            near.append(copy)
    own.wait()
    for copy in near:
        copy.wait()
    for copy in first + far:
        copy.wait_send()


def feature_slices(rows, collective_id):
    levels = lax.axis_size("req") // SIDE
    places = SIDE * lax.axis_size("tp")
    width = rows.shape[1] // levels
    chips = places // 2
    gathered = pl.pallas_call(
        slices_kernel,
        out_shape=jax.ShapeDtypeStruct((levels, places, rows.shape[0], width), rows.dtype),
        in_specs=[ANY],
        out_specs=ANY,
        scratch_shapes=[
            pltpu.SemaphoreType.DMA((levels - 1,)),
            pltpu.SemaphoreType.DMA((levels - 1,)),
            pltpu.SemaphoreType.DMA((levels * (chips - 1),)),
            pltpu.SemaphoreType.DMA((levels * (chips - 1),)),
            pltpu.SemaphoreType.DMA((levels * chips,)),
            pltpu.SemaphoreType.DMA((levels * chips,)),
            pltpu.SemaphoreType.DMA,
        ],
        compiler_params=pltpu.CompilerParams(collective_id=collective_id, has_side_effects=True),
    )(rows)
    return gathered.reshape(-1, width)


def paired_halves(shard, axis):
    side = lax.axis_index("req") % SIDE
    half = shard.shape[axis] // 2
    kept = lax.dynamic_slice_in_dim(shard, side * half, half, axis)
    sent = lax.dynamic_slice_in_dim(shard, (1 - side) * half, half, axis)
    return kept, sent


def joined(kept, received, axis):
    side = lax.axis_index("req") % SIDE
    low = jnp.where(side == 0, kept, received)
    high = jnp.where(side == 0, received, kept)
    return jnp.concatenate([low, high], axis=axis)


def attention_kernel(
    limit_ref, query_ref, key_ref, value_ref, fresh_key_ref, fresh_value_ref, allowed_ref,
    top_ref, total_ref, sum_ref,
):
    group_size = query_ref.shape[1] // HEAD_DIM
    query = jnp.concatenate(
        [query_ref[:, at * HEAD_DIM : (at + 1) * HEAD_DIM] for at in range(group_size)], axis=0
    )
    score_scale = HEAD_DIM ** (-0.5)
    limit = limit_ref[0]
    chunk = key_ref.shape[0] // 4

    def score(keys):
        return (
            lax.dot_general(
                query, keys, (((1,), (1,)), ((), ())), preferred_element_type=jnp.float32
            )
            * score_scale
        )

    def weigh(scores, top, allowed):
        weights = jnp.where(allowed, jnp.exp(scores - top), 0.0).astype(jnp.bfloat16)
        return weights, jnp.sum(weights.astype(jnp.float32), axis=-1, keepdims=True)

    allowed = jnp.concatenate([allowed_ref[...]] * group_size, axis=0) > 0.5
    scores = jnp.where(allowed, score(fresh_key_ref[...]), NEG)
    top = jnp.max(scores, axis=-1, keepdims=True)
    weights, total = weigh(scores, top, allowed)
    summed = jnp.dot(weights, fresh_value_ref[...], preferred_element_type=jnp.float32)

    def step(index, running):
        top, total, summed = running
        start = pl.multiple_of(index * chunk, chunk)
        keys = key_ref[pl.ds(start, chunk), :]
        values = value_ref[pl.ds(start, chunk), :]
        allowed = lax.broadcasted_iota(jnp.int32, (query.shape[0], chunk), 1) + start < limit
        scores = jnp.where(allowed, score(keys), NEG)
        new_top = jnp.maximum(top, jnp.max(scores, axis=-1, keepdims=True))
        weights, chunk_total = weigh(scores, new_top, allowed)
        shrink = jnp.exp(top - new_top)
        summed = summed * shrink + jnp.dot(weights, values, preferred_element_type=jnp.float32)
        return new_top, total * shrink + chunk_total, summed

    live = jnp.clip((limit + chunk - 1) // chunk, 0, 4)
    top, total, summed = lax.fori_loop(0, live, step, (top, total, summed))
    top_ref[0] = top
    total_ref[0] = total
    sum_ref[0] = summed


def attend(limit, query, keys, values, fresh_keys, fresh_values, allowed):
    rows, fresh_rows, cached_rows = query.shape[0], fresh_keys.shape[0], keys.shape[0]
    group_size = HEADS // KV_HEADS
    group_rows = rows * group_size

    def columns(block_rows, width):
        return pl.BlockSpec((block_rows, width), lambda head, limit_ref: (0, head))

    def lead(width):
        return pl.BlockSpec((1, group_rows, width), lambda head, limit_ref: (head, 0, 0))

    results = pl.pallas_call(
        attention_kernel,
        out_shape=[
            jax.ShapeDtypeStruct((KV_HEADS, group_rows, width), jnp.float32)
            for width in (1, 1, HEAD_DIM)
        ],
        grid_spec=pltpu.PrefetchScalarGridSpec(
            num_scalar_prefetch=1,
            grid=(KV_HEADS,),
            in_specs=[
                columns(rows, group_size * HEAD_DIM),
                columns(cached_rows, HEAD_DIM),
                columns(cached_rows, HEAD_DIM),
                columns(fresh_rows, HEAD_DIM),
                columns(fresh_rows, HEAD_DIM),
                pl.BlockSpec((rows, fresh_rows), lambda head, limit_ref: (0, 0)),
            ],
            out_specs=[lead(1), lead(1), lead(HEAD_DIM)],
        ),
        compiler_params=pltpu.CompilerParams(vmem_limit_bytes=32 * 2**20),
        cost_estimate=pl.CostEstimate(
            flops=4 * group_rows * cached_rows * KV_HEADS * HEAD_DIM,
            bytes_accessed=4 * cached_rows * KV_HEADS * HEAD_DIM,
            transcendentals=group_rows * cached_rows * KV_HEADS,
        ),
    )(limit, query, keys, values, fresh_keys, fresh_values, allowed)
    return [
        result.reshape(KV_HEADS, group_size, rows, result.shape[2]) for result in results
    ]


def ancestors(parent_row):
    node_count = parent_row.shape[0]
    node_ids = jnp.arange(node_count, dtype=jnp.int32)
    identity_mat = (node_ids[:, None] == node_ids[None, :]).astype(jnp.float32)
    parent_mat = (parent_row[:, None] == node_ids[None, :]).astype(jnp.float32) * (
        1.0 - identity_mat
    )
    reached = jnp.minimum(identity_mat + parent_mat, 1.0)
    for sweep in range(node_count.bit_length()):
        reached = jnp.minimum(jnp.dot(reached, reached, precision=lax.Precision.HIGHEST), 1.0)
    return reached


def per_device(
    hidden_in,
    queries,
    new_keys,
    new_values,
    key_cache,
    value_cache,
    cache_lengths,
    parent_ids,
    accepted_leaf,
    query_gain,
    key_gain,
    post_gain,
    out_weight,
    gate_weight,
    up_weight,
    down_weight,
):
    half_rows = queries.shape[0]
    out_kept, out_sent = paired_halves(out_weight, 1)
    out_received = swapped(out_sent, "req", 0)
    gate_kept, gate_sent = paired_halves(gate_weight, 1)
    up_kept, up_sent = paired_halves(up_weight, 1)
    gate_up_received = swapped(jnp.concatenate([gate_sent, up_sent], axis=1), "req", 0)
    gate_up_kept = jnp.concatenate([gate_kept, up_kept], axis=1)
    down_kept, down_sent = paired_halves(down_weight, 0)
    out_full = joined(out_kept, out_received, 0)
    gate_up_full = joined(gate_up_kept, gate_up_received, 0)
    tree_size = 2 * half_rows
    kv_width = new_keys.shape[1]
    q_width = queries.shape[1]
    tp_count = lax.axis_size("tp")
    device = lax.axis_index(("req", "tp"))
    request = device // 2
    pair_side = lax.axis_index("tp") % 2
    cache_length = lax.dynamic_index_in_dim(cache_lengths, request, 0, keepdims=False)
    parent_row = lax.dynamic_index_in_dim(parent_ids, request, 0, keepdims=False)
    leaf_index = lax.dynamic_index_in_dim(accepted_leaf, request, 0, keepdims=False)
    reached = ancestors(parent_row)
    node_depth = jnp.sum(reached, axis=1) - 1.0
    node_ids = jnp.arange(tree_size, dtype=jnp.int32)
    local_ids = jnp.arange(half_rows, dtype=jnp.int32)
    node_order = jnp.concatenate(
        [pair_side * half_rows + local_ids, (1 - pair_side) * half_rows + local_ids]
    )
    reorder = (node_order[:, None] == node_ids[None, :]).astype(jnp.float32)
    reached_rows = jnp.dot(reorder, reached, precision=lax.Precision.HIGHEST)
    own_cols = jnp.dot(reached_rows, reorder[:half_rows].T, precision=lax.Precision.HIGHEST) > 0.5
    own_depth = jnp.dot(reorder[:half_rows], node_depth, precision=lax.Precision.HIGHEST)
    position = cache_length.astype(jnp.float32) + own_depth
    query_heads = rotate(
        head_norm(queries.astype(jnp.float32).reshape(half_rows, HEADS, HEAD_DIM), query_gain),
        position,
    ).astype(jnp.bfloat16)
    key_heads = rotate(
        head_norm(new_keys.astype(jnp.float32).reshape(half_rows, KV_HEADS, HEAD_DIM), key_gain),
        position,
    ).astype(jnp.bfloat16)
    query_own = query_heads.reshape(half_rows, q_width)
    fresh_own = jnp.concatenate([key_heads.reshape(half_rows, kv_width), new_values], axis=1)
    query_other, fresh_other = swapped((query_own, fresh_own), "tp", 0)
    query_all = jnp.concatenate([query_own, query_other], axis=0)
    limit = (cache_length - pair_side * key_cache.shape[0]).reshape(1)
    run_top, run_total, summed = attend(
        limit,
        query_all,
        key_cache,
        value_cache,
        key_heads.reshape(half_rows, kv_width),
        new_values,
        own_cols.astype(jnp.float32),
    )
    far_top, far_total, far_sum = (
        swapped(run_top[:, :, half_rows:].astype(jnp.bfloat16), "tp", 0).astype(jnp.float32),
        swapped(run_total[:, :, half_rows:].astype(jnp.bfloat16), "tp", 0).astype(jnp.float32),
        swapped(summed[:, :, half_rows:].astype(jnp.bfloat16), "tp", 0).astype(jnp.float32),
    )
    near_top = run_top[:, :, :half_rows]
    joint_top = jnp.maximum(near_top, far_top)
    near_scale = jnp.exp(near_top - joint_top)
    far_scale = jnp.exp(far_top - joint_top)
    denominator = run_total[:, :, :half_rows] * near_scale + far_total * far_scale
    merged = (summed[:, :, :half_rows] * near_scale + far_sum * far_scale) / denominator
    attended = jnp.transpose(merged, (2, 0, 1, 3)).reshape(half_rows, q_width).astype(jnp.bfloat16)
    leaf_pick = (node_ids == leaf_index).astype(jnp.float32)
    leaf_row = jnp.dot(leaf_pick, reached, precision=lax.Precision.HIGHEST)
    out_depths = (pair_side * half_rows + local_ids).astype(jnp.float32)
    chosen = leaf_row[None, :] * (node_depth[None, :] == out_depths[:, None]).astype(jnp.float32)
    chosen = jnp.dot(chosen, reorder.T, precision=lax.Precision.HIGHEST)
    fresh_all = jnp.concatenate([fresh_own, fresh_other], axis=0)
    accepted_kv = jnp.dot(
        chosen.astype(jnp.bfloat16), fresh_all, preferred_element_type=jnp.float32
    ).astype(jnp.bfloat16)
    levels = lax.axis_size("req") // SIDE
    places = SIDE * tp_count
    attn_slice = feature_slices(attended, 0)
    attn_slice, down_sent = lax.optimization_barrier((attn_slice, down_sent))
    down_full = joined(down_kept, swapped(down_sent, "req", 0), 1)
    projected = jnp.dot(attn_slice, out_full, preferred_element_type=jnp.float32)
    projected = projected.astype(jnp.bfloat16).reshape(levels, places, half_rows, -1)
    projected = reduced(projected, "level", "lead", 1).astype(jnp.bfloat16)
    projected = exchange(projected.reshape(places, half_rows, -1), "place", 2)
    own_projected = jnp.transpose(
        projected.reshape(SIDE, tp_count, half_rows, -1), (2, 1, 0, 3)
    ).reshape(half_rows, -1)
    residual = (hidden_in.astype(jnp.float32) + own_projected.astype(jnp.float32)).astype(
        jnp.bfloat16
    )
    residual_wide = residual.astype(jnp.float32)
    mean_sq = jnp.mean(residual_wide * residual_wide, axis=-1, keepdims=True)
    normed = (residual_wide * lax.rsqrt(mean_sq + EPS) * post_gain.astype(jnp.float32)).astype(
        jnp.bfloat16
    )
    normed_slice = feature_slices(normed, 3)
    sums = jnp.dot(normed_slice, gate_up_full, preferred_element_type=jnp.float32)
    sums = sums.astype(jnp.bfloat16).reshape(levels, places, half_rows, -1)
    sums = reduced(sums, "level", "lead", 4).reshape(places * half_rows, -1)
    hidden_width = sums.shape[1] // 2
    hidden = (jax.nn.silu(sums[:, :hidden_width]) * sums[:, hidden_width:]).astype(jnp.bfloat16)
    hidden_all = gathered_levels(hidden, 5).reshape(-1, hidden_width)
    partial_out = jnp.dot(hidden_all, down_full, preferred_element_type=jnp.float32)
    partial_out = partial_out.astype(jnp.bfloat16).reshape(levels, places, half_rows, -1)
    paired_sum = reduced(partial_out, "place", "inner", 6).astype(jnp.bfloat16)
    mlp_own = exchange(paired_sum, "level", 7)
    mlp_own = jnp.transpose(mlp_own, (1, 0, 2)).reshape(half_rows, -1).astype(jnp.float32)
    layer_out = (residual_wide + mlp_own).astype(jnp.bfloat16)
    return (layer_out, accepted_kv)


def flip(value, bit):
    return 1 - value if bit else value


class Place:
    def __init__(self):
        req, tp = lax.axis_index("req"), lax.axis_index("tp")
        level = req // SIDE
        self.h, self.p = level // 2, level % 2
        self.x, self.y, self.c = req % SIDE, tp // 2, tp % 2

    def away(self, h=0, p=0, x=0, y=0, c=0):
        return self.at(flip(self.h, h), flip(self.p, p), flip(self.x, x), flip(self.y, y), flip(self.c, c))

    def at(self, h, p, x, y, c):
        return {"req": (h * 2 + p) * SIDE + x, "tp": y * 2 + c}


class Wires:
    def __init__(self, send_sems, recv_sems):
        self.send_sems, self.recv_sems = send_sems, recv_sems
        self.started = []

    def make(self, source, target, peer):
        at = len(self.started)
        copy = remote(source, target, self.send_sems.at[at], self.recv_sems.at[at], peer)
        self.started.append(copy)
        return copy

    def send(self, source, target, peer):
        copy = self.make(source, target, peer)
        copy.start()
        return copy


def aligned(value, by):
    return pl.multiple_of(value, by)


HOPS = ((0, 0), (1, 0), (0, 1), (1, 1))


SEMAPHORES = 192
TILE = 256


class Gather:
    def __init__(self, place, wires, own_ref, all_ref, local_sem):
        self.place, self.wires, self.all_ref = place, wires, all_ref
        self.rows, self.width = own_ref.shape[0], all_ref.shape[2]
        at, width = place, self.width
        kept = own_ref.at[:, pl.ds(aligned(at.h * width, width), width)]
        given = own_ref.at[:, pl.ds(aligned((1 - at.h) * width, width), width)]
        self.far = wires.send(given, self.block(0, 0, 0), at.away(h=1))
        mine = self.block(0, 0, 0)
        self.local = pltpu.make_async_copy(kept, mine, local_sem)
        self.local.start()
        self.pair = [wires.send(kept, mine, at.away(p=1))]
        self.inward = {1: [], 2: [], 3: [None] * 4}
        self.core = {0: [], 1: [], 2: [], 3: []}
        self.spread(kept, 0, 0)

    def block(self, chunk, dh, dp):
        at = self.place
        level = flip(at.h, dh) * 2 + flip(at.p, dp)
        start = aligned((level * 2 + at.c) * self.rows, self.rows)
        return self.all_ref.at[chunk, pl.ds(start, self.rows)]

    def spread(self, source, dh, dp):
        at, wires = self.place, self.wires
        self.core[0].append(wires.send(source, self.block(0, dh, dp), at.away(c=1)))
        self.inward[1].append(wires.send(source, self.block(1, dh, dp), at.away(x=1)))
        self.inward[2].append(wires.send(source, self.block(2, dh, dp), at.away(y=1)))

    def own_column(self):
        self.forward(1, 0)
        self.forward(2, 0)
        far = self.block(0, 1, 0)
        self.far.wait_recv()
        self.pair.append(self.wires.send(far, far, self.place.away(p=1)))
        self.spread(far, 1, 0)
        self.pair[0].wait_recv()
        self.spread(self.block(0, 0, 1), 0, 1)
        self.pair[1].wait_recv()
        self.spread(self.block(0, 1, 1), 1, 1)
        self.local.wait()
        for copy in self.core[0]:
            copy.wait_recv()

    def forward(self, chunk, index):
        at, wires = self.place, self.wires
        dh, dp = ((0, 0), (1, 0), (0, 1), (1, 1))[index]
        self.inward[chunk][index].wait_recv()
        block = self.block(chunk, dh, dp)
        self.core[chunk].append(wires.send(block, block, at.away(c=1)))
        if chunk == 1 and index % 2 == 0:
            self.inward[3][index] = wires.send(block, self.block(3, dh, dp), at.away(y=1))
        if chunk == 2 and index % 2 == 1:
            self.inward[3][index] = wires.send(block, self.block(3, dh, dp), at.away(x=1))

    def neighbours(self):
        for index in range(1, 4):
            self.forward(1, index)
            self.forward(2, index)

    def diagonal(self):
        for index in range(4):
            self.forward(3, index)

    def landed(self, chunk):
        for copy in self.core[chunk]:
            copy.wait_recv()


def normalized(values, gain):
    mean_sq = jnp.mean(values * values, axis=-1, keepdims=True)
    return values * lax.rsqrt(mean_sq + EPS) * gain


def closure(parent_row):
    count = parent_row.shape[1]
    down = lax.broadcasted_iota(jnp.int32, (count, count), 0)
    across = lax.broadcasted_iota(jnp.int32, (count, count), 1)
    same = down == across
    identity = jnp.where(same, 1.0, 0.0).astype(jnp.bfloat16)
    turned = jnp.where(same | (parent_row == down), 1.0, 0.0)
    for sweep in range((count - 1).bit_length()):
        factor = turned.astype(jnp.bfloat16)
        turned = jnp.minimum(jnp.dot(factor, factor, preferred_element_type=jnp.float32), 1.0)
    reached = lax.dot_general(
        identity, turned.astype(jnp.bfloat16), (((1,), (1,)), ((), ())),
        preferred_element_type=jnp.float32,
    )
    return reached, turned


def attention_phase(
    at, length, leaf, parent_row, frequency, query_gain, key_gain,
    query_rows, key_rows, value_rows, arrived_rows, arrived_group, cache_k, cache_v,
    query_heads, key_heads, mixed, accepted_ref,
):
    bf16, f32 = jnp.bfloat16, jnp.float32
    tree = key_rows.shape[0]
    rows = tree // 2
    groups = query_heads.shape[0]
    group_size = HEADS // KV_HEADS
    reached, turned = closure(parent_row)
    depth = jnp.sum(reached, axis=1, keepdims=True) - 1.0
    depth_across = jnp.sum(turned, axis=0, keepdims=True) - 1.0
    angles = (length + depth) * frequency
    lane = lax.broadcasted_iota(jnp.int32, angles.shape, 1)
    cosine = jnp.cos(angles)
    sine = jnp.where(lane < HEAD_DIM // 2, -1.0, 1.0) * jnp.sin(angles)

    def rotated(values, gain):
        normed = normalized(values.astype(f32), gain)
        return (normed * cosine + pltpu.roll(normed, HEAD_DIM // 2, 1) * sine).astype(bf16)

    def lanes(head):
        return pl.ds(aligned(head * HEAD_DIM, HEAD_DIM), HEAD_DIM)

    arrived_rows()
    for group in range(groups):
        for member in range(group_size):
            head = group * group_size + member
            query_heads[group, pl.ds(member * tree, tree), :] = rotated(
                query_rows[:, head * HEAD_DIM : (head + 1) * HEAD_DIM], query_gain
            )
    for head in range(KV_HEADS):
        span = slice(head * HEAD_DIM, (head + 1) * HEAD_DIM)
        key_heads[:, span] = rotated(key_rows[:, span], key_gain)

    node = lax.broadcasted_iota(jnp.int32, (tree, tree), 0).astype(f32)
    leaf_row = jnp.sum(jnp.where(node == leaf, reached, 0.0), axis=0, keepdims=True)
    place = (at.c * rows + lax.broadcasted_iota(jnp.int32, (rows, tree), 0)).astype(f32)
    chosen = jnp.where(depth_across == place, leaf_row, 0.0).astype(bf16)
    kv_width = key_heads.shape[1]
    accepted_ref[:, :kv_width] = jnp.dot(
        chosen, key_heads[...], preferred_element_type=f32
    ).astype(bf16)
    accepted_ref[:, kv_width:] = jnp.dot(
        chosen, value_rows[...], preferred_element_type=f32
    ).astype(bf16)

    scale = HEAD_DIM**-0.5 * 1.4426950408889634
    tree_bias = jnp.where(reached > 0.5, 0.0, NEG)
    tree_bias = jnp.concatenate([tree_bias] * group_size, axis=0)
    chunk = cache_k.shape[0] // 4
    position = lax.broadcasted_iota(jnp.int32, (1, chunk), 1).astype(f32)
    biases = [
        jnp.where(position + index * chunk < length, 0.0, NEG) for index in range(4)
    ]

    def score(query, keys, bias):
        scores = lax.dot_general(
            query, keys, (((1,), (1,)), ((), ())), preferred_element_type=f32
        )
        return scores * scale + bias

    def weighed(scores, top, values):
        weights = jnp.exp2(scores - top).astype(bf16)
        ones = jnp.ones(values.shape, bf16)
        return jnp.dot(
            weights, jnp.concatenate([values, ones], axis=1), preferred_element_type=f32
        )

    for group in range(groups):
        arrived_group(group)
        query = query_heads[group]
        own = lanes(at.c * groups + group)
        scores = score(query, key_heads[:, own], tree_bias)
        top = jnp.max(scores, axis=-1, keepdims=True)
        summed = weighed(scores, top, value_rows[:, own])
        for index in range(4):
            span = pl.ds(index * chunk, chunk)
            scores = score(query, cache_k[span, lanes(group)], biases[index])
            new_top = jnp.maximum(top, jnp.max(scores, axis=-1, keepdims=True))
            summed = summed * jnp.exp2(top - new_top) + weighed(
                scores, new_top, cache_v[span, lanes(group)]
            )
            top = new_top
        result = (summed[:, :HEAD_DIM] / summed[:, HEAD_DIM:]).astype(bf16)
        for member in range(group_size):
            mixed[:, lanes(group * group_size + member)] = result[
                member * tree : (member + 1) * tree
            ]


def layer_kernel(
    lengths_ref, leaf_ref, parent_ref, frequency_ref, query_gain_ref, key_gain_ref, gain_ref,
    queries_ref, new_keys_ref, new_values_ref, key_cache_ref, value_cache_ref, hidden_in_ref,
    out_w_ref, gate_w_ref, up_w_ref, down_w_ref,
    o_ref, accepted_ref,
    lengths, leaves, parents, frequency, query_gain, key_gain, gain,
    query_rows, key_rows, value_rows, cache_k, cache_v, query_heads, key_heads, mixed, attended_ref,
    hidden_ref,
    att_all, norm_all, out_w, gate_up_w, down_w,
    out_total, out_sent, out_landed, out_done, projected, residual_ref, normed_ref,
    total, sums_sent, sums_landed, hidden_all,
    partial, partial_landed, pair_sent, pair_landed, last_sent, final,
    send_sems, recv_sems, local_sems,
):
    at = Place()
    wires = Wires(send_sems, recv_sems)
    rows = queries_ref.shape[0]
    column = 4 * 2 * rows
    half_rows = column // 2
    local = []

    def keep(source, target):
        copy = pltpu.make_async_copy(source, target, local_sems.at[len(local)])
        local.append(copy)
        copy.start()
        return copy

    small = [
        keep(lengths_ref, lengths), keep(leaf_ref, leaves), keep(parent_ref, parents),
        keep(frequency_ref, frequency), keep(query_gain_ref, query_gain),
        keep(key_gain_ref, key_gain), keep(gain_ref, gain),
    ]
    barrier = pltpu.get_barrier_semaphore()
    peers = [
        at.away(p=dp, x=dx, y=dy, c=dc)
        for dp in range(2) for dx in range(2) for dy in range(2) for dc in range(2)
        if dp + dx + dy + dc
    ] + [at.away(h=1), at.away(h=1, c=1)]
    for peer in peers:
        pl.semaphore_signal(barrier, inc=1, device_id=peer, device_id_type=MESH)
    pl.semaphore_wait(barrier, len(peers))

    def row_block(ref, start_col, cols):
        depth = ref.shape[0] // 4
        start = aligned((at.p * 2 + at.x) * depth, depth)
        return ref.at[pl.ds(start, depth), pl.ds(start_col, cols)]

    def quarters(source_ref, target_ref, start_col):
        width = source_ref.shape[1] // 4
        copies = []
        for dp, dx in ((0, 1), (1, 0), (1, 1)):
            quarter = flip(at.p, dp) * 2 + flip(at.x, dx)
            source = source_ref.at[:, pl.ds(aligned(quarter * width, width), width)]
            copies.append(
                wires.send(source, row_block(target_ref, start_col, width), at.away(p=dp, x=dx))
            )
        quarter = at.p * 2 + at.x
        source = source_ref.at[:, pl.ds(aligned(quarter * width, width), width)]
        own = keep(source, row_block(target_ref, start_col, width))
        return copies, own

    def down_blocks():
        depth, width = down_w.shape[0] // 2, down_w_ref.shape[1]
        target = down_w.at[
            pl.ds(aligned(at.c * depth, depth), depth), pl.ds(aligned(at.x * width, width), width)
        ]
        copies = []
        for da, db in ((0, 1), (1, 0), (1, 1), (0, 0)):
            pt, xt, ct = flip(at.c, db), flip(at.x, da), at.p
            start = aligned((pt * 2 + xt) * depth, depth)
            source = down_w_ref.at[pl.ds(start, depth)]
            copies.append(wires.make(source, target, at.at(at.h, pt, xt, at.y, ct)))
            if da + db:
                copies[-1].start()
        own = pltpu.make_async_copy(
            down_w_ref.at[pl.ds(aligned((at.p * 2 + at.x) * depth, depth), depth)],
            target,
            local_sems.at[61],
        )

        @pl.when(at.p != at.c)
        def _():
            copies[-1].start()

        @pl.when(at.p == at.c)
        def _():
            own.start()

        return copies, own

    def arrived(copies, own):
        for copy in copies:
            copy.wait_recv()
        own.wait()

    def shared(source_ref, target_ref, split=True, part=0, parts=1):
        depth, width = source_ref.shape[0], target_ref.shape[1] // parts
        rows_here = pl.ds(aligned(at.c * depth, depth), depth)
        target = target_ref.at[rows_here, pl.ds(part * width, width)]
        own = given = source_ref
        if split:
            own = source_ref.at[:, pl.ds(aligned((at.c * parts + part) * width, width), width)]
            start = aligned(((1 - at.c) * parts + part) * width, width)
            given = source_ref.at[:, pl.ds(start, width)]
        return [wires.send(given, target, at.away(c=1))], keep(own, target)

    moving_rows = [
        shared(queries_ref, query_rows),
        shared(new_keys_ref, key_rows, split=False),
        shared(new_values_ref, value_rows, split=False),
    ]
    moving_cache = []
    for group in range(query_heads.shape[0]):
        moving_cache.append(
            [
                shared(key_cache_ref, cache_k, part=group, parts=query_heads.shape[0]),
                shared(value_cache_ref, cache_v, part=group, parts=query_heads.shape[0]),
            ]
        )
    moving_out = quarters(out_w_ref, out_w, 0)
    moving_gate = quarters(gate_w_ref, gate_up_w, 0)
    own_hidden = keep(hidden_in_ref, hidden_ref)
    for copy in small:
        copy.wait()
    request = ((at.h * 2 + at.p) * SIDE + at.x) * 2 + at.y

    def of_request(ref):
        spot = lax.broadcasted_iota(jnp.int32, ref.shape, 1)
        picked = jnp.where(spot == request, ref[...].astype(jnp.float32), 0.0)
        return jnp.sum(picked, axis=1, keepdims=True)

    def arrived_rows():
        for moving in moving_rows:
            arrived(*moving)

    def arrived_group(group):
        for moving in moving_cache[group]:
            arrived(*moving)

    attention_phase(
        at, of_request(lengths), of_request(leaves), parents[pl.ds(request, 1), :],
        frequency[...], query_gain[...].astype(jnp.float32), key_gain[...].astype(jnp.float32),
        query_rows, key_rows, value_rows, arrived_rows, arrived_group,
        cache_k, cache_v, query_heads, key_heads, mixed, accepted_ref,
    )
    mixed_width = mixed.shape[1]
    mixed_target = attended_ref.at[:, pl.ds(aligned(at.c * mixed_width, mixed_width), mixed_width)]
    mixed_copy = wires.send(
        mixed.at[pl.ds(aligned((1 - at.c) * rows, rows), rows)], mixed_target, at.away(c=1)
    )
    own_mixed = keep(mixed.at[pl.ds(aligned(at.c * rows, rows), rows)], mixed_target)
    arrived([mixed_copy], own_mixed)
    gather = Gather(at, wires, attended_ref, att_all, local_sems.at[62])
    gather.own_column()

    near = pl.ds(aligned(at.h * half_rows, half_rows), half_rows)
    far = pl.ds(aligned((1 - at.h) * half_rows, half_rows), half_rows)
    tile = TILE

    def multiply(chunk, all_ref, weight, total_ref, sent_ref):
        @pl.loop(0, weight.shape[1] // tile)
        def _(index):
            cols = pl.ds(aligned(index * tile, tile), tile)
            total_ref[chunk, :, cols] = jnp.dot(
                all_ref[chunk], weight[:, cols], preferred_element_type=jnp.float32
            )
        sent_ref[chunk] = total_ref[chunk, far, :].astype(sent_ref.dtype)

    arrived(*moving_out)
    crossing = []

    def project(chunk):
        multiply(chunk, att_all, out_w, out_total, out_sent)
        crossing.append(wires.send(out_sent.at[chunk], out_landed.at[chunk], at.away(h=1)))

    width = out_w.shape[1]

    def out_column(p, x, y, c):
        return pl.ds(aligned((y * 2 + c) * (4 * width) + (p * 2 + x) * width, width), width)

    own_cols = out_column(at.p, at.x, at.y, at.c)
    returning, own_projected = [], []

    def give_back(chunk):
        dx, dy = HOPS[chunk]
        crossing[chunk].wait_recv()
        done = out_total[chunk, near, :] + out_landed[chunk].astype(jnp.float32)
        out_done[chunk] = done.astype(out_done.dtype)
        for dp in range(2):
            for dc in range(2):
                start = aligned((flip(at.p, dp) * 2 + flip(at.c, dc)) * rows, rows)
                source = out_done.at[chunk, pl.ds(start, rows)]
                target = projected.at[:, own_cols]
                if dx + dy + dp + dc:
                    returning.append(
                        wires.send(source, target, at.away(p=dp, x=dx, y=dy, c=dc))
                    )
                else:
                    own_projected.append(keep(source, target))

    project(0)
    gather.neighbours()
    gather.landed(1)
    project(1)
    give_back(0)
    gather.landed(2)
    project(2)
    gather.diagonal()
    moving_up = quarters(up_w_ref, gate_up_w, gate_up_w.shape[1] // 2)
    give_back(1)
    gather.landed(3)
    project(3)
    give_back(2)
    give_back(3)
    for copy in returning:
        copy.wait_recv()
    own_projected[0].wait()
    own_hidden.wait()
    residual = (hidden_ref[...].astype(jnp.float32) + projected[...].astype(jnp.float32)).astype(
        jnp.bfloat16
    )
    residual_ref[...] = residual
    wide = residual.astype(jnp.float32)
    mean_sq = jnp.mean(wide * wide, axis=-1, keepdims=True)
    normed_ref[...] = (
        wide * lax.rsqrt(mean_sq + EPS) * gain[...].astype(jnp.float32).reshape(1, -1)
    ).astype(jnp.bfloat16)

    gather = Gather(at, wires, normed_ref, norm_all, local_sems.at[63])
    gather.own_column()
    arrived(*moving_gate)
    arrived(*moving_up)
    units = gate_up_w.shape[1] // 2
    own_units = pl.ds(aligned(at.c * units, units), units)
    crossing, hidden_far, hidden_core = [], [], {}

    def expand(chunk):
        multiply(chunk, norm_all, gate_up_w, total, sums_sent)
        crossing.append(wires.send(sums_sent.at[chunk], sums_landed.at[chunk], at.away(h=1)))

    def activate(chunk):
        crossing[chunk].wait_recv()
        gate = total[chunk, near, :units] + sums_landed[chunk, :, :units].astype(jnp.float32)
        up = total[chunk, near, units:] + sums_landed[chunk, :, units:].astype(jnp.float32)
        hidden = gate / (1.0 + jnp.exp(-gate)) * up
        hidden_all[chunk, near, own_units] = hidden.astype(hidden_all.dtype)
        block = hidden_all.at[chunk, near, own_units]
        hidden_far.append(wires.send(block, block, at.away(h=1)))
        hidden_core[chunk] = [wires.send(block, block, at.away(c=1))]

    def relay(chunk):
        hidden_far[chunk].wait_recv()
        block = hidden_all.at[chunk, far, own_units]
        hidden_core[chunk].append(wires.send(block, block, at.away(c=1)))

    tiles = partial.shape[1]
    back = {}

    def contract(chunk):
        for copy in hidden_core[chunk]:
            copy.wait_recv()
        dx, dy = HOPS[chunk]
        for index in range(tiles):
            cols = pl.ds(index * tile, tile)
            partial[chunk, index] = jnp.dot(
                hidden_all[chunk], down_w[:, cols], preferred_element_type=jnp.float32
            ).astype(partial.dtype)
            if chunk:
                back[chunk, index] = wires.send(
                    partial.at[chunk, index],
                    partial_landed.at[chunk - 1, index],
                    at.away(x=dx, y=dy),
                )

    expand(0)
    gather.neighbours()
    gather.landed(1)
    expand(1)
    activate(0)
    gather.landed(2)
    expand(2)
    gather.diagonal()
    moving_down = down_blocks()
    activate(1)
    relay(0)
    gather.landed(3)
    expand(3)
    activate(2)
    relay(1)
    down_copies, down_own = moving_down
    for copy in down_copies[:-1]:
        copy.wait_recv()

    @pl.when(at.p != at.c)
    def _():
        down_copies[-1].wait_recv()

    @pl.when(at.p == at.c)
    def _():
        down_own.wait()

    contract(1)
    activate(3)
    relay(2)
    contract(2)
    relay(3)
    contract(3)
    contract(0)

    level_rows = 2 * rows

    def level_sum(level, index):
        span = pl.ds(aligned(level * level_rows, level_rows), level_rows)
        sums = partial[0, index, span, :].astype(jnp.float32)
        for chunk in range(3):
            sums = sums + partial_landed[chunk, index, span, :].astype(jnp.float32)
        return sums

    paired = []
    for index in range(tiles):
        for chunk in (1, 2, 3):
            back[chunk, index].wait_recv()
        for half in range(2):
            pair_sent[index, half] = level_sum(half * 2 + 1 - at.p, index).astype(pair_sent.dtype)
        paired.append(wires.send(pair_sent.at[index], pair_landed.at[index], at.away(p=1)))
    lasting, own_last = [], []
    for index in range(tiles):
        paired[index].wait_recv()
        for half in range(2):
            last_sent[index, half] = (
                level_sum(half * 2 + at.p, index) + pair_landed[index, half].astype(jnp.float32)
            ).astype(last_sent.dtype)
        start = (at.h * 2 + at.c) * (tiles * tile) + index * tile
        target = final.at[:, pl.ds(aligned(start, tile), tile)]
        for dh, dc in ((1, 0), (1, 1), (0, 1), (0, 0)):
            start = aligned(flip(at.c, dc) * rows, rows)
            source = last_sent.at[index, flip(at.h, dh), pl.ds(start, rows)]
            if dh + dc:
                lasting.append(wires.send(source, target, at.away(h=dh, c=dc)))
            else:
                own_last.append(keep(source, target))
    for copy in lasting:
        copy.wait_recv()
    for copy in own_last:
        copy.wait()
    o_ref[...] = (
        residual_ref[...].astype(jnp.float32) + final[...].astype(jnp.float32)
    ).astype(o_ref.dtype)

    for copy in wires.started:
        if copy is not down_copies[-1]:
            copy.wait_send()

    @pl.when(at.p != at.c)
    def _():
        down_copies[-1].wait_send()


def per_device_halves(
    hidden_in, queries, new_keys, new_values, key_cache, value_cache, cache_lengths, parent_ids,
    accepted_leaf, query_gain, key_gain, post_gain, out_weight, gate_weight, up_weight, down_weight,
):
    rows, model = hidden_in.shape
    kv_width = new_keys.shape[1]
    tree, positions = 2 * rows, 2 * key_cache.shape[0]
    column = 8 * rows
    groups = KV_HEADS // 2
    out_cols = out_weight.shape[1] // 4
    units = gate_weight.shape[1] // 4
    bf16, f32 = jnp.bfloat16, jnp.float32
    exponent = -2.0 * (np.arange(HEAD_DIM) % (HEAD_DIM // 2)) / HEAD_DIM
    frequency = (ROPE_BASE**exponent).astype(np.float32).reshape(1, -1)
    tiles = model // 4 // TILE
    vmem = pl.BlockSpec(memory_space=pltpu.VMEM)
    hbm = pl.BlockSpec(memory_space=pltpu.HBM)
    layer_out, accepted_kv = pl.pallas_call(
        layer_kernel,
        out_shape=[
            jax.ShapeDtypeStruct((rows, model), bf16),
            jax.ShapeDtypeStruct((rows, 2 * kv_width), bf16),
        ],
        in_specs=[hbm] * 17,
        out_specs=[vmem, vmem],
        scratch_shapes=[
            pltpu.VMEM((1, cache_lengths.shape[0]), jnp.int32),
            pltpu.VMEM((1, cache_lengths.shape[0]), jnp.int32),
            pltpu.VMEM(parent_ids.shape, jnp.int32),
            pltpu.VMEM((1, HEAD_DIM), f32),
            pltpu.VMEM((1, HEAD_DIM), bf16),
            pltpu.VMEM((1, HEAD_DIM), bf16),
            pltpu.VMEM(post_gain.shape, bf16),
            pltpu.VMEM((tree, model // 2), bf16),
            pltpu.VMEM((tree, kv_width), bf16),
            pltpu.VMEM((tree, kv_width), bf16),
            pltpu.VMEM((positions, kv_width // 2), bf16),
            pltpu.VMEM((positions, kv_width // 2), bf16),
            pltpu.VMEM((groups, tree * HEADS // KV_HEADS, HEAD_DIM), bf16),
            pltpu.VMEM((tree, kv_width), bf16),
            pltpu.VMEM((tree, model // 2), bf16),
            pltpu.VMEM((rows, model), bf16),
            pltpu.VMEM((rows, model), bf16),
            pltpu.VMEM((4, column, model // 2), bf16),
            pltpu.VMEM((4, column, model // 2), bf16),
            pltpu.VMEM((model // 2, out_cols), bf16),
            pltpu.VMEM((model // 2, 2 * units), bf16),
            pltpu.VMEM((2 * units, model // 4), bf16),
            pltpu.VMEM((4, column, out_cols), f32),
            pltpu.VMEM((4, column // 2, out_cols), bf16),
            pltpu.VMEM((4, column // 2, out_cols), bf16),
            pltpu.VMEM((4, column // 2, out_cols), bf16),
            pltpu.VMEM((rows, model), bf16),
            pltpu.VMEM((rows, model), bf16),
            pltpu.VMEM((rows, model), bf16),
            pltpu.VMEM((4, column, 2 * units), f32),
            pltpu.VMEM((4, column // 2, 2 * units), bf16),
            pltpu.VMEM((4, column // 2, 2 * units), bf16),
            pltpu.VMEM((4, column, 2 * units), bf16),
            pltpu.VMEM((4, tiles, column, TILE), bf16),
            pltpu.VMEM((3, tiles, column, TILE), bf16),
            pltpu.VMEM((tiles, 2, 2 * rows, TILE), bf16),
            pltpu.VMEM((tiles, 2, 2 * rows, TILE), bf16),
            pltpu.VMEM((tiles, 2, 2 * rows, TILE), bf16),
            pltpu.VMEM((rows, model), bf16),
            pltpu.SemaphoreType.DMA((SEMAPHORES,)),
            pltpu.SemaphoreType.DMA((SEMAPHORES,)),
            pltpu.SemaphoreType.DMA((64,)),
        ],
        compiler_params=pltpu.CompilerParams(
            collective_id=8, has_side_effects=True, vmem_limit_bytes=63 * 2**20
        ),
    )(
        cache_lengths.reshape(1, -1), accepted_leaf.reshape(1, -1), parent_ids, frequency,
        query_gain.reshape(1, -1), key_gain.reshape(1, -1), post_gain, queries, new_keys,
        new_values, key_cache, value_cache, hidden_in, out_weight, gate_weight, up_weight, down_weight,
    )
    return layer_out, accepted_kv


def solution(mesh):
    in_specs = (
        P(("req", "tp"), None),
        P(("req", "tp"), None),
        P(("req", "tp"), None),
        P(("req", "tp"), None),
        P(("req", "tp"), None),
        P(("req", "tp"), None),
        P(),
        P(),
        P(),
        P(),
        P(),
        P(),
        P("req", "tp"),
        P("req", "tp"),
        P("req", "tp"),
        P("tp", "req"),
    )
    out_specs = (P(("req", "tp"), None), P(("req", "tp"), None))
    by_halves = mesh.shape["req"] == 4 * SIDE and mesh.shape["tp"] == 4
    return jax.shard_map(
        per_device_halves if by_halves else per_device, mesh=mesh, in_specs=in_specs, out_specs=out_specs, check_vma=False
    )
```

```python
import functools

import jax
import jax.numpy as jnp
import numpy as np
from jax import lax
from jax.experimental import pallas as pl
from jax.experimental.pallas import tpu as pltpu
from jax.sharding import PartitionSpec as P

HEADS = 32
KV_HEADS = 8
HEAD_DIM = 128


NEG = -1e30
EPS = 1e-06
ROPE_BASE = 1000000.0


def swapped(value, axis, bit):
    mask = 2**bit
    pairs = [(source, source ^ mask) for source in range(lax.axis_size(axis))]
    return lax.ppermute(value, axis, pairs)


def head_norm(values, gain_vec):
    mean_sq = jnp.mean(values * values, axis=-1, keepdims=True)
    return values * lax.rsqrt(mean_sq + EPS) * gain_vec.astype(jnp.float32)


def rotate(values, position):
    head_width = values.shape[-1]
    half_width = head_width // 2
    frequency = ROPE_BASE ** (-2.0 * jnp.arange(half_width, dtype=jnp.float32) / head_width)
    angles = position[:, None] * frequency[None, :]
    cosine = jnp.cos(angles)[:, None, :]
    sine_part = jnp.sin(angles)[:, None, :]
    front_half = values[..., :half_width]
    back_half = values[..., half_width:]
    return jnp.concatenate(
        [front_half * cosine - back_half * sine_part, back_half * cosine + front_half * sine_part],
        axis=-1,
    )


SIDE = 2
MESH = pl.DeviceIdType.MESH
ANY = pl.BlockSpec(memory_space=pl.ANY)


def meet(peers):
    barrier = pltpu.get_barrier_semaphore()
    for peer in peers:
        pl.semaphore_signal(barrier, inc=1, device_id=peer, device_id_type=MESH)
    pl.semaphore_wait(barrier, len(peers))


def remote(source, target, send_sem, recv_sem, peer):
    return pltpu.make_async_remote_copy(
        src_ref=source,
        dst_ref=target,
        send_sem=send_sem,
        recv_sem=recv_sem,
        device_id=peer,
        device_id_type=MESH,
    )


def line_of(along):
    tp_count = lax.axis_size("tp")
    req, tp = lax.axis_index("req"), lax.axis_index("tp")
    level, side = req // SIDE, req % SIDE
    if along == "level":
        return (
            lax.axis_size("req") // SIDE,
            level,
            lambda index: {"req": index * SIDE + side, "tp": tp},
        )
    return (
        SIDE * tp_count,
        side * tp_count + tp,
        lambda index: {"req": level * SIDE + index // tp_count, "tp": index % tp_count},
    )


def exchange_kernel(along, rows_ref, out_ref, send_sem, recv_sem, own_sem):
    count, mine, device = line_of(along)

    def part(index):
        return rows_ref.at[index]

    others = [(mine + step) % count for step in range(1, count)]
    meet([device(index) for index in others])
    copies = [
        remote(part(index), out_ref.at[mine], send_sem.at[at], recv_sem.at[at], device(index))
        for at, index in enumerate(others)
    ]
    for copy in copies:
        copy.start()
    own = pltpu.make_async_copy(part(mine), out_ref.at[mine], own_sem)
    own.start()
    for copy in copies:
        copy.wait()
    own.wait()


def exchange(rows, along, collective_id):
    count = lax.axis_size("req") // SIDE if along == "level" else SIDE * lax.axis_size("tp")
    part_shape = rows.shape[1:]
    return pl.pallas_call(
        functools.partial(exchange_kernel, along),
        out_shape=jax.ShapeDtypeStruct((count, *part_shape), rows.dtype),
        in_specs=[ANY],
        out_specs=ANY,
        scratch_shapes=[
            pltpu.SemaphoreType.DMA((count - 1,)),
            pltpu.SemaphoreType.DMA((count - 1,)),
            pltpu.SemaphoreType.DMA,
        ],
        compiler_params=pltpu.CompilerParams(collective_id=collective_id, has_side_effects=True),
    )(rows)


def reduce_kernel(
    along, mode, rows_ref, out_ref, landed, held,
    pair_send, pair_recv, far_send, far_recv, last_send, last_recv, own_sems,
):
    count, mine, device = line_of(along)
    half, place, parity = count // 2, mine // 2, mine % 2
    depth = landed.shape[1]
    piece = depth // 2

    def part(index, start, size):
        if mode == "inner":
            return rows_ref.at[pl.ds(start, size), index]
        return rows_ref.at[index, pl.ds(start, size)]

    order = [(place + step) % half for step in range(1, half)]
    pair = device(place * 2 + 1 - parity)
    far_devices = [device(index * 2 + parity) for index in order]
    meet(far_devices + [pair])
    inward, kept, outward = [], [], []
    for at, index in enumerate(order):
        for cut in range(2):
            copy = remote(
                part(index * 2 + 1 - parity, cut * piece, piece),
                landed.at[at, pl.ds(cut * piece, piece)],
                pair_send.at[at * 2 + cut],
                pair_recv.at[at * 2 + cut],
                pair,
            )
            copy.start()
            inward.append(copy)
        copy = pltpu.make_async_copy(
            part(index * 2 + parity, 0, depth), held.at[at], own_sems.at[at + 1]
        )
        copy.start()
        kept.append(copy)
    last = remote(
        part(place * 2 + 1 - parity, 0, depth), out_ref.at[1], last_send, last_recv, pair
    )
    last.start()
    own = pltpu.make_async_copy(part(mine, 0, depth), out_ref.at[0], own_sems.at[0])
    own.start()
    for at, peer in enumerate(far_devices):
        kept[at].wait()
        for cut in range(2):
            inward[at * 2 + cut].wait_recv()

            @pl.loop(cut * piece, (cut + 1) * piece)
            def _(row):
                total = held[at, row].astype(jnp.float32) + landed[at, row].astype(jnp.float32)
                held[at, row] = total.astype(held.dtype)

            copy = remote(
                held.at[at, pl.ds(cut * piece, piece)],
                out_ref.at[at + 2, pl.ds(cut * piece, piece)],
                far_send.at[at * 2 + cut],
                far_recv.at[at * 2 + cut],
                peer,
            )
            copy.start()
            outward.append(copy)
    own.wait()
    last.wait()
    for copy in inward:
        copy.wait_send()
    for copy in outward:
        copy.wait()


def reduced(rows, along, mode, collective_id):
    count = lax.axis_size("req") // SIDE if along == "level" else SIDE * lax.axis_size("tp")
    half = count // 2
    if mode == "inner":
        part_shape = rows.shape[:1] + rows.shape[2:]
    else:
        part_shape = rows.shape[1:]
    parts = pl.pallas_call(
        functools.partial(reduce_kernel, along, mode),
        out_shape=jax.ShapeDtypeStruct((half + 1, *part_shape), rows.dtype),
        in_specs=[ANY],
        out_specs=ANY,
        scratch_shapes=[
            pltpu.VMEM((half - 1, *part_shape), rows.dtype),
            pltpu.VMEM((half - 1, *part_shape), rows.dtype),
            pltpu.SemaphoreType.DMA((2 * (half - 1),)),
            pltpu.SemaphoreType.DMA((2 * (half - 1),)),
            pltpu.SemaphoreType.DMA((2 * (half - 1),)),
            pltpu.SemaphoreType.DMA((2 * (half - 1),)),
            pltpu.SemaphoreType.DMA,
            pltpu.SemaphoreType.DMA,
            pltpu.SemaphoreType.DMA((half,)),
        ],
        compiler_params=pltpu.CompilerParams(
            collective_id=collective_id, has_side_effects=True, vmem_limit_bytes=40 * 2**20
        ),
    )(rows)
    return jnp.sum(parts.astype(jnp.float32), axis=0)


def gather_kernel(rows_ref, out_ref, far_send, far_recv, near_send, near_recv, own_sem):
    count, mine, device = line_of("level")
    half, place, parity = count // 2, mine // 2, mine % 2
    pair = device(place * 2 + 1 - parity)
    order = [(place + step) % half for step in range(1, half)]
    far_devices = [device(index * 2 + parity) for index in order]
    meet(far_devices + [pair])
    far, near = [], []
    for cut in range(2):
        for peer in far_devices:
            at = len(far)
            copy = remote(
                rows_ref.at[cut], out_ref.at[mine, cut], far_send.at[at], far_recv.at[at], peer
            )
            copy.start()
            far.append(copy)
    own = pltpu.make_async_copy(rows_ref, out_ref.at[mine], own_sem)
    own.start()
    for cut in range(2):
        at = len(near)
        copy = remote(
            rows_ref.at[cut], out_ref.at[mine, cut], near_send.at[at], near_recv.at[at], pair
        )
        copy.start()
        near.append(copy)
    for cut in range(2):
        for step in range(1, half):
            far[cut * (half - 1) + step - 1].wait_recv()
            landed = out_ref.at[((place - step + half) % half) * 2 + parity, cut]
            at = len(near)
            copy = remote(landed, landed, near_send.at[at], near_recv.at[at], pair)
            copy.start()
            near.append(copy)
    own.wait()
    for copy in near:
        copy.wait()
    for copy in far:
        copy.wait_send()


def gathered_levels(rows, collective_id):
    count = lax.axis_size("req") // SIDE
    half = count // 2
    rows = rows.reshape(2, rows.shape[0] // 2, rows.shape[1])
    return pl.pallas_call(
        gather_kernel,
        out_shape=jax.ShapeDtypeStruct((count, *rows.shape), rows.dtype),
        in_specs=[ANY],
        out_specs=ANY,
        scratch_shapes=[
            pltpu.SemaphoreType.DMA((2 * (half - 1),)),
            pltpu.SemaphoreType.DMA((2 * (half - 1),)),
            pltpu.SemaphoreType.DMA((2 * half,)),
            pltpu.SemaphoreType.DMA((2 * half,)),
            pltpu.SemaphoreType.DMA,
        ],
        compiler_params=pltpu.CompilerParams(collective_id=collective_id, has_side_effects=True),
    )(rows)


def slices_kernel(
    rows_ref, out_ref, send_level, recv_level, send_far, recv_far, send_core, recv_core, own_sem
):
    tp_count = lax.axis_size("tp")
    levels = lax.axis_size("req") // SIDE
    req, tp = lax.axis_index("req"), lax.axis_index("tp")
    level, side = req // SIDE, req % SIDE
    place = side * tp_count + tp
    core, chip = tp % 2, place // 2
    chips = SIDE * tp_count // 2
    width = rows_ref.shape[1] // levels

    def columns(index):
        return rows_ref.at[:, pl.ds(pl.multiple_of(index * width, width), width)]

    def chip_place(index):
        return index * 2 + core

    def device(at):
        return {"req": level * SIDE + at // tp_count, "tp": at % tp_count}

    level_ids = [(level + step) % levels for step in range(1, levels)]
    level_devices = [{"req": index * SIDE + side, "tp": tp} for index in level_ids]
    far_devices = [device(chip_place((chip + step) % chips)) for step in range(1, chips)]
    core_device = device(chip * 2 + 1 - core)
    meet(level_devices + far_devices + [core_device])
    first = [
        remote(columns(index), out_ref.at[level, place], send_level.at[at], recv_level.at[at], peer)
        for at, (index, peer) in enumerate(zip(level_ids, level_devices))
    ]
    for copy in first:
        copy.start()
    own = pltpu.make_async_copy(columns(level), out_ref.at[level, place], own_sem)
    own.start()
    far, near = [], []
    for step in range(levels):
        source_level = (level - step + levels) % levels
        target = out_ref.at[source_level, place]
        if step > 0:
            first[step - 1].wait_recv()
        source = columns(level) if step == 0 else target
        for peer in far_devices:
            at = len(far)
            copy = remote(source, target, send_far.at[at], recv_far.at[at], peer)
            copy.start()
            far.append(copy)
        at = len(near)
        copy = remote(source, target, send_core.at[at], recv_core.at[at], core_device)
        copy.start()
        near.append(copy)
    for step in range(levels):
        source_level = (level - step + levels) % levels
        for hop in range(1, chips):
            far[step * (chips - 1) + hop - 1].wait_recv()
            landed = out_ref.at[source_level, chip_place((chip - hop + chips) % chips)]
            at = len(near)
            copy = remote(landed, landed, send_core.at[at], recv_core.at[at], core_device)
            copy.start()
            near.append(copy)
    own.wait()
    for copy in near:
        copy.wait()
    for copy in first + far:
        copy.wait_send()


def feature_slices(rows, collective_id):
    levels = lax.axis_size("req") // SIDE
    places = SIDE * lax.axis_size("tp")
    width = rows.shape[1] // levels
    chips = places // 2
    gathered = pl.pallas_call(
        slices_kernel,
        out_shape=jax.ShapeDtypeStruct((levels, places, rows.shape[0], width), rows.dtype),
        in_specs=[ANY],
        out_specs=ANY,
        scratch_shapes=[
            pltpu.SemaphoreType.DMA((levels - 1,)),
            pltpu.SemaphoreType.DMA((levels - 1,)),
            pltpu.SemaphoreType.DMA((levels * (chips - 1),)),
            pltpu.SemaphoreType.DMA((levels * (chips - 1),)),
            pltpu.SemaphoreType.DMA((levels * chips,)),
            pltpu.SemaphoreType.DMA((levels * chips,)),
            pltpu.SemaphoreType.DMA,
        ],
        compiler_params=pltpu.CompilerParams(collective_id=collective_id, has_side_effects=True),
    )(rows)
    return gathered.reshape(-1, width)


def paired_halves(shard, axis):
    side = lax.axis_index("req") % SIDE
    half = shard.shape[axis] // 2
    kept = lax.dynamic_slice_in_dim(shard, side * half, half, axis)
    sent = lax.dynamic_slice_in_dim(shard, (1 - side) * half, half, axis)
    return kept, sent


def joined(kept, received, axis):
    side = lax.axis_index("req") % SIDE
    low = jnp.where(side == 0, kept, received)
    high = jnp.where(side == 0, received, kept)
    return jnp.concatenate([low, high], axis=axis)


def attention_kernel(
    limit_ref, query_ref, key_ref, value_ref, fresh_key_ref, fresh_value_ref, allowed_ref,
    top_ref, total_ref, sum_ref,
):
    group_size = query_ref.shape[1] // HEAD_DIM
    query = jnp.concatenate(
        [query_ref[:, at * HEAD_DIM : (at + 1) * HEAD_DIM] for at in range(group_size)], axis=0
    )
    score_scale = HEAD_DIM ** (-0.5)
    limit = limit_ref[0]
    chunk = key_ref.shape[0] // 4

    def score(keys):
        return (
            lax.dot_general(
                query, keys, (((1,), (1,)), ((), ())), preferred_element_type=jnp.float32
            )
            * score_scale
        )

    def weigh(scores, top, allowed):
        weights = jnp.where(allowed, jnp.exp(scores - top), 0.0).astype(jnp.bfloat16)
        return weights, jnp.sum(weights.astype(jnp.float32), axis=-1, keepdims=True)

    allowed = jnp.concatenate([allowed_ref[...]] * group_size, axis=0) > 0.5
    scores = jnp.where(allowed, score(fresh_key_ref[...]), NEG)
    top = jnp.max(scores, axis=-1, keepdims=True)
    weights, total = weigh(scores, top, allowed)
    summed = jnp.dot(weights, fresh_value_ref[...], preferred_element_type=jnp.float32)

    def step(index, running):
        top, total, summed = running
        start = pl.multiple_of(index * chunk, chunk)
        keys = key_ref[pl.ds(start, chunk), :]
        values = value_ref[pl.ds(start, chunk), :]
        allowed = lax.broadcasted_iota(jnp.int32, (query.shape[0], chunk), 1) + start < limit
        scores = jnp.where(allowed, score(keys), NEG)
        new_top = jnp.maximum(top, jnp.max(scores, axis=-1, keepdims=True))
        weights, chunk_total = weigh(scores, new_top, allowed)
        shrink = jnp.exp(top - new_top)
        summed = summed * shrink + jnp.dot(weights, values, preferred_element_type=jnp.float32)
        return new_top, total * shrink + chunk_total, summed

    live = jnp.clip((limit + chunk - 1) // chunk, 0, 4)
    top, total, summed = lax.fori_loop(0, live, step, (top, total, summed))
    top_ref[0] = top
    total_ref[0] = total
    sum_ref[0] = summed


def attend(limit, query, keys, values, fresh_keys, fresh_values, allowed):
    rows, fresh_rows, cached_rows = query.shape[0], fresh_keys.shape[0], keys.shape[0]
    group_size = HEADS // KV_HEADS
    group_rows = rows * group_size

    def columns(block_rows, width):
        return pl.BlockSpec((block_rows, width), lambda head, limit_ref: (0, head))

    def lead(width):
        return pl.BlockSpec((1, group_rows, width), lambda head, limit_ref: (head, 0, 0))

    results = pl.pallas_call(
        attention_kernel,
        out_shape=[
            jax.ShapeDtypeStruct((KV_HEADS, group_rows, width), jnp.float32)
            for width in (1, 1, HEAD_DIM)
        ],
        grid_spec=pltpu.PrefetchScalarGridSpec(
            num_scalar_prefetch=1,
            grid=(KV_HEADS,),
            in_specs=[
                columns(rows, group_size * HEAD_DIM),
                columns(cached_rows, HEAD_DIM),
                columns(cached_rows, HEAD_DIM),
                columns(fresh_rows, HEAD_DIM),
                columns(fresh_rows, HEAD_DIM),
                pl.BlockSpec((rows, fresh_rows), lambda head, limit_ref: (0, 0)),
            ],
            out_specs=[lead(1), lead(1), lead(HEAD_DIM)],
        ),
        compiler_params=pltpu.CompilerParams(vmem_limit_bytes=32 * 2**20),
        cost_estimate=pl.CostEstimate(
            flops=4 * group_rows * cached_rows * KV_HEADS * HEAD_DIM,
            bytes_accessed=4 * cached_rows * KV_HEADS * HEAD_DIM,
            transcendentals=group_rows * cached_rows * KV_HEADS,
        ),
    )(limit, query, keys, values, fresh_keys, fresh_values, allowed)
    return [
        result.reshape(KV_HEADS, group_size, rows, result.shape[2]) for result in results
    ]


def ancestors(parent_row):
    node_count = parent_row.shape[0]
    node_ids = jnp.arange(node_count, dtype=jnp.int32)
    identity_mat = (node_ids[:, None] == node_ids[None, :]).astype(jnp.float32)
    parent_mat = (parent_row[:, None] == node_ids[None, :]).astype(jnp.float32) * (
        1.0 - identity_mat
    )
    reached = jnp.minimum(identity_mat + parent_mat, 1.0)
    for sweep in range(node_count.bit_length()):
        reached = jnp.minimum(jnp.dot(reached, reached, precision=lax.Precision.HIGHEST), 1.0)
    return reached


def per_device(
    hidden_in,
    queries,
    new_keys,
    new_values,
    key_cache,
    value_cache,
    cache_lengths,
    parent_ids,
    accepted_leaf,
    query_gain,
    key_gain,
    post_gain,
    out_weight,
    gate_weight,
    up_weight,
    down_weight,
):
    half_rows = queries.shape[0]
    out_kept, out_sent = paired_halves(out_weight, 1)
    out_received = swapped(out_sent, "req", 0)
    gate_kept, gate_sent = paired_halves(gate_weight, 1)
    up_kept, up_sent = paired_halves(up_weight, 1)
    gate_up_received = swapped(jnp.concatenate([gate_sent, up_sent], axis=1), "req", 0)
    gate_up_kept = jnp.concatenate([gate_kept, up_kept], axis=1)
    down_kept, down_sent = paired_halves(down_weight, 0)
    out_full = joined(out_kept, out_received, 0)
    gate_up_full = joined(gate_up_kept, gate_up_received, 0)
    tree_size = 2 * half_rows
    kv_width = new_keys.shape[1]
    q_width = queries.shape[1]
    tp_count = lax.axis_size("tp")
    device = lax.axis_index(("req", "tp"))
    request = device // 2
    pair_side = lax.axis_index("tp") % 2
    cache_length = lax.dynamic_index_in_dim(cache_lengths, request, 0, keepdims=False)
    parent_row = lax.dynamic_index_in_dim(parent_ids, request, 0, keepdims=False)
    leaf_index = lax.dynamic_index_in_dim(accepted_leaf, request, 0, keepdims=False)
    reached = ancestors(parent_row)
    node_depth = jnp.sum(reached, axis=1) - 1.0
    node_ids = jnp.arange(tree_size, dtype=jnp.int32)
    local_ids = jnp.arange(half_rows, dtype=jnp.int32)
    node_order = jnp.concatenate(
        [pair_side * half_rows + local_ids, (1 - pair_side) * half_rows + local_ids]
    )
    reorder = (node_order[:, None] == node_ids[None, :]).astype(jnp.float32)
    reached_rows = jnp.dot(reorder, reached, precision=lax.Precision.HIGHEST)
    own_cols = jnp.dot(reached_rows, reorder[:half_rows].T, precision=lax.Precision.HIGHEST) > 0.5
    own_depth = jnp.dot(reorder[:half_rows], node_depth, precision=lax.Precision.HIGHEST)
    position = cache_length.astype(jnp.float32) + own_depth
    query_heads = rotate(
        head_norm(queries.astype(jnp.float32).reshape(half_rows, HEADS, HEAD_DIM), query_gain),
        position,
    ).astype(jnp.bfloat16)
    key_heads = rotate(
        head_norm(new_keys.astype(jnp.float32).reshape(half_rows, KV_HEADS, HEAD_DIM), key_gain),
        position,
    ).astype(jnp.bfloat16)
    query_own = query_heads.reshape(half_rows, q_width)
    fresh_own = jnp.concatenate([key_heads.reshape(half_rows, kv_width), new_values], axis=1)
    query_other, fresh_other = swapped((query_own, fresh_own), "tp", 0)
    query_all = jnp.concatenate([query_own, query_other], axis=0)
    limit = (cache_length - pair_side * key_cache.shape[0]).reshape(1)
    run_top, run_total, summed = attend(
        limit,
        query_all,
        key_cache,
        value_cache,
        key_heads.reshape(half_rows, kv_width),
        new_values,
        own_cols.astype(jnp.float32),
    )
    far_top, far_total, far_sum = (
        swapped(run_top[:, :, half_rows:].astype(jnp.bfloat16), "tp", 0).astype(jnp.float32),
        swapped(run_total[:, :, half_rows:].astype(jnp.bfloat16), "tp", 0).astype(jnp.float32),
        swapped(summed[:, :, half_rows:].astype(jnp.bfloat16), "tp", 0).astype(jnp.float32),
    )
    near_top = run_top[:, :, :half_rows]
    joint_top = jnp.maximum(near_top, far_top)
    near_scale = jnp.exp(near_top - joint_top)
    far_scale = jnp.exp(far_top - joint_top)
    denominator = run_total[:, :, :half_rows] * near_scale + far_total * far_scale
    merged = (summed[:, :, :half_rows] * near_scale + far_sum * far_scale) / denominator
    attended = jnp.transpose(merged, (2, 0, 1, 3)).reshape(half_rows, q_width).astype(jnp.bfloat16)
    leaf_pick = (node_ids == leaf_index).astype(jnp.float32)
    leaf_row = jnp.dot(leaf_pick, reached, precision=lax.Precision.HIGHEST)
    out_depths = (pair_side * half_rows + local_ids).astype(jnp.float32)
    chosen = leaf_row[None, :] * (node_depth[None, :] == out_depths[:, None]).astype(jnp.float32)
    chosen = jnp.dot(chosen, reorder.T, precision=lax.Precision.HIGHEST)
    fresh_all = jnp.concatenate([fresh_own, fresh_other], axis=0)
    accepted_kv = jnp.dot(
        chosen.astype(jnp.bfloat16), fresh_all, preferred_element_type=jnp.float32
    ).astype(jnp.bfloat16)
    levels = lax.axis_size("req") // SIDE
    places = SIDE * tp_count
    attn_slice = feature_slices(attended, 0)
    attn_slice, down_sent = lax.optimization_barrier((attn_slice, down_sent))
    down_full = joined(down_kept, swapped(down_sent, "req", 0), 1)
    projected = jnp.dot(attn_slice, out_full, preferred_element_type=jnp.float32)
    projected = projected.astype(jnp.bfloat16).reshape(levels, places, half_rows, -1)
    projected = reduced(projected, "level", "lead", 1).astype(jnp.bfloat16)
    projected = exchange(projected.reshape(places, half_rows, -1), "place", 2)
    own_projected = jnp.transpose(
        projected.reshape(SIDE, tp_count, half_rows, -1), (2, 1, 0, 3)
    ).reshape(half_rows, -1)
    residual = (hidden_in.astype(jnp.float32) + own_projected.astype(jnp.float32)).astype(
        jnp.bfloat16
    )
    residual_wide = residual.astype(jnp.float32)
    mean_sq = jnp.mean(residual_wide * residual_wide, axis=-1, keepdims=True)
    normed = (residual_wide * lax.rsqrt(mean_sq + EPS) * post_gain.astype(jnp.float32)).astype(
        jnp.bfloat16
    )
    normed_slice = feature_slices(normed, 3)
    sums = jnp.dot(normed_slice, gate_up_full, preferred_element_type=jnp.float32)
    sums = sums.astype(jnp.bfloat16).reshape(levels, places, half_rows, -1)
    sums = reduced(sums, "level", "lead", 4).reshape(places * half_rows, -1)
    hidden_width = sums.shape[1] // 2
    hidden = (jax.nn.silu(sums[:, :hidden_width]) * sums[:, hidden_width:]).astype(jnp.bfloat16)
    hidden_all = gathered_levels(hidden, 5).reshape(-1, hidden_width)
    partial_out = jnp.dot(hidden_all, down_full, preferred_element_type=jnp.float32)
    partial_out = partial_out.astype(jnp.bfloat16).reshape(levels, places, half_rows, -1)
    paired_sum = reduced(partial_out, "place", "inner", 6).astype(jnp.bfloat16)
    mlp_own = exchange(paired_sum, "level", 7)
    mlp_own = jnp.transpose(mlp_own, (1, 0, 2)).reshape(half_rows, -1).astype(jnp.float32)
    layer_out = (residual_wide + mlp_own).astype(jnp.bfloat16)
    return (layer_out, accepted_kv)


def flip(value, bit):
    return 1 - value if bit else value


class Place:
    def __init__(self):
        req, tp = lax.axis_index("req"), lax.axis_index("tp")
        level = req // SIDE
        self.h, self.p = level // 2, level % 2
        self.x, self.y, self.c = req % SIDE, tp // 2, tp % 2

    def away(self, h=0, p=0, x=0, y=0, c=0):
        return self.at(flip(self.h, h), flip(self.p, p), flip(self.x, x), flip(self.y, y), flip(self.c, c))

    def at(self, h, p, x, y, c):
        return {"req": (h * 2 + p) * SIDE + x, "tp": y * 2 + c}


class Wires:
    def __init__(self, send_sems, recv_sems):
        self.send_sems, self.recv_sems = send_sems, recv_sems
        self.started = []

    def make(self, source, target, peer):
        at = len(self.started)
        copy = remote(source, target, self.send_sems.at[at], self.recv_sems.at[at], peer)
        self.started.append(copy)
        return copy

    def send(self, source, target, peer):
        copy = self.make(source, target, peer)
        copy.start()
        return copy


def aligned(value, by):
    return pl.multiple_of(value, by)


HOPS = ((0, 0), (1, 0), (0, 1), (1, 1))


SEMAPHORES = 192
TILE = 256


class Gather:
    def __init__(self, place, wires, own_ref, all_ref, local_sem):
        self.place, self.wires, self.all_ref = place, wires, all_ref
        self.rows, self.width = own_ref.shape[0], all_ref.shape[2]
        at, width = place, self.width
        kept = own_ref.at[:, pl.ds(aligned(at.h * width, width), width)]
        given = own_ref.at[:, pl.ds(aligned((1 - at.h) * width, width), width)]
        self.far = wires.send(given, self.block(0, 0, 0), at.away(h=1))
        mine = self.block(0, 0, 0)
        self.local = pltpu.make_async_copy(kept, mine, local_sem)
        self.local.start()
        self.pair = [wires.send(kept, mine, at.away(p=1))]
        self.inward = {1: [], 2: [], 3: [None] * 4}
        self.core = {0: [], 1: [], 2: [], 3: []}
        self.spread(kept, 0, 0)

    def block(self, chunk, dh, dp):
        at = self.place
        level = flip(at.h, dh) * 2 + flip(at.p, dp)
        start = aligned((level * 2 + at.c) * self.rows, self.rows)
        return self.all_ref.at[chunk, pl.ds(start, self.rows)]

    def spread(self, source, dh, dp):
        at, wires = self.place, self.wires
        self.core[0].append(wires.send(source, self.block(0, dh, dp), at.away(c=1)))
        self.inward[1].append(wires.send(source, self.block(1, dh, dp), at.away(x=1)))
        self.inward[2].append(wires.send(source, self.block(2, dh, dp), at.away(y=1)))

    def own_column(self):
        self.forward(1, 0)
        self.forward(2, 0)
        far = self.block(0, 1, 0)
        self.far.wait_recv()
        self.pair.append(self.wires.send(far, far, self.place.away(p=1)))
        self.spread(far, 1, 0)
        self.pair[0].wait_recv()
        self.spread(self.block(0, 0, 1), 0, 1)
        self.pair[1].wait_recv()
        self.spread(self.block(0, 1, 1), 1, 1)
        self.local.wait()
        for copy in self.core[0]:
            copy.wait_recv()

    def forward(self, chunk, index):
        at, wires = self.place, self.wires
        dh, dp = ((0, 0), (1, 0), (0, 1), (1, 1))[index]
        self.inward[chunk][index].wait_recv()
        block = self.block(chunk, dh, dp)
        self.core[chunk].append(wires.send(block, block, at.away(c=1)))
        if chunk == 1 and index % 2 == 0:
            self.inward[3][index] = wires.send(block, self.block(3, dh, dp), at.away(y=1))
        if chunk == 2 and index % 2 == 1:
            self.inward[3][index] = wires.send(block, self.block(3, dh, dp), at.away(x=1))

    def neighbours(self):
        for index in range(1, 4):
            self.forward(1, index)
            self.forward(2, index)

    def diagonal(self):
        for index in range(4):
            self.forward(3, index)

    def landed(self, chunk):
        for copy in self.core[chunk]:
            copy.wait_recv()


def normalized(values, gain):
    mean_sq = jnp.mean(values * values, axis=-1, keepdims=True)
    return values * lax.rsqrt(mean_sq + EPS) * gain


def closure(parent_row):
    count = parent_row.shape[1]
    down = lax.broadcasted_iota(jnp.int32, (count, count), 0)
    across = lax.broadcasted_iota(jnp.int32, (count, count), 1)
    same = down == across
    identity = jnp.where(same, 1.0, 0.0).astype(jnp.bfloat16)
    turned = jnp.where(same | (parent_row == down), 1.0, 0.0)
    for sweep in range((count - 1).bit_length()):
        factor = turned.astype(jnp.bfloat16)
        turned = jnp.minimum(jnp.dot(factor, factor, preferred_element_type=jnp.float32), 1.0)
    reached = lax.dot_general(
        identity, turned.astype(jnp.bfloat16), (((1,), (1,)), ((), ())),
        preferred_element_type=jnp.float32,
    )
    return reached, turned


def rotary_phase(
    at, length, parent_row, frequency, query_gain, key_gain, query_rows, key_rows,
    query_heads, query_sent, key_heads,
):
    bf16, f32 = jnp.bfloat16, jnp.float32
    rows = query_rows.shape[0]
    heads = query_heads.shape[0]
    reached, turned = closure(parent_row)
    depth = jnp.sum(reached, axis=1, keepdims=True) - 1.0
    depth = jnp.where(at.c == 0, depth[:rows], depth[rows:])
    angles = (length + depth) * frequency
    lane = lax.broadcasted_iota(jnp.int32, angles.shape, 1)
    cosine = jnp.cos(angles)
    sine = jnp.where(lane < HEAD_DIM // 2, -1.0, 1.0) * jnp.sin(angles)
    own_rows = pl.ds(aligned(at.c * rows, rows), rows)

    def rotated(values, gain):
        normed = normalized(values.astype(f32), gain)
        return (normed * cosine + pltpu.roll(normed, HEAD_DIM // 2, 1) * sine).astype(bf16)

    def lanes(head):
        return pl.ds(aligned(head * HEAD_DIM, HEAD_DIM), HEAD_DIM)

    for head in range(heads):
        query_heads[head, own_rows, :] = rotated(
            query_rows[:, lanes(at.c * heads + head)], query_gain
        )
        query_sent[head] = rotated(query_rows[:, lanes((1 - at.c) * heads + head)], query_gain)
    for head in range(KV_HEADS):
        key_heads[own_rows, lanes(head)] = rotated(key_rows[:, lanes(head)], key_gain)
    return reached, turned


def accept_phase(at, leaf, reached, turned, key_heads, value_rows, accepted_ref):
    bf16, f32 = jnp.bfloat16, jnp.float32
    rows, tree = accepted_ref.shape[0], reached.shape[0]
    depth_across = jnp.sum(turned, axis=0, keepdims=True) - 1.0
    node = lax.broadcasted_iota(jnp.int32, (tree, tree), 0).astype(f32)
    leaf_row = jnp.sum(jnp.where(node == leaf, reached, 0.0), axis=0, keepdims=True)
    place = (at.c * rows + lax.broadcasted_iota(jnp.int32, (rows, tree), 0)).astype(f32)
    chosen = jnp.where(depth_across == place, leaf_row, 0.0).astype(bf16)
    kv_width = key_heads.shape[1]
    accepted_ref[:, :kv_width] = jnp.dot(
        chosen, key_heads[...], preferred_element_type=f32
    ).astype(bf16)
    accepted_ref[:, kv_width:] = jnp.dot(
        chosen, value_rows[...], preferred_element_type=f32
    ).astype(bf16)


def attention_phase(
    at, length, reached, value_rows, arrived_rows, arrived_group, cache_k, cache_v,
    query_heads, key_heads, mixed,
):
    bf16, f32 = jnp.bfloat16, jnp.float32
    tree = key_heads.shape[0]
    group_size = HEADS // KV_HEADS
    groups = query_heads.shape[0] // group_size

    def lanes(head):
        return pl.ds(aligned(head * HEAD_DIM, HEAD_DIM), HEAD_DIM)

    arrived_rows()
    scale = HEAD_DIM**-0.5 * 1.4426950408889634
    tree_bias = jnp.where(reached > 0.5, 0.0, NEG)
    tree_bias = jnp.concatenate([tree_bias] * group_size, axis=0)
    chunk = cache_k.shape[0] // 4
    position = lax.broadcasted_iota(jnp.int32, (1, chunk), 1).astype(f32)
    biases = [
        jnp.where(position + index * chunk < length, 0.0, NEG) for index in range(4)
    ]

    def score(query, keys, bias):
        scores = lax.dot_general(
            query, keys, (((1,), (1,)), ((), ())), preferred_element_type=f32
        )
        return scores * scale + bias

    def weighed(scores, top, values):
        weights = jnp.exp2(scores - top).astype(bf16)
        ones = jnp.ones(values.shape, bf16)
        return jnp.dot(
            weights, jnp.concatenate([values, ones], axis=1), preferred_element_type=f32
        )

    for group in range(groups):
        arrived_group(group)
        query = query_heads[group * group_size : (group + 1) * group_size].reshape(
            group_size * tree, HEAD_DIM
        )
        own = lanes(at.c * groups + group)
        scores = score(query, key_heads[:, own], tree_bias)
        top = jnp.max(scores, axis=-1, keepdims=True)
        summed = weighed(scores, top, value_rows[:, own])
        for index in range(4):
            span = pl.ds(index * chunk, chunk)
            scores = score(query, cache_k[span, lanes(group)], biases[index])
            new_top = jnp.maximum(top, jnp.max(scores, axis=-1, keepdims=True))
            summed = summed * jnp.exp2(top - new_top) + weighed(
                scores, new_top, cache_v[span, lanes(group)]
            )
            top = new_top
        result = (summed[:, :HEAD_DIM] / summed[:, HEAD_DIM:]).astype(bf16)
        for member in range(group_size):
            mixed[:, lanes(group * group_size + member)] = result[
                member * tree : (member + 1) * tree
            ]


def layer_kernel(
    lengths_ref, leaf_ref, parent_ref, frequency_ref, query_gain_ref, key_gain_ref, gain_ref,
    queries_ref, new_keys_ref, new_values_ref, key_cache_ref, value_cache_ref, hidden_in_ref,
    out_w_ref, gate_w_ref, up_w_ref, down_w_ref,
    o_ref, accepted_ref,
    lengths, leaves, parents, frequency, query_gain, key_gain, gain,
    query_rows, query_sent, key_rows, value_rows, cache_k, cache_v, query_heads, key_heads, mixed, attended_ref,
    hidden_ref,
    att_all, norm_all, out_w, gate_up_w, down_w,
    out_total, out_sent, out_landed, out_done, projected, residual_ref, normed_ref,
    total, sums_sent, sums_landed, hidden_all,
    partial, partial_landed, pair_sent, pair_landed, last_sent, final,
    send_sems, recv_sems, local_sems,
):
    at = Place()
    wires = Wires(send_sems, recv_sems)
    rows = queries_ref.shape[0]
    column = 4 * 2 * rows
    half_rows = column // 2
    local = []

    def keep(source, target):
        copy = pltpu.make_async_copy(source, target, local_sems.at[len(local)])
        local.append(copy)
        copy.start()
        return copy

    small = [
        keep(lengths_ref, lengths), keep(leaf_ref, leaves), keep(parent_ref, parents),
        keep(frequency_ref, frequency), keep(query_gain_ref, query_gain),
        keep(key_gain_ref, key_gain), keep(gain_ref, gain),
    ]
    barrier = pltpu.get_barrier_semaphore()
    peers = [
        at.away(p=dp, x=dx, y=dy, c=dc)
        for dp in range(2) for dx in range(2) for dy in range(2) for dc in range(2)
        if dp + dx + dy + dc
    ] + [at.away(h=1), at.away(h=1, c=1)]
    for peer in peers:
        pl.semaphore_signal(barrier, inc=1, device_id=peer, device_id_type=MESH)

    own_span = pl.ds(aligned(at.c * rows, rows), rows)
    small += [keep(queries_ref, query_rows), keep(new_keys_ref, key_rows)]
    own_values = keep(new_values_ref, value_rows.at[own_span])
    groups = KV_HEADS // 2
    cache_copies = []

    def cache_target(target_ref, group):
        depth = key_cache_ref.shape[0]
        return target_ref.at[
            pl.ds(aligned(at.c * depth, depth), depth), pl.ds(group * HEAD_DIM, HEAD_DIM)
        ]

    def cache_source(source_ref, core, group):
        start = aligned((core * groups + group) * HEAD_DIM, HEAD_DIM)
        return source_ref.at[:, pl.ds(start, HEAD_DIM)]

    for group in range(groups):
        cache_copies.append(
            [
                keep(cache_source(source, at.c, group), cache_target(target, group))
                for source, target in ((key_cache_ref, cache_k), (value_cache_ref, cache_v))
            ]
        )
    own_hidden = keep(hidden_in_ref, hidden_ref)
    for copy in small:
        copy.wait()
    request = ((at.h * 2 + at.p) * SIDE + at.x) * 2 + at.y

    def of_request(ref):
        spot = lax.broadcasted_iota(jnp.int32, ref.shape, 1)
        picked = jnp.where(spot == request, ref[...].astype(jnp.float32), 0.0)
        return jnp.sum(picked, axis=1, keepdims=True)

    length = of_request(lengths)
    reached, turned = rotary_phase(
        at, length, parents[pl.ds(request, 1), :], frequency[...],
        query_gain[...].astype(jnp.float32), key_gain[...].astype(jnp.float32),
        query_rows, key_rows, query_heads, query_sent, key_heads,
    )
    pl.semaphore_wait(barrier, len(peers))

    def row_block(ref, start_col, cols):
        depth = ref.shape[0] // 4
        start = aligned((at.p * 2 + at.x) * depth, depth)
        return ref.at[pl.ds(start, depth), pl.ds(start_col, cols)]

    def quarters(source_ref, target_ref, start_col):
        width = source_ref.shape[1] // 4
        copies = []
        for dp, dx in ((0, 1), (1, 0), (1, 1)):
            quarter = flip(at.p, dp) * 2 + flip(at.x, dx)
            source = source_ref.at[:, pl.ds(aligned(quarter * width, width), width)]
            copies.append(
                wires.send(source, row_block(target_ref, start_col, width), at.away(p=dp, x=dx))
            )
        quarter = at.p * 2 + at.x
        source = source_ref.at[:, pl.ds(aligned(quarter * width, width), width)]
        own = keep(source, row_block(target_ref, start_col, width))
        return copies, own

    def down_blocks():
        depth, width = down_w.shape[0] // 2, down_w_ref.shape[1]
        target = down_w.at[
            pl.ds(aligned(at.c * depth, depth), depth), pl.ds(aligned(at.x * width, width), width)
        ]
        copies = []
        for da, db in ((0, 1), (1, 0), (1, 1), (0, 0)):
            pt, xt, ct = flip(at.c, db), flip(at.x, da), at.p
            start = aligned((pt * 2 + xt) * depth, depth)
            source = down_w_ref.at[pl.ds(start, depth)]
            copies.append(wires.make(source, target, at.at(at.h, pt, xt, at.y, ct)))
            if da + db:
                copies[-1].start()
        own = pltpu.make_async_copy(
            down_w_ref.at[pl.ds(aligned((at.p * 2 + at.x) * depth, depth), depth)],
            target,
            local_sems.at[61],
        )

        @pl.when(at.p != at.c)
        def _():
            copies[-1].start()

        @pl.when(at.p == at.c)
        def _():
            own.start()

        return copies, own

    def arrived(copies, own):
        for copy in copies:
            copy.wait_recv()
        own.wait()

    other = at.away(c=1)
    moving_rows = [
        wires.send(query_sent, query_heads.at[:, own_span], other),
        wires.send(key_heads.at[own_span], key_heads.at[own_span], other),
        wires.send(new_values_ref, value_rows.at[own_span], other),
    ]
    moving_cache = [
        [
            wires.send(cache_source(source, 1 - at.c, group), cache_target(target, group), other)
            for source, target in ((key_cache_ref, cache_k), (value_cache_ref, cache_v))
        ]
        for group in range(groups)
    ]
    moving_out = quarters(out_w_ref, out_w, 0)

    def arrived_rows():
        arrived(moving_rows, own_values)

    def arrived_group(group):
        for sent, own in zip(moving_cache[group], cache_copies[group]):
            arrived([sent], own)

    attention_phase(
        at, length, reached, value_rows, arrived_rows, arrived_group, cache_k, cache_v,
        query_heads, key_heads, mixed,
    )
    mixed_width = mixed.shape[1]
    mixed_target = attended_ref.at[:, pl.ds(aligned(at.c * mixed_width, mixed_width), mixed_width)]
    mixed_copy = wires.send(
        mixed.at[pl.ds(aligned((1 - at.c) * rows, rows), rows)], mixed_target, at.away(c=1)
    )
    own_mixed = keep(mixed.at[pl.ds(aligned(at.c * rows, rows), rows)], mixed_target)
    arrived([mixed_copy], own_mixed)
    gather = Gather(at, wires, attended_ref, att_all, local_sems.at[62])
    accept_phase(at, of_request(leaves), reached, turned, key_heads, value_rows, accepted_ref)
    gather.own_column()

    near = pl.ds(aligned(at.h * half_rows, half_rows), half_rows)
    far = pl.ds(aligned((1 - at.h) * half_rows, half_rows), half_rows)
    tile = TILE

    def multiply(chunk, all_ref, weight, total_ref, sent_ref):
        @pl.loop(0, weight.shape[1] // tile)
        def _(index):
            cols = pl.ds(aligned(index * tile, tile), tile)
            total_ref[chunk, :, cols] = jnp.dot(
                all_ref[chunk], weight[:, cols], preferred_element_type=jnp.float32
            )
        sent_ref[chunk] = total_ref[chunk, far, :].astype(sent_ref.dtype)

    arrived(*moving_out)
    crossing = []

    def project(chunk):
        multiply(chunk, att_all, out_w, out_total, out_sent)
        crossing.append(wires.send(out_sent.at[chunk], out_landed.at[chunk], at.away(h=1)))

    width = out_w.shape[1]

    def out_column(p, x, y, c):
        return pl.ds(aligned((y * 2 + c) * (4 * width) + (p * 2 + x) * width, width), width)

    own_cols = out_column(at.p, at.x, at.y, at.c)
    returning, own_projected = [], []

    def give_back(chunk):
        dx, dy = HOPS[chunk]
        crossing[chunk].wait_recv()
        done = out_total[chunk, near, :] + out_landed[chunk].astype(jnp.float32)
        out_done[chunk] = done.astype(out_done.dtype)
        for dp in range(2):
            for dc in range(2):
                start = aligned((flip(at.p, dp) * 2 + flip(at.c, dc)) * rows, rows)
                source = out_done.at[chunk, pl.ds(start, rows)]
                target = projected.at[:, own_cols]
                if dx + dy + dp + dc:
                    returning.append(
                        wires.send(source, target, at.away(p=dp, x=dx, y=dy, c=dc))
                    )
                else:
                    own_projected.append(keep(source, target))

    project(0)
    gather.neighbours()
    gather.landed(1)
    project(1)
    give_back(0)
    gather.landed(2)
    project(2)
    gather.diagonal()
    moving_gate = quarters(gate_w_ref, gate_up_w, 0)
    give_back(1)
    gather.landed(3)
    project(3)
    give_back(2)
    give_back(3)
    moving_up = quarters(up_w_ref, gate_up_w, gate_up_w.shape[1] // 2)
    for copy in returning:
        copy.wait_recv()
    own_projected[0].wait()
    own_hidden.wait()
    residual = (hidden_ref[...].astype(jnp.float32) + projected[...].astype(jnp.float32)).astype(
        jnp.bfloat16
    )
    residual_ref[...] = residual
    wide = residual.astype(jnp.float32)
    mean_sq = jnp.mean(wide * wide, axis=-1, keepdims=True)
    normed_ref[...] = (
        wide * lax.rsqrt(mean_sq + EPS) * gain[...].astype(jnp.float32).reshape(1, -1)
    ).astype(jnp.bfloat16)

    gather = Gather(at, wires, normed_ref, norm_all, local_sems.at[63])
    gather.own_column()
    arrived(*moving_gate)
    arrived(*moving_up)
    units = gate_up_w.shape[1] // 2
    own_units = pl.ds(aligned(at.c * units, units), units)
    crossing, hidden_far, hidden_core = [], [], {}

    def expand(chunk):
        multiply(chunk, norm_all, gate_up_w, total, sums_sent)
        crossing.append(wires.send(sums_sent.at[chunk], sums_landed.at[chunk], at.away(h=1)))

    def activate(chunk):
        crossing[chunk].wait_recv()
        gate = total[chunk, near, :units] + sums_landed[chunk, :, :units].astype(jnp.float32)
        up = total[chunk, near, units:] + sums_landed[chunk, :, units:].astype(jnp.float32)
        hidden = gate / (1.0 + jnp.exp(-gate)) * up
        hidden_all[chunk, near, own_units] = hidden.astype(hidden_all.dtype)
        block = hidden_all.at[chunk, near, own_units]
        hidden_far.append(wires.send(block, block, at.away(h=1)))
        hidden_core[chunk] = [wires.send(block, block, at.away(c=1))]

    def relay(chunk):
        hidden_far[chunk].wait_recv()
        block = hidden_all.at[chunk, far, own_units]
        hidden_core[chunk].append(wires.send(block, block, at.away(c=1)))

    tiles = partial.shape[1]
    back = {}

    def contract(chunk):
        for copy in hidden_core[chunk]:
            copy.wait_recv()
        dx, dy = HOPS[chunk]
        for index in range(tiles):
            cols = pl.ds(index * tile, tile)
            partial[chunk, index] = jnp.dot(
                hidden_all[chunk], down_w[:, cols], preferred_element_type=jnp.float32
            ).astype(partial.dtype)
            if chunk:
                back[chunk, index] = wires.send(
                    partial.at[chunk, index],
                    partial_landed.at[chunk - 1, index],
                    at.away(x=dx, y=dy),
                )

    expand(0)
    gather.neighbours()
    gather.landed(1)
    expand(1)
    activate(0)
    gather.landed(2)
    expand(2)
    gather.diagonal()
    moving_down = down_blocks()
    activate(1)
    relay(0)
    gather.landed(3)
    expand(3)
    activate(2)
    relay(1)
    down_copies, down_own = moving_down
    for copy in down_copies[:-1]:
        copy.wait_recv()

    @pl.when(at.p != at.c)
    def _():
        down_copies[-1].wait_recv()

    @pl.when(at.p == at.c)
    def _():
        down_own.wait()

    contract(1)
    activate(3)
    relay(2)
    contract(2)
    relay(3)
    contract(3)
    contract(0)

    level_rows = 2 * rows

    def level_sum(level, index):
        span = pl.ds(aligned(level * level_rows, level_rows), level_rows)
        sums = partial[0, index, span, :].astype(jnp.float32)
        for chunk in range(3):
            sums = sums + partial_landed[chunk, index, span, :].astype(jnp.float32)
        return sums

    paired = []
    for index in range(tiles):
        for chunk in (1, 2, 3):
            back[chunk, index].wait_recv()
        for half in range(2):
            pair_sent[index, half] = level_sum(half * 2 + 1 - at.p, index).astype(pair_sent.dtype)
        paired.append(wires.send(pair_sent.at[index], pair_landed.at[index], at.away(p=1)))
    lasting, own_last = [], []
    for index in range(tiles):
        paired[index].wait_recv()
        for half in range(2):
            last_sent[index, half] = (
                level_sum(half * 2 + at.p, index) + pair_landed[index, half].astype(jnp.float32)
            ).astype(last_sent.dtype)
        start = (at.h * 2 + at.c) * (tiles * tile) + index * tile
        target = final.at[:, pl.ds(aligned(start, tile), tile)]
        for dh, dc in ((1, 0), (1, 1), (0, 1), (0, 0)):
            start = aligned(flip(at.c, dc) * rows, rows)
            source = last_sent.at[index, flip(at.h, dh), pl.ds(start, rows)]
            if dh + dc:
                lasting.append(wires.send(source, target, at.away(h=dh, c=dc)))
            else:
                own_last.append(keep(source, target))
    for copy in lasting:
        copy.wait_recv()
    for copy in own_last:
        copy.wait()
    o_ref[...] = (
        residual_ref[...].astype(jnp.float32) + final[...].astype(jnp.float32)
    ).astype(o_ref.dtype)

    for copy in wires.started:
        if copy is not down_copies[-1]:
            copy.wait_send()

    @pl.when(at.p != at.c)
    def _():
        down_copies[-1].wait_send()


def per_device_halves(
    hidden_in, queries, new_keys, new_values, key_cache, value_cache, cache_lengths, parent_ids,
    accepted_leaf, query_gain, key_gain, post_gain, out_weight, gate_weight, up_weight, down_weight,
):
    rows, model = hidden_in.shape
    kv_width = new_keys.shape[1]
    tree, positions = 2 * rows, 2 * key_cache.shape[0]
    column = 8 * rows
    out_cols = out_weight.shape[1] // 4
    units = gate_weight.shape[1] // 4
    bf16, f32 = jnp.bfloat16, jnp.float32
    exponent = -2.0 * (np.arange(HEAD_DIM) % (HEAD_DIM // 2)) / HEAD_DIM
    frequency = (ROPE_BASE**exponent).astype(np.float32).reshape(1, -1)
    tiles = model // 4 // TILE
    vmem = pl.BlockSpec(memory_space=pltpu.VMEM)
    hbm = pl.BlockSpec(memory_space=pltpu.HBM)
    layer_out, accepted_kv = pl.pallas_call(
        layer_kernel,
        out_shape=[
            jax.ShapeDtypeStruct((rows, model), bf16),
            jax.ShapeDtypeStruct((rows, 2 * kv_width), bf16),
        ],
        in_specs=[hbm] * 17,
        out_specs=[vmem, vmem],
        scratch_shapes=[
            pltpu.VMEM((1, cache_lengths.shape[0]), jnp.int32),
            pltpu.VMEM((1, cache_lengths.shape[0]), jnp.int32),
            pltpu.VMEM(parent_ids.shape, jnp.int32),
            pltpu.VMEM((1, HEAD_DIM), f32),
            pltpu.VMEM((1, HEAD_DIM), bf16),
            pltpu.VMEM((1, HEAD_DIM), bf16),
            pltpu.VMEM(post_gain.shape, bf16),
            pltpu.VMEM((rows, model), bf16),
            pltpu.VMEM((HEADS // 2, rows, HEAD_DIM), bf16),
            pltpu.VMEM((rows, kv_width), bf16),
            pltpu.VMEM((tree, kv_width), bf16),
            pltpu.VMEM((positions, kv_width // 2), bf16),
            pltpu.VMEM((positions, kv_width // 2), bf16),
            pltpu.VMEM((HEADS // 2, tree, HEAD_DIM), bf16),
            pltpu.VMEM((tree, kv_width), bf16),
            pltpu.VMEM((tree, model // 2), bf16),
            pltpu.VMEM((rows, model), bf16),
            pltpu.VMEM((rows, model), bf16),
            pltpu.VMEM((4, column, model // 2), bf16),
            pltpu.VMEM((4, column, model // 2), bf16),
            pltpu.VMEM((model // 2, out_cols), bf16),
            pltpu.VMEM((model // 2, 2 * units), bf16),
            pltpu.VMEM((2 * units, model // 4), bf16),
            pltpu.VMEM((4, column, out_cols), f32),
            pltpu.VMEM((4, column // 2, out_cols), bf16),
            pltpu.VMEM((4, column // 2, out_cols), bf16),
            pltpu.VMEM((4, column // 2, out_cols), bf16),
            pltpu.VMEM((rows, model), bf16),
            pltpu.VMEM((rows, model), bf16),
            pltpu.VMEM((rows, model), bf16),
            pltpu.VMEM((4, column, 2 * units), f32),
            pltpu.VMEM((4, column // 2, 2 * units), bf16),
            pltpu.VMEM((4, column // 2, 2 * units), bf16),
            pltpu.VMEM((4, column, 2 * units), bf16),
            pltpu.VMEM((4, tiles, column, TILE), bf16),
            pltpu.VMEM((3, tiles, column, TILE), bf16),
            pltpu.VMEM((tiles, 2, 2 * rows, TILE), bf16),
            pltpu.VMEM((tiles, 2, 2 * rows, TILE), bf16),
            pltpu.VMEM((tiles, 2, 2 * rows, TILE), bf16),
            pltpu.VMEM((rows, model), bf16),
            pltpu.SemaphoreType.DMA((SEMAPHORES,)),
            pltpu.SemaphoreType.DMA((SEMAPHORES,)),
            pltpu.SemaphoreType.DMA((64,)),
        ],
        compiler_params=pltpu.CompilerParams(
            collective_id=8, has_side_effects=True, vmem_limit_bytes=63 * 2**20
        ),
    )(
        cache_lengths.reshape(1, -1), accepted_leaf.reshape(1, -1), parent_ids, frequency,
        query_gain.reshape(1, -1), key_gain.reshape(1, -1), post_gain, queries, new_keys,
        new_values, key_cache, value_cache, hidden_in, out_weight, gate_weight, up_weight, down_weight,
    )
    return layer_out, accepted_kv


def solution(mesh):
    in_specs = (
        P(("req", "tp"), None),
        P(("req", "tp"), None),
        P(("req", "tp"), None),
        P(("req", "tp"), None),
        P(("req", "tp"), None),
        P(("req", "tp"), None),
        P(),
        P(),
        P(),
        P(),
        P(),
        P(),
        P("req", "tp"),
        P("req", "tp"),
        P("req", "tp"),
        P("tp", "req"),
    )
    out_specs = (P(("req", "tp"), None), P(("req", "tp"), None))
    by_halves = mesh.shape["req"] == 4 * SIDE and mesh.shape["tp"] == 4
    return jax.shard_map(
        per_device_halves if by_halves else per_device, mesh=mesh, in_specs=in_specs, out_specs=out_specs, check_vma=False
    )
```

```python
import functools

import jax
import jax.numpy as jnp
import numpy as np
from jax import lax
from jax.experimental import pallas as pl
from jax.experimental.pallas import tpu as pltpu
from jax.sharding import PartitionSpec as P

HEADS = 32
KV_HEADS = 8
HEAD_DIM = 128


NEG = -1e30
EPS = 1e-06
ROPE_BASE = 1000000.0


def swapped(value, axis, bit):
    mask = 2**bit
    pairs = [(source, source ^ mask) for source in range(lax.axis_size(axis))]
    return lax.ppermute(value, axis, pairs)


def head_norm(values, gain_vec):
    mean_sq = jnp.mean(values * values, axis=-1, keepdims=True)
    return values * lax.rsqrt(mean_sq + EPS) * gain_vec.astype(jnp.float32)


def rotate(values, position):
    head_width = values.shape[-1]
    half_width = head_width // 2
    frequency = ROPE_BASE ** (-2.0 * jnp.arange(half_width, dtype=jnp.float32) / head_width)
    angles = position[:, None] * frequency[None, :]
    cosine = jnp.cos(angles)[:, None, :]
    sine_part = jnp.sin(angles)[:, None, :]
    front_half = values[..., :half_width]
    back_half = values[..., half_width:]
    return jnp.concatenate(
        [front_half * cosine - back_half * sine_part, back_half * cosine + front_half * sine_part],
        axis=-1,
    )


SIDE = 2
MESH = pl.DeviceIdType.MESH
ANY = pl.BlockSpec(memory_space=pl.ANY)


def meet(peers):
    barrier = pltpu.get_barrier_semaphore()
    for peer in peers:
        pl.semaphore_signal(barrier, inc=1, device_id=peer, device_id_type=MESH)
    pl.semaphore_wait(barrier, len(peers))


def remote(source, target, send_sem, recv_sem, peer):
    return pltpu.make_async_remote_copy(
        src_ref=source,
        dst_ref=target,
        send_sem=send_sem,
        recv_sem=recv_sem,
        device_id=peer,
        device_id_type=MESH,
    )


def line_of(along):
    tp_count = lax.axis_size("tp")
    req, tp = lax.axis_index("req"), lax.axis_index("tp")
    level, side = req // SIDE, req % SIDE
    if along == "level":
        return (
            lax.axis_size("req") // SIDE,
            level,
            lambda index: {"req": index * SIDE + side, "tp": tp},
        )
    return (
        SIDE * tp_count,
        side * tp_count + tp,
        lambda index: {"req": level * SIDE + index // tp_count, "tp": index % tp_count},
    )


def exchange_kernel(along, rows_ref, out_ref, send_sem, recv_sem, own_sem):
    count, mine, device = line_of(along)

    def part(index):
        return rows_ref.at[index]

    others = [(mine + step) % count for step in range(1, count)]
    meet([device(index) for index in others])
    copies = [
        remote(part(index), out_ref.at[mine], send_sem.at[at], recv_sem.at[at], device(index))
        for at, index in enumerate(others)
    ]
    for copy in copies:
        copy.start()
    own = pltpu.make_async_copy(part(mine), out_ref.at[mine], own_sem)
    own.start()
    for copy in copies:
        copy.wait()
    own.wait()


def exchange(rows, along, collective_id):
    count = lax.axis_size("req") // SIDE if along == "level" else SIDE * lax.axis_size("tp")
    part_shape = rows.shape[1:]
    return pl.pallas_call(
        functools.partial(exchange_kernel, along),
        out_shape=jax.ShapeDtypeStruct((count, *part_shape), rows.dtype),
        in_specs=[ANY],
        out_specs=ANY,
        scratch_shapes=[
            pltpu.SemaphoreType.DMA((count - 1,)),
            pltpu.SemaphoreType.DMA((count - 1,)),
            pltpu.SemaphoreType.DMA,
        ],
        compiler_params=pltpu.CompilerParams(collective_id=collective_id, has_side_effects=True),
    )(rows)


def reduce_kernel(
    along, mode, rows_ref, out_ref, landed, held,
    pair_send, pair_recv, far_send, far_recv, last_send, last_recv, own_sems,
):
    count, mine, device = line_of(along)
    half, place, parity = count // 2, mine // 2, mine % 2
    depth = landed.shape[1]
    piece = depth // 2

    def part(index, start, size):
        if mode == "inner":
            return rows_ref.at[pl.ds(start, size), index]
        return rows_ref.at[index, pl.ds(start, size)]

    order = [(place + step) % half for step in range(1, half)]
    pair = device(place * 2 + 1 - parity)
    far_devices = [device(index * 2 + parity) for index in order]
    meet(far_devices + [pair])
    inward, kept, outward = [], [], []
    for at, index in enumerate(order):
        for cut in range(2):
            copy = remote(
                part(index * 2 + 1 - parity, cut * piece, piece),
                landed.at[at, pl.ds(cut * piece, piece)],
                pair_send.at[at * 2 + cut],
                pair_recv.at[at * 2 + cut],
                pair,
            )
            copy.start()
            inward.append(copy)
        copy = pltpu.make_async_copy(
            part(index * 2 + parity, 0, depth), held.at[at], own_sems.at[at + 1]
        )
        copy.start()
        kept.append(copy)
    last = remote(
        part(place * 2 + 1 - parity, 0, depth), out_ref.at[1], last_send, last_recv, pair
    )
    last.start()
    own = pltpu.make_async_copy(part(mine, 0, depth), out_ref.at[0], own_sems.at[0])
    own.start()
    for at, peer in enumerate(far_devices):
        kept[at].wait()
        for cut in range(2):
            inward[at * 2 + cut].wait_recv()

            @pl.loop(cut * piece, (cut + 1) * piece)
            def _(row):
                total = held[at, row].astype(jnp.float32) + landed[at, row].astype(jnp.float32)
                held[at, row] = total.astype(held.dtype)

            copy = remote(
                held.at[at, pl.ds(cut * piece, piece)],
                out_ref.at[at + 2, pl.ds(cut * piece, piece)],
                far_send.at[at * 2 + cut],
                far_recv.at[at * 2 + cut],
                peer,
            )
            copy.start()
            outward.append(copy)
    own.wait()
    last.wait()
    for copy in inward:
        copy.wait_send()
    for copy in outward:
        copy.wait()


def reduced(rows, along, mode, collective_id):
    count = lax.axis_size("req") // SIDE if along == "level" else SIDE * lax.axis_size("tp")
    half = count // 2
    if mode == "inner":
        part_shape = rows.shape[:1] + rows.shape[2:]
    else:
        part_shape = rows.shape[1:]
    parts = pl.pallas_call(
        functools.partial(reduce_kernel, along, mode),
        out_shape=jax.ShapeDtypeStruct((half + 1, *part_shape), rows.dtype),
        in_specs=[ANY],
        out_specs=ANY,
        scratch_shapes=[
            pltpu.VMEM((half - 1, *part_shape), rows.dtype),
            pltpu.VMEM((half - 1, *part_shape), rows.dtype),
            pltpu.SemaphoreType.DMA((2 * (half - 1),)),
            pltpu.SemaphoreType.DMA((2 * (half - 1),)),
            pltpu.SemaphoreType.DMA((2 * (half - 1),)),
            pltpu.SemaphoreType.DMA((2 * (half - 1),)),
            pltpu.SemaphoreType.DMA,
            pltpu.SemaphoreType.DMA,
            pltpu.SemaphoreType.DMA((half,)),
        ],
        compiler_params=pltpu.CompilerParams(
            collective_id=collective_id, has_side_effects=True, vmem_limit_bytes=40 * 2**20
        ),
    )(rows)
    return jnp.sum(parts.astype(jnp.float32), axis=0)


def gather_kernel(rows_ref, out_ref, far_send, far_recv, near_send, near_recv, own_sem):
    count, mine, device = line_of("level")
    half, place, parity = count // 2, mine // 2, mine % 2
    pair = device(place * 2 + 1 - parity)
    order = [(place + step) % half for step in range(1, half)]
    far_devices = [device(index * 2 + parity) for index in order]
    meet(far_devices + [pair])
    far, near = [], []
    for cut in range(2):
        for peer in far_devices:
            at = len(far)
            copy = remote(
                rows_ref.at[cut], out_ref.at[mine, cut], far_send.at[at], far_recv.at[at], peer
            )
            copy.start()
            far.append(copy)
    own = pltpu.make_async_copy(rows_ref, out_ref.at[mine], own_sem)
    own.start()
    for cut in range(2):
        at = len(near)
        copy = remote(
            rows_ref.at[cut], out_ref.at[mine, cut], near_send.at[at], near_recv.at[at], pair
        )
        copy.start()
        near.append(copy)
    for cut in range(2):
        for step in range(1, half):
            far[cut * (half - 1) + step - 1].wait_recv()
            landed = out_ref.at[((place - step + half) % half) * 2 + parity, cut]
            at = len(near)
            copy = remote(landed, landed, near_send.at[at], near_recv.at[at], pair)
            copy.start()
            near.append(copy)
    own.wait()
    for copy in near:
        copy.wait()
    for copy in far:
        copy.wait_send()


def gathered_levels(rows, collective_id):
    count = lax.axis_size("req") // SIDE
    half = count // 2
    rows = rows.reshape(2, rows.shape[0] // 2, rows.shape[1])
    return pl.pallas_call(
        gather_kernel,
        out_shape=jax.ShapeDtypeStruct((count, *rows.shape), rows.dtype),
        in_specs=[ANY],
        out_specs=ANY,
        scratch_shapes=[
            pltpu.SemaphoreType.DMA((2 * (half - 1),)),
            pltpu.SemaphoreType.DMA((2 * (half - 1),)),
            pltpu.SemaphoreType.DMA((2 * half,)),
            pltpu.SemaphoreType.DMA((2 * half,)),
            pltpu.SemaphoreType.DMA,
        ],
        compiler_params=pltpu.CompilerParams(collective_id=collective_id, has_side_effects=True),
    )(rows)


def slices_kernel(
    rows_ref, out_ref, send_level, recv_level, send_far, recv_far, send_core, recv_core, own_sem
):
    tp_count = lax.axis_size("tp")
    levels = lax.axis_size("req") // SIDE
    req, tp = lax.axis_index("req"), lax.axis_index("tp")
    level, side = req // SIDE, req % SIDE
    place = side * tp_count + tp
    core, chip = tp % 2, place // 2
    chips = SIDE * tp_count // 2
    width = rows_ref.shape[1] // levels

    def columns(index):
        return rows_ref.at[:, pl.ds(pl.multiple_of(index * width, width), width)]

    def chip_place(index):
        return index * 2 + core

    def device(at):
        return {"req": level * SIDE + at // tp_count, "tp": at % tp_count}

    level_ids = [(level + step) % levels for step in range(1, levels)]
    level_devices = [{"req": index * SIDE + side, "tp": tp} for index in level_ids]
    far_devices = [device(chip_place((chip + step) % chips)) for step in range(1, chips)]
    core_device = device(chip * 2 + 1 - core)
    meet(level_devices + far_devices + [core_device])
    first = [
        remote(columns(index), out_ref.at[level, place], send_level.at[at], recv_level.at[at], peer)
        for at, (index, peer) in enumerate(zip(level_ids, level_devices))
    ]
    for copy in first:
        copy.start()
    own = pltpu.make_async_copy(columns(level), out_ref.at[level, place], own_sem)
    own.start()
    far, near = [], []
    for step in range(levels):
        source_level = (level - step + levels) % levels
        target = out_ref.at[source_level, place]
        if step > 0:
            first[step - 1].wait_recv()
        source = columns(level) if step == 0 else target
        for peer in far_devices:
            at = len(far)
            copy = remote(source, target, send_far.at[at], recv_far.at[at], peer)
            copy.start()
            far.append(copy)
        at = len(near)
        copy = remote(source, target, send_core.at[at], recv_core.at[at], core_device)
        copy.start()
        near.append(copy)
    for step in range(levels):
        source_level = (level - step + levels) % levels
        for hop in range(1, chips):
            far[step * (chips - 1) + hop - 1].wait_recv()
            landed = out_ref.at[source_level, chip_place((chip - hop + chips) % chips)]
            at = len(near)
            copy = remote(landed, landed, send_core.at[at], recv_core.at[at], core_device)
            copy.start()
            near.append(copy)
    own.wait()
    for copy in near:
        copy.wait()
    for copy in first + far:
        copy.wait_send()


def feature_slices(rows, collective_id):
    levels = lax.axis_size("req") // SIDE
    places = SIDE * lax.axis_size("tp")
    width = rows.shape[1] // levels
    chips = places // 2
    gathered = pl.pallas_call(
        slices_kernel,
        out_shape=jax.ShapeDtypeStruct((levels, places, rows.shape[0], width), rows.dtype),
        in_specs=[ANY],
        out_specs=ANY,
        scratch_shapes=[
            pltpu.SemaphoreType.DMA((levels - 1,)),
            pltpu.SemaphoreType.DMA((levels - 1,)),
            pltpu.SemaphoreType.DMA((levels * (chips - 1),)),
            pltpu.SemaphoreType.DMA((levels * (chips - 1),)),
            pltpu.SemaphoreType.DMA((levels * chips,)),
            pltpu.SemaphoreType.DMA((levels * chips,)),
            pltpu.SemaphoreType.DMA,
        ],
        compiler_params=pltpu.CompilerParams(collective_id=collective_id, has_side_effects=True),
    )(rows)
    return gathered.reshape(-1, width)


def paired_halves(shard, axis):
    side = lax.axis_index("req") % SIDE
    half = shard.shape[axis] // 2
    kept = lax.dynamic_slice_in_dim(shard, side * half, half, axis)
    sent = lax.dynamic_slice_in_dim(shard, (1 - side) * half, half, axis)
    return kept, sent


def joined(kept, received, axis):
    side = lax.axis_index("req") % SIDE
    low = jnp.where(side == 0, kept, received)
    high = jnp.where(side == 0, received, kept)
    return jnp.concatenate([low, high], axis=axis)


def attention_kernel(
    limit_ref, query_ref, key_ref, value_ref, fresh_key_ref, fresh_value_ref, allowed_ref,
    top_ref, total_ref, sum_ref,
):
    group_size = query_ref.shape[1] // HEAD_DIM
    query = jnp.concatenate(
        [query_ref[:, at * HEAD_DIM : (at + 1) * HEAD_DIM] for at in range(group_size)], axis=0
    )
    score_scale = HEAD_DIM ** (-0.5)
    limit = limit_ref[0]
    chunk = key_ref.shape[0] // 4

    def score(keys):
        return (
            lax.dot_general(
                query, keys, (((1,), (1,)), ((), ())), preferred_element_type=jnp.float32
            )
            * score_scale
        )

    def weigh(scores, top, allowed):
        weights = jnp.where(allowed, jnp.exp(scores - top), 0.0).astype(jnp.bfloat16)
        return weights, jnp.sum(weights.astype(jnp.float32), axis=-1, keepdims=True)

    allowed = jnp.concatenate([allowed_ref[...]] * group_size, axis=0) > 0.5
    scores = jnp.where(allowed, score(fresh_key_ref[...]), NEG)
    top = jnp.max(scores, axis=-1, keepdims=True)
    weights, total = weigh(scores, top, allowed)
    summed = jnp.dot(weights, fresh_value_ref[...], preferred_element_type=jnp.float32)

    def step(index, running):
        top, total, summed = running
        start = pl.multiple_of(index * chunk, chunk)
        keys = key_ref[pl.ds(start, chunk), :]
        values = value_ref[pl.ds(start, chunk), :]
        allowed = lax.broadcasted_iota(jnp.int32, (query.shape[0], chunk), 1) + start < limit
        scores = jnp.where(allowed, score(keys), NEG)
        new_top = jnp.maximum(top, jnp.max(scores, axis=-1, keepdims=True))
        weights, chunk_total = weigh(scores, new_top, allowed)
        shrink = jnp.exp(top - new_top)
        summed = summed * shrink + jnp.dot(weights, values, preferred_element_type=jnp.float32)
        return new_top, total * shrink + chunk_total, summed

    live = jnp.clip((limit + chunk - 1) // chunk, 0, 4)
    top, total, summed = lax.fori_loop(0, live, step, (top, total, summed))
    top_ref[0] = top
    total_ref[0] = total
    sum_ref[0] = summed


def attend(limit, query, keys, values, fresh_keys, fresh_values, allowed):
    rows, fresh_rows, cached_rows = query.shape[0], fresh_keys.shape[0], keys.shape[0]
    group_size = HEADS // KV_HEADS
    group_rows = rows * group_size

    def columns(block_rows, width):
        return pl.BlockSpec((block_rows, width), lambda head, limit_ref: (0, head))

    def lead(width):
        return pl.BlockSpec((1, group_rows, width), lambda head, limit_ref: (head, 0, 0))

    results = pl.pallas_call(
        attention_kernel,
        out_shape=[
            jax.ShapeDtypeStruct((KV_HEADS, group_rows, width), jnp.float32)
            for width in (1, 1, HEAD_DIM)
        ],
        grid_spec=pltpu.PrefetchScalarGridSpec(
            num_scalar_prefetch=1,
            grid=(KV_HEADS,),
            in_specs=[
                columns(rows, group_size * HEAD_DIM),
                columns(cached_rows, HEAD_DIM),
                columns(cached_rows, HEAD_DIM),
                columns(fresh_rows, HEAD_DIM),
                columns(fresh_rows, HEAD_DIM),
                pl.BlockSpec((rows, fresh_rows), lambda head, limit_ref: (0, 0)),
            ],
            out_specs=[lead(1), lead(1), lead(HEAD_DIM)],
        ),
        compiler_params=pltpu.CompilerParams(vmem_limit_bytes=32 * 2**20),
        cost_estimate=pl.CostEstimate(
            flops=4 * group_rows * cached_rows * KV_HEADS * HEAD_DIM,
            bytes_accessed=4 * cached_rows * KV_HEADS * HEAD_DIM,
            transcendentals=group_rows * cached_rows * KV_HEADS,
        ),
    )(limit, query, keys, values, fresh_keys, fresh_values, allowed)
    return [
        result.reshape(KV_HEADS, group_size, rows, result.shape[2]) for result in results
    ]


def ancestors(parent_row):
    node_count = parent_row.shape[0]
    node_ids = jnp.arange(node_count, dtype=jnp.int32)
    identity_mat = (node_ids[:, None] == node_ids[None, :]).astype(jnp.float32)
    parent_mat = (parent_row[:, None] == node_ids[None, :]).astype(jnp.float32) * (
        1.0 - identity_mat
    )
    reached = jnp.minimum(identity_mat + parent_mat, 1.0)
    for sweep in range(node_count.bit_length()):
        reached = jnp.minimum(jnp.dot(reached, reached, precision=lax.Precision.HIGHEST), 1.0)
    return reached


def per_device(
    hidden_in,
    queries,
    new_keys,
    new_values,
    key_cache,
    value_cache,
    cache_lengths,
    parent_ids,
    accepted_leaf,
    query_gain,
    key_gain,
    post_gain,
    out_weight,
    gate_weight,
    up_weight,
    down_weight,
):
    half_rows = queries.shape[0]
    out_kept, out_sent = paired_halves(out_weight, 1)
    out_received = swapped(out_sent, "req", 0)
    gate_kept, gate_sent = paired_halves(gate_weight, 1)
    up_kept, up_sent = paired_halves(up_weight, 1)
    gate_up_received = swapped(jnp.concatenate([gate_sent, up_sent], axis=1), "req", 0)
    gate_up_kept = jnp.concatenate([gate_kept, up_kept], axis=1)
    down_kept, down_sent = paired_halves(down_weight, 0)
    out_full = joined(out_kept, out_received, 0)
    gate_up_full = joined(gate_up_kept, gate_up_received, 0)
    tree_size = 2 * half_rows
    kv_width = new_keys.shape[1]
    q_width = queries.shape[1]
    tp_count = lax.axis_size("tp")
    device = lax.axis_index(("req", "tp"))
    request = device // 2
    pair_side = lax.axis_index("tp") % 2
    cache_length = lax.dynamic_index_in_dim(cache_lengths, request, 0, keepdims=False)
    parent_row = lax.dynamic_index_in_dim(parent_ids, request, 0, keepdims=False)
    leaf_index = lax.dynamic_index_in_dim(accepted_leaf, request, 0, keepdims=False)
    reached = ancestors(parent_row)
    node_depth = jnp.sum(reached, axis=1) - 1.0
    node_ids = jnp.arange(tree_size, dtype=jnp.int32)
    local_ids = jnp.arange(half_rows, dtype=jnp.int32)
    node_order = jnp.concatenate(
        [pair_side * half_rows + local_ids, (1 - pair_side) * half_rows + local_ids]
    )
    reorder = (node_order[:, None] == node_ids[None, :]).astype(jnp.float32)
    reached_rows = jnp.dot(reorder, reached, precision=lax.Precision.HIGHEST)
    own_cols = jnp.dot(reached_rows, reorder[:half_rows].T, precision=lax.Precision.HIGHEST) > 0.5
    own_depth = jnp.dot(reorder[:half_rows], node_depth, precision=lax.Precision.HIGHEST)
    position = cache_length.astype(jnp.float32) + own_depth
    query_heads = rotate(
        head_norm(queries.astype(jnp.float32).reshape(half_rows, HEADS, HEAD_DIM), query_gain),
        position,
    ).astype(jnp.bfloat16)
    key_heads = rotate(
        head_norm(new_keys.astype(jnp.float32).reshape(half_rows, KV_HEADS, HEAD_DIM), key_gain),
        position,
    ).astype(jnp.bfloat16)
    query_own = query_heads.reshape(half_rows, q_width)
    fresh_own = jnp.concatenate([key_heads.reshape(half_rows, kv_width), new_values], axis=1)
    query_other, fresh_other = swapped((query_own, fresh_own), "tp", 0)
    query_all = jnp.concatenate([query_own, query_other], axis=0)
    limit = (cache_length - pair_side * key_cache.shape[0]).reshape(1)
    run_top, run_total, summed = attend(
        limit,
        query_all,
        key_cache,
        value_cache,
        key_heads.reshape(half_rows, kv_width),
        new_values,
        own_cols.astype(jnp.float32),
    )
    far_top, far_total, far_sum = (
        swapped(run_top[:, :, half_rows:].astype(jnp.bfloat16), "tp", 0).astype(jnp.float32),
        swapped(run_total[:, :, half_rows:].astype(jnp.bfloat16), "tp", 0).astype(jnp.float32),
        swapped(summed[:, :, half_rows:].astype(jnp.bfloat16), "tp", 0).astype(jnp.float32),
    )
    near_top = run_top[:, :, :half_rows]
    joint_top = jnp.maximum(near_top, far_top)
    near_scale = jnp.exp(near_top - joint_top)
    far_scale = jnp.exp(far_top - joint_top)
    denominator = run_total[:, :, :half_rows] * near_scale + far_total * far_scale
    merged = (summed[:, :, :half_rows] * near_scale + far_sum * far_scale) / denominator
    attended = jnp.transpose(merged, (2, 0, 1, 3)).reshape(half_rows, q_width).astype(jnp.bfloat16)
    leaf_pick = (node_ids == leaf_index).astype(jnp.float32)
    leaf_row = jnp.dot(leaf_pick, reached, precision=lax.Precision.HIGHEST)
    out_depths = (pair_side * half_rows + local_ids).astype(jnp.float32)
    chosen = leaf_row[None, :] * (node_depth[None, :] == out_depths[:, None]).astype(jnp.float32)
    chosen = jnp.dot(chosen, reorder.T, precision=lax.Precision.HIGHEST)
    fresh_all = jnp.concatenate([fresh_own, fresh_other], axis=0)
    accepted_kv = jnp.dot(
        chosen.astype(jnp.bfloat16), fresh_all, preferred_element_type=jnp.float32
    ).astype(jnp.bfloat16)
    levels = lax.axis_size("req") // SIDE
    places = SIDE * tp_count
    attn_slice = feature_slices(attended, 0)
    attn_slice, down_sent = lax.optimization_barrier((attn_slice, down_sent))
    down_full = joined(down_kept, swapped(down_sent, "req", 0), 1)
    projected = jnp.dot(attn_slice, out_full, preferred_element_type=jnp.float32)
    projected = projected.astype(jnp.bfloat16).reshape(levels, places, half_rows, -1)
    projected = reduced(projected, "level", "lead", 1).astype(jnp.bfloat16)
    projected = exchange(projected.reshape(places, half_rows, -1), "place", 2)
    own_projected = jnp.transpose(
        projected.reshape(SIDE, tp_count, half_rows, -1), (2, 1, 0, 3)
    ).reshape(half_rows, -1)
    residual = (hidden_in.astype(jnp.float32) + own_projected.astype(jnp.float32)).astype(
        jnp.bfloat16
    )
    residual_wide = residual.astype(jnp.float32)
    mean_sq = jnp.mean(residual_wide * residual_wide, axis=-1, keepdims=True)
    normed = (residual_wide * lax.rsqrt(mean_sq + EPS) * post_gain.astype(jnp.float32)).astype(
        jnp.bfloat16
    )
    normed_slice = feature_slices(normed, 3)
    sums = jnp.dot(normed_slice, gate_up_full, preferred_element_type=jnp.float32)
    sums = sums.astype(jnp.bfloat16).reshape(levels, places, half_rows, -1)
    sums = reduced(sums, "level", "lead", 4).reshape(places * half_rows, -1)
    hidden_width = sums.shape[1] // 2
    hidden = (jax.nn.silu(sums[:, :hidden_width]) * sums[:, hidden_width:]).astype(jnp.bfloat16)
    hidden_all = gathered_levels(hidden, 5).reshape(-1, hidden_width)
    partial_out = jnp.dot(hidden_all, down_full, preferred_element_type=jnp.float32)
    partial_out = partial_out.astype(jnp.bfloat16).reshape(levels, places, half_rows, -1)
    paired_sum = reduced(partial_out, "place", "inner", 6).astype(jnp.bfloat16)
    mlp_own = exchange(paired_sum, "level", 7)
    mlp_own = jnp.transpose(mlp_own, (1, 0, 2)).reshape(half_rows, -1).astype(jnp.float32)
    layer_out = (residual_wide + mlp_own).astype(jnp.bfloat16)
    return (layer_out, accepted_kv)


def flip(value, bit):
    return 1 - value if bit else value


class Place:
    def __init__(self):
        req, tp = lax.axis_index("req"), lax.axis_index("tp")
        level = req // SIDE
        self.h, self.p = level // 2, level % 2
        self.x, self.y, self.c = req % SIDE, tp // 2, tp % 2

    def away(self, h=0, p=0, x=0, y=0, c=0):
        return self.at(flip(self.h, h), flip(self.p, p), flip(self.x, x), flip(self.y, y), flip(self.c, c))

    def at(self, h, p, x, y, c):
        return {"req": (h * 2 + p) * SIDE + x, "tp": y * 2 + c}


class Wires:
    def __init__(self, send_sems, recv_sems):
        self.send_sems, self.recv_sems = send_sems, recv_sems
        self.started = []

    def make(self, source, target, peer):
        at = len(self.started)
        copy = remote(source, target, self.send_sems.at[at], self.recv_sems.at[at], peer)
        self.started.append(copy)
        return copy

    def send(self, source, target, peer):
        copy = self.make(source, target, peer)
        copy.start()
        return copy


def aligned(value, by):
    return pl.multiple_of(value, by)


HOPS = ((0, 0), (1, 0), (0, 1), (1, 1))


SEMAPHORES = 192
TILE = 256


class Gather:
    def __init__(self, place, wires, own_ref, all_ref, local_sem):
        self.place, self.wires, self.all_ref = place, wires, all_ref
        self.rows, self.width = own_ref.shape[0], all_ref.shape[2]
        at, width = place, self.width
        kept = own_ref.at[:, pl.ds(aligned(at.h * width, width), width)]
        given = own_ref.at[:, pl.ds(aligned((1 - at.h) * width, width), width)]
        self.far = wires.send(given, self.block(0, 0, 0), at.away(h=1))
        mine = self.block(0, 0, 0)
        self.local = pltpu.make_async_copy(kept, mine, local_sem)
        self.local.start()
        self.pair = [wires.send(kept, mine, at.away(p=1))]
        self.inward = {1: [], 2: [], 3: [None] * 4}
        self.core = {0: [], 1: [], 2: [], 3: []}
        self.spread(kept, 0, 0)

    def block(self, chunk, dh, dp):
        at = self.place
        level = flip(at.h, dh) * 2 + flip(at.p, dp)
        start = aligned((level * 2 + at.c) * self.rows, self.rows)
        return self.all_ref.at[chunk, pl.ds(start, self.rows)]

    def spread(self, source, dh, dp):
        at, wires = self.place, self.wires
        self.core[0].append(wires.send(source, self.block(0, dh, dp), at.away(c=1)))
        self.inward[1].append(wires.send(source, self.block(1, dh, dp), at.away(x=1)))
        self.inward[2].append(wires.send(source, self.block(2, dh, dp), at.away(y=1)))

    def own_column(self):
        self.forward(1, 0)
        self.forward(2, 0)
        far = self.block(0, 1, 0)
        self.far.wait_recv()
        self.pair.append(self.wires.send(far, far, self.place.away(p=1)))
        self.spread(far, 1, 0)
        self.pair[0].wait_recv()
        self.spread(self.block(0, 0, 1), 0, 1)
        self.pair[1].wait_recv()
        self.spread(self.block(0, 1, 1), 1, 1)
        self.local.wait()
        for copy in self.core[0]:
            copy.wait_recv()

    def forward(self, chunk, index):
        at, wires = self.place, self.wires
        dh, dp = ((0, 0), (1, 0), (0, 1), (1, 1))[index]
        self.inward[chunk][index].wait_recv()
        block = self.block(chunk, dh, dp)
        self.core[chunk].append(wires.send(block, block, at.away(c=1)))
        if chunk == 1 and index % 2 == 0:
            self.inward[3][index] = wires.send(block, self.block(3, dh, dp), at.away(y=1))
        if chunk == 2 and index % 2 == 1:
            self.inward[3][index] = wires.send(block, self.block(3, dh, dp), at.away(x=1))

    def neighbours(self):
        for index in range(1, 4):
            self.forward(1, index)
            self.forward(2, index)

    def diagonal(self):
        for index in range(4):
            self.forward(3, index)

    def landed(self, chunk):
        for copy in self.core[chunk]:
            copy.wait_recv()


def normalized(values, gain):
    mean_sq = jnp.mean(values * values, axis=-1, keepdims=True)
    return values * lax.rsqrt(mean_sq + EPS) * gain


def closure(parent_row):
    count = parent_row.shape[1]
    down = lax.broadcasted_iota(jnp.int32, (count, count), 0)
    across = lax.broadcasted_iota(jnp.int32, (count, count), 1)
    same = down == across
    identity = jnp.where(same, 1.0, 0.0).astype(jnp.bfloat16)
    turned = jnp.where(same | (parent_row == down), 1.0, 0.0)
    for sweep in range((count - 1).bit_length()):
        factor = turned.astype(jnp.bfloat16)
        turned = jnp.minimum(jnp.dot(factor, factor, preferred_element_type=jnp.float32), 1.0)
    reached = lax.dot_general(
        identity, turned.astype(jnp.bfloat16), (((1,), (1,)), ((), ())),
        preferred_element_type=jnp.float32,
    )
    return reached, turned


def rotary_phase(
    at, length, parent_row, frequency, query_gain, key_gain, query_rows, key_rows,
    query_heads, query_sent, key_heads,
):
    bf16, f32 = jnp.bfloat16, jnp.float32
    rows = query_rows.shape[0]
    heads = query_heads.shape[0]
    reached, turned = closure(parent_row)
    depth = jnp.sum(reached, axis=1, keepdims=True) - 1.0
    depth = jnp.where(at.c == 0, depth[:rows], depth[rows:])
    angles = (length + depth) * frequency
    lane = lax.broadcasted_iota(jnp.int32, angles.shape, 1)
    cosine = jnp.cos(angles)
    sine = jnp.where(lane < HEAD_DIM // 2, -1.0, 1.0) * jnp.sin(angles)
    own_rows = pl.ds(aligned(at.c * rows, rows), rows)

    def rotated(values, gain):
        normed = normalized(values.astype(f32), gain)
        return (normed * cosine + pltpu.roll(normed, HEAD_DIM // 2, 1) * sine).astype(bf16)

    def lanes(head):
        return pl.ds(aligned(head * HEAD_DIM, HEAD_DIM), HEAD_DIM)

    for head in range(heads):
        query_heads[head, own_rows, :] = rotated(
            query_rows[:, lanes(at.c * heads + head)], query_gain
        )
        query_sent[head] = rotated(query_rows[:, lanes((1 - at.c) * heads + head)], query_gain)
    for head in range(KV_HEADS):
        key_heads[own_rows, lanes(head)] = rotated(key_rows[:, lanes(head)], key_gain)
    return reached, turned


def accept_phase(at, leaf, reached, turned, key_heads, value_rows, accepted_ref):
    bf16, f32 = jnp.bfloat16, jnp.float32
    rows, tree = accepted_ref.shape[0], reached.shape[0]
    depth_across = jnp.sum(turned, axis=0, keepdims=True) - 1.0
    node = lax.broadcasted_iota(jnp.int32, (tree, tree), 0).astype(f32)
    leaf_row = jnp.sum(jnp.where(node == leaf, reached, 0.0), axis=0, keepdims=True)
    place = (at.c * rows + lax.broadcasted_iota(jnp.int32, (rows, tree), 0)).astype(f32)
    chosen = jnp.where(depth_across == place, leaf_row, 0.0).astype(bf16)
    kv_width = key_heads.shape[1]
    accepted_ref[:, :kv_width] = jnp.dot(
        chosen, key_heads[...], preferred_element_type=f32
    ).astype(bf16)
    accepted_ref[:, kv_width:] = jnp.dot(
        chosen, value_rows[...], preferred_element_type=f32
    ).astype(bf16)


def attention_phase(
    at, length, reached, value_rows, arrived_rows, arrived_group, cache_k, cache_v,
    query_heads, key_heads, mixed,
):
    bf16, f32 = jnp.bfloat16, jnp.float32
    tree = key_heads.shape[0]
    group_size = HEADS // KV_HEADS
    groups = query_heads.shape[0] // group_size

    def lanes(head):
        return pl.ds(aligned(head * HEAD_DIM, HEAD_DIM), HEAD_DIM)

    arrived_rows()
    scale = HEAD_DIM**-0.5 * 1.4426950408889634
    tree_bias = jnp.where(reached > 0.5, 0.0, NEG)
    tree_bias = jnp.concatenate([tree_bias] * group_size, axis=0)
    chunk = cache_k.shape[0] // 4
    position = lax.broadcasted_iota(jnp.int32, (1, chunk), 1).astype(f32)
    biases = [
        jnp.where(position + index * chunk < length, 0.0, NEG) for index in range(4)
    ]

    def score(query, keys, bias):
        scores = lax.dot_general(
            query, keys, (((1,), (1,)), ((), ())), preferred_element_type=f32
        )
        return scores * scale + bias

    def weighed(scores, top, values):
        weights = jnp.exp2(scores - top).astype(bf16)
        ones = jnp.ones(values.shape, bf16)
        return jnp.dot(
            weights, jnp.concatenate([values, ones], axis=1), preferred_element_type=f32
        )

    for group in range(groups):
        arrived_group(group)
        query = query_heads[group * group_size : (group + 1) * group_size].reshape(
            group_size * tree, HEAD_DIM
        )
        own = lanes(at.c * groups + group)
        scores = score(query, key_heads[:, own], tree_bias)
        top = jnp.max(scores, axis=-1, keepdims=True)
        summed = weighed(scores, top, value_rows[:, own])
        for index in range(4):
            span = pl.ds(index * chunk, chunk)
            scores = score(query, cache_k[span, lanes(group)], biases[index])
            new_top = jnp.maximum(top, jnp.max(scores, axis=-1, keepdims=True))
            summed = summed * jnp.exp2(top - new_top) + weighed(
                scores, new_top, cache_v[span, lanes(group)]
            )
            top = new_top
        result = (summed[:, :HEAD_DIM] / summed[:, HEAD_DIM:]).astype(bf16)
        for member in range(group_size):
            mixed[:, lanes(group * group_size + member)] = result[
                member * tree : (member + 1) * tree
            ]


def layer_kernel(
    lengths_ref, leaf_ref, parent_ref, frequency_ref, query_gain_ref, key_gain_ref, gain_ref,
    queries_ref, new_keys_ref, new_values_ref, key_cache_ref, value_cache_ref, hidden_in_ref,
    out_w_ref, gate_w_ref, up_w_ref, down_w_ref,
    o_ref, accepted_ref,
    lengths, leaves, parents, frequency, query_gain, key_gain, gain,
    query_rows, query_sent, key_rows, value_rows, cache_k, cache_v, query_heads, key_heads, mixed, attended_ref,
    hidden_ref,
    att_all, norm_all, out_w, gate_up_w, down_w,
    out_total, out_sent, out_landed, out_done, projected, residual_ref, normed_ref,
    total, sums_sent, sums_landed, hidden_all,
    partial, partial_landed, pair_sent, pair_landed, last_sent, final,
    send_sems, recv_sems, local_sems,
):
    at = Place()
    wires = Wires(send_sems, recv_sems)
    rows = queries_ref.shape[0]
    column = 4 * 2 * rows
    half_rows = column // 2
    local = []

    def keep(source, target):
        copy = pltpu.make_async_copy(source, target, local_sems.at[len(local)])
        local.append(copy)
        copy.start()
        return copy

    small = [
        keep(lengths_ref, lengths), keep(leaf_ref, leaves), keep(parent_ref, parents),
        keep(frequency_ref, frequency), keep(query_gain_ref, query_gain),
        keep(key_gain_ref, key_gain), keep(gain_ref, gain),
    ]
    barrier = pltpu.get_barrier_semaphore()
    peers = [
        at.away(p=dp, x=dx, y=dy, c=dc)
        for dp in range(2) for dx in range(2) for dy in range(2) for dc in range(2)
        if dp + dx + dy + dc
    ] + [at.away(h=1), at.away(h=1, c=1)]
    for peer in peers:
        pl.semaphore_signal(barrier, inc=1, device_id=peer, device_id_type=MESH)

    own_span = pl.ds(aligned(at.c * rows, rows), rows)
    small += [keep(queries_ref, query_rows), keep(new_keys_ref, key_rows)]
    own_values = keep(new_values_ref, value_rows.at[own_span])
    groups = KV_HEADS // 2
    cache_copies = []

    def cache_target(target_ref, group):
        depth = key_cache_ref.shape[0]
        return target_ref.at[
            pl.ds(aligned(at.c * depth, depth), depth), pl.ds(group * HEAD_DIM, HEAD_DIM)
        ]

    def cache_source(source_ref, core, group):
        start = aligned((core * groups + group) * HEAD_DIM, HEAD_DIM)
        return source_ref.at[:, pl.ds(start, HEAD_DIM)]

    for group in range(groups):
        cache_copies.append(
            [
                keep(cache_source(source, at.c, group), cache_target(target, group))
                for source, target in ((key_cache_ref, cache_k), (value_cache_ref, cache_v))
            ]
        )
    own_hidden = keep(hidden_in_ref, hidden_ref)
    for copy in small:
        copy.wait()
    request = ((at.h * 2 + at.p) * SIDE + at.x) * 2 + at.y

    def of_request(ref):
        spot = lax.broadcasted_iota(jnp.int32, ref.shape, 1)
        picked = jnp.where(spot == request, ref[...].astype(jnp.float32), 0.0)
        return jnp.sum(picked, axis=1, keepdims=True)

    length = of_request(lengths)
    reached, turned = rotary_phase(
        at, length, parents[pl.ds(request, 1), :], frequency[...],
        query_gain[...].astype(jnp.float32), key_gain[...].astype(jnp.float32),
        query_rows, key_rows, query_heads, query_sent, key_heads,
    )
    pl.semaphore_wait(barrier, len(peers))

    def row_block(ref, start_col, cols):
        depth = ref.shape[0] // 4
        start = aligned((at.p * 2 + at.x) * depth, depth)
        return ref.at[pl.ds(start, depth), pl.ds(start_col, cols)]

    def quarters(source_ref, target_ref, start_col):
        width = source_ref.shape[1] // 4
        copies = []
        for dp, dx in ((0, 1), (1, 0), (1, 1)):
            quarter = flip(at.p, dp) * 2 + flip(at.x, dx)
            source = source_ref.at[:, pl.ds(aligned(quarter * width, width), width)]
            copies.append(
                wires.send(source, row_block(target_ref, start_col, width), at.away(p=dp, x=dx))
            )
        quarter = at.p * 2 + at.x
        source = source_ref.at[:, pl.ds(aligned(quarter * width, width), width)]
        own = keep(source, row_block(target_ref, start_col, width))
        return copies, own

    def down_blocks():
        depth, width = down_w.shape[0] // 2, down_w_ref.shape[1]
        target = down_w.at[
            pl.ds(aligned(at.c * depth, depth), depth), pl.ds(aligned(at.x * width, width), width)
        ]
        copies = []
        for da, db in ((0, 1), (1, 0), (1, 1), (0, 0)):
            pt, xt, ct = flip(at.c, db), flip(at.x, da), at.p
            start = aligned((pt * 2 + xt) * depth, depth)
            source = down_w_ref.at[pl.ds(start, depth)]
            copies.append(wires.make(source, target, at.at(at.h, pt, xt, at.y, ct)))
            if da + db:
                copies[-1].start()
        own = pltpu.make_async_copy(
            down_w_ref.at[pl.ds(aligned((at.p * 2 + at.x) * depth, depth), depth)],
            target,
            local_sems.at[61],
        )

        @pl.when(at.p != at.c)
        def _():
            copies[-1].start()

        @pl.when(at.p == at.c)
        def _():
            own.start()

        return copies, own

    def arrived(copies, own):
        for copy in copies:
            copy.wait_recv()
        own.wait()

    other = at.away(c=1)
    moving_rows = [
        wires.send(query_sent, query_heads.at[:, own_span], other),
        wires.send(key_heads.at[own_span], key_heads.at[own_span], other),
        wires.send(new_values_ref, value_rows.at[own_span], other),
    ]
    moving_cache = [
        [
            wires.send(cache_source(source, 1 - at.c, group), cache_target(target, group), other)
            for source, target in ((key_cache_ref, cache_k), (value_cache_ref, cache_v))
        ]
        for group in range(groups)
    ]
    moving_out = quarters(out_w_ref, out_w, 0)

    def arrived_rows():
        arrived(moving_rows, own_values)

    def arrived_group(group):
        for sent, own in zip(moving_cache[group], cache_copies[group]):
            arrived([sent], own)

    attention_phase(
        at, length, reached, value_rows, arrived_rows, arrived_group, cache_k, cache_v,
        query_heads, key_heads, mixed,
    )
    mixed_width = mixed.shape[1]
    mixed_target = attended_ref.at[:, pl.ds(aligned(at.c * mixed_width, mixed_width), mixed_width)]
    mixed_copy = wires.send(
        mixed.at[pl.ds(aligned((1 - at.c) * rows, rows), rows)], mixed_target, at.away(c=1)
    )
    own_mixed = keep(mixed.at[pl.ds(aligned(at.c * rows, rows), rows)], mixed_target)
    arrived([mixed_copy], own_mixed)
    gather = Gather(at, wires, attended_ref, att_all, local_sems.at[62])
    accept_phase(at, of_request(leaves), reached, turned, key_heads, value_rows, accepted_ref)
    gather.own_column()

    near = pl.ds(aligned(at.h * half_rows, half_rows), half_rows)
    far = pl.ds(aligned((1 - at.h) * half_rows, half_rows), half_rows)
    tile = TILE

    def multiply(chunk, all_ref, weight, total_ref, sent_ref):
        @pl.loop(0, weight.shape[1] // tile)
        def _(index):
            cols = pl.ds(aligned(index * tile, tile), tile)
            total_ref[chunk, :, cols] = jnp.dot(
                all_ref[chunk], weight[:, cols], preferred_element_type=jnp.float32
            )
        sent_ref[chunk] = total_ref[chunk, far, :].astype(sent_ref.dtype)

    arrived(*moving_out)
    crossing = []

    def project(chunk):
        multiply(chunk, att_all, out_w, out_total, out_sent)
        crossing.append(wires.send(out_sent.at[chunk], out_landed.at[chunk], at.away(h=1)))

    width = out_w.shape[1]

    def out_column(p, x, y, c):
        return pl.ds(aligned((y * 2 + c) * (4 * width) + (p * 2 + x) * width, width), width)

    own_cols = out_column(at.p, at.x, at.y, at.c)
    returning, own_projected = [], []

    def give_back(chunk):
        dx, dy = HOPS[chunk]
        crossing[chunk].wait_recv()
        done = out_total[chunk, near, :] + out_landed[chunk].astype(jnp.float32)
        out_done[chunk] = done.astype(out_done.dtype)
        for dp in range(2):
            for dc in range(2):
                start = aligned((flip(at.p, dp) * 2 + flip(at.c, dc)) * rows, rows)
                source = out_done.at[chunk, pl.ds(start, rows)]
                target = projected.at[:, own_cols]
                if dx + dy + dp + dc:
                    returning.append(
                        wires.send(source, target, at.away(p=dp, x=dx, y=dy, c=dc))
                    )
                else:
                    own_projected.append(keep(source, target))

    project(0)
    gather.neighbours()
    gather.landed(1)
    project(1)
    give_back(0)
    gather.landed(2)
    project(2)
    gather.diagonal()
    give_back(1)
    moving_gate = quarters(gate_w_ref, gate_up_w, 0)
    gather.landed(3)
    project(3)
    give_back(2)
    give_back(3)
    moving_up = quarters(up_w_ref, gate_up_w, gate_up_w.shape[1] // 2)
    for copy in returning:
        copy.wait_recv()
    own_projected[0].wait()
    own_hidden.wait()
    residual = (hidden_ref[...].astype(jnp.float32) + projected[...].astype(jnp.float32)).astype(
        jnp.bfloat16
    )
    residual_ref[...] = residual
    wide = residual.astype(jnp.float32)
    mean_sq = jnp.mean(wide * wide, axis=-1, keepdims=True)
    normed_ref[...] = (
        wide * lax.rsqrt(mean_sq + EPS) * gain[...].astype(jnp.float32).reshape(1, -1)
    ).astype(jnp.bfloat16)

    gather = Gather(at, wires, normed_ref, norm_all, local_sems.at[63])
    gather.own_column()
    arrived(*moving_gate)
    arrived(*moving_up)
    units = gate_up_w.shape[1] // 2
    own_units = pl.ds(aligned(at.c * units, units), units)
    crossing, hidden_far, hidden_core = [], [], {}

    def expand(chunk):
        multiply(chunk, norm_all, gate_up_w, total, sums_sent)
        crossing.append(wires.send(sums_sent.at[chunk], sums_landed.at[chunk], at.away(h=1)))

    def activate(chunk):
        crossing[chunk].wait_recv()
        gate = total[chunk, near, :units] + sums_landed[chunk, :, :units].astype(jnp.float32)
        up = total[chunk, near, units:] + sums_landed[chunk, :, units:].astype(jnp.float32)
        hidden = gate / (1.0 + jnp.exp(-gate)) * up
        hidden_all[chunk, near, own_units] = hidden.astype(hidden_all.dtype)
        block = hidden_all.at[chunk, near, own_units]
        hidden_far.append(wires.send(block, block, at.away(h=1)))
        hidden_core[chunk] = [wires.send(block, block, at.away(c=1))]

    def relay(chunk):
        hidden_far[chunk].wait_recv()
        block = hidden_all.at[chunk, far, own_units]
        hidden_core[chunk].append(wires.send(block, block, at.away(c=1)))

    tiles = partial.shape[1]
    back = {}

    def contract(chunk):
        for copy in hidden_core[chunk]:
            copy.wait_recv()
        dx, dy = HOPS[chunk]
        for index in range(tiles):
            cols = pl.ds(index * tile, tile)
            partial[chunk, index] = jnp.dot(
                hidden_all[chunk], down_w[:, cols], preferred_element_type=jnp.float32
            ).astype(partial.dtype)
            if chunk:
                back[chunk, index] = wires.send(
                    partial.at[chunk, index],
                    partial_landed.at[chunk - 1, index],
                    at.away(x=dx, y=dy),
                )

    expand(0)
    gather.neighbours()
    gather.landed(1)
    expand(1)
    activate(0)
    gather.landed(2)
    expand(2)
    moving_down = down_blocks()
    gather.diagonal()
    activate(1)
    relay(0)
    gather.landed(3)
    expand(3)
    activate(2)
    relay(1)
    down_copies, down_own = moving_down
    for copy in down_copies[:-1]:
        copy.wait_recv()

    @pl.when(at.p != at.c)
    def _():
        down_copies[-1].wait_recv()

    @pl.when(at.p == at.c)
    def _():
        down_own.wait()

    contract(1)
    activate(3)
    relay(2)
    contract(2)
    relay(3)
    contract(3)
    contract(0)

    level_rows = 2 * rows

    def level_sum(level, index):
        span = pl.ds(aligned(level * level_rows, level_rows), level_rows)
        sums = partial[0, index, span, :].astype(jnp.float32)
        for chunk in range(3):
            sums = sums + partial_landed[chunk, index, span, :].astype(jnp.float32)
        return sums

    paired = []
    for index in range(tiles):
        for chunk in (1, 2, 3):
            back[chunk, index].wait_recv()
        for half in range(2):
            pair_sent[index, half] = level_sum(half * 2 + 1 - at.p, index).astype(pair_sent.dtype)
        paired.append(wires.send(pair_sent.at[index], pair_landed.at[index], at.away(p=1)))
    lasting, own_last = [], []
    for index in range(tiles):
        paired[index].wait_recv()
        for half in range(2):
            last_sent[index, half] = (
                level_sum(half * 2 + at.p, index) + pair_landed[index, half].astype(jnp.float32)
            ).astype(last_sent.dtype)
        start = (at.h * 2 + at.c) * (tiles * tile) + index * tile
        target = final.at[:, pl.ds(aligned(start, tile), tile)]
        for dh, dc in ((1, 0), (1, 1), (0, 1), (0, 0)):
            start = aligned(flip(at.c, dc) * rows, rows)
            source = last_sent.at[index, flip(at.h, dh), pl.ds(start, rows)]
            if dh + dc:
                lasting.append(wires.send(source, target, at.away(h=dh, c=dc)))
            else:
                own_last.append(keep(source, target))
    for copy in lasting:
        copy.wait_recv()
    for copy in own_last:
        copy.wait()
    o_ref[...] = (
        residual_ref[...].astype(jnp.float32) + final[...].astype(jnp.float32)
    ).astype(o_ref.dtype)

    for copy in wires.started:
        if copy is not down_copies[-1]:
            copy.wait_send()

    @pl.when(at.p != at.c)
    def _():
        down_copies[-1].wait_send()


def per_device_halves(
    hidden_in, queries, new_keys, new_values, key_cache, value_cache, cache_lengths, parent_ids,
    accepted_leaf, query_gain, key_gain, post_gain, out_weight, gate_weight, up_weight, down_weight,
):
    rows, model = hidden_in.shape
    kv_width = new_keys.shape[1]
    tree, positions = 2 * rows, 2 * key_cache.shape[0]
    column = 8 * rows
    out_cols = out_weight.shape[1] // 4
    units = gate_weight.shape[1] // 4
    bf16, f32 = jnp.bfloat16, jnp.float32
    exponent = -2.0 * (np.arange(HEAD_DIM) % (HEAD_DIM // 2)) / HEAD_DIM
    frequency = (ROPE_BASE**exponent).astype(np.float32).reshape(1, -1)
    tiles = model // 4 // TILE
    vmem = pl.BlockSpec(memory_space=pltpu.VMEM)
    hbm = pl.BlockSpec(memory_space=pltpu.HBM)
    layer_out, accepted_kv = pl.pallas_call(
        layer_kernel,
        out_shape=[
            jax.ShapeDtypeStruct((rows, model), bf16),
            jax.ShapeDtypeStruct((rows, 2 * kv_width), bf16),
        ],
        in_specs=[hbm] * 17,
        out_specs=[vmem, vmem],
        scratch_shapes=[
            pltpu.VMEM((1, cache_lengths.shape[0]), jnp.int32),
            pltpu.VMEM((1, cache_lengths.shape[0]), jnp.int32),
            pltpu.VMEM(parent_ids.shape, jnp.int32),
            pltpu.VMEM((1, HEAD_DIM), f32),
            pltpu.VMEM((1, HEAD_DIM), bf16),
            pltpu.VMEM((1, HEAD_DIM), bf16),
            pltpu.VMEM(post_gain.shape, bf16),
            pltpu.VMEM((rows, model), bf16),
            pltpu.VMEM((HEADS // 2, rows, HEAD_DIM), bf16),
            pltpu.VMEM((rows, kv_width), bf16),
            pltpu.VMEM((tree, kv_width), bf16),
            pltpu.VMEM((positions, kv_width // 2), bf16),
            pltpu.VMEM((positions, kv_width // 2), bf16),
            pltpu.VMEM((HEADS // 2, tree, HEAD_DIM), bf16),
            pltpu.VMEM((tree, kv_width), bf16),
            pltpu.VMEM((tree, model // 2), bf16),
            pltpu.VMEM((rows, model), bf16),
            pltpu.VMEM((rows, model), bf16),
            pltpu.VMEM((4, column, model // 2), bf16),
            pltpu.VMEM((4, column, model // 2), bf16),
            pltpu.VMEM((model // 2, out_cols), bf16),
            pltpu.VMEM((model // 2, 2 * units), bf16),
            pltpu.VMEM((2 * units, model // 4), bf16),
            pltpu.VMEM((4, column, out_cols), f32),
            pltpu.VMEM((4, column // 2, out_cols), bf16),
            pltpu.VMEM((4, column // 2, out_cols), bf16),
            pltpu.VMEM((4, column // 2, out_cols), bf16),
            pltpu.VMEM((rows, model), bf16),
            pltpu.VMEM((rows, model), bf16),
            pltpu.VMEM((rows, model), bf16),
            pltpu.VMEM((4, column, 2 * units), f32),
            pltpu.VMEM((4, column // 2, 2 * units), bf16),
            pltpu.VMEM((4, column // 2, 2 * units), bf16),
            pltpu.VMEM((4, column, 2 * units), bf16),
            pltpu.VMEM((4, tiles, column, TILE), bf16),
            pltpu.VMEM((3, tiles, column, TILE), bf16),
            pltpu.VMEM((tiles, 2, 2 * rows, TILE), bf16),
            pltpu.VMEM((tiles, 2, 2 * rows, TILE), bf16),
            pltpu.VMEM((tiles, 2, 2 * rows, TILE), bf16),
            pltpu.VMEM((rows, model), bf16),
            pltpu.SemaphoreType.DMA((SEMAPHORES,)),
            pltpu.SemaphoreType.DMA((SEMAPHORES,)),
            pltpu.SemaphoreType.DMA((64,)),
        ],
        compiler_params=pltpu.CompilerParams(
            collective_id=8, has_side_effects=True, vmem_limit_bytes=63 * 2**20
        ),
    )(
        cache_lengths.reshape(1, -1), accepted_leaf.reshape(1, -1), parent_ids, frequency,
        query_gain.reshape(1, -1), key_gain.reshape(1, -1), post_gain, queries, new_keys,
        new_values, key_cache, value_cache, hidden_in, out_weight, gate_weight, up_weight, down_weight,
    )
    return layer_out, accepted_kv


def solution(mesh):
    in_specs = (
        P(("req", "tp"), None),
        P(("req", "tp"), None),
        P(("req", "tp"), None),
        P(("req", "tp"), None),
        P(("req", "tp"), None),
        P(("req", "tp"), None),
        P(),
        P(),
        P(),
        P(),
        P(),
        P(),
        P("req", "tp"),
        P("req", "tp"),
        P("req", "tp"),
        P("tp", "req"),
    )
    out_specs = (P(("req", "tp"), None), P(("req", "tp"), None))
    by_halves = mesh.shape["req"] == 4 * SIDE and mesh.shape["tp"] == 4
    return jax.shard_map(
        per_device_halves if by_halves else per_device, mesh=mesh, in_specs=in_specs, out_specs=out_specs, check_vma=False
    )
```
